32 devices in a mesh: rep: 8 (over z, x), shard: 4 (over y, core).
Axes of the slice: x: 2, y: 2, z: 4, core: 2. Of those that a mesh axis runs over, the one named last changes fastest.
Arguments:
- tokens: bfloat16 [16384, 768], P(('rep', 'shard')), may hold values from -6 to 6
- condition: bfloat16 [64, 768], P(('rep', 'shard')), may hold values from -5 to 5
- counts: int32 [32], P(('rep', 'shard')), may hold values from 0 to 2, as said below
- cotangent: bfloat16 [16384, 768], P(('rep', 'shard')), may hold values from -6 to 6
- ada_weight: bfloat16 [768, 4608], P('shard'), may hold values from -0.21875 to 0.21875
- ada_bias: bfloat16 [4608], P('shard'), may hold values from -3 to 3
- qkv_weight: bfloat16 [768, 2304], P('shard'), may hold values from -0.21875 to 0.21875
- qv_bias: bfloat16 [1536], P('shard'), may hold values from -3 to 3
- proj_weight: bfloat16 [768, 768], P('shard'), may hold values from -0.875 to 0.875
- proj_bias: bfloat16 [768], P('shard'), may hold values from -3 to 3
- fc1_weight: bfloat16 [768, 3072], P('shard'), may hold values from -0.21875 to 0.21875
- fc1_bias: bfloat16 [3072], P('shard'), may hold values from -3 to 3
- fc2_weight: bfloat16 [3072, 768], P('shard'), may hold values from -0.109375 to 0.109375
- fc2_bias: bfloat16 [768], P('shard'), may hold values from -3 to 3
Outputs:
- block_out: bfloat16 [16384, 768], P(('rep', 'shard'))
- grad_tokens: float32 [16384, 768], P(('rep', 'shard'))
- grad_condition: float32 [64, 768], P(('rep', 'shard'))
- grad_ada_weight: float32 [768, 4608], P('shard')
- grad_ada_bias: float32 [4608], P('shard')
- grad_qkv_weight: float32 [768, 2304], P('shard')
- grad_qv_bias: float32 [1536], P('shard')
- grad_proj_weight: float32 [768, 768], P('shard')
- grad_proj_bias: float32 [768], P('shard')
- grad_fc1_weight: float32 [768, 3072], P('shard')
- grad_fc1_bias: float32 [3072], P('shard')
- grad_fc2_weight: float32 [3072, 768], P('shard')
- grad_fc2_bias: float32 [768], P('shard')
The draws below stay inside these ranges and needn't reach their ends.
Inputs may be any that keep to these rules, and one draw needn't show every extreme that they name: counts[i] is the number of live latent slots of device i, devices taken in the order of rep then shard, each device holding 2 slots with its live ones first; the counts of the 4 devices of one replica group (consecutive entries) sum to 4; in every group some device holds 2 live latents and some holds none.
All inputs are finite; a program needn't handle non-finite values.
Results may differ from the reference program's by a relative error of at most 0.012.
The reference program's roundings to bfloat16 on the way count: a program that leaves them out, or rounds other values in their place, can miss the bound.
Values may be sent and summed in bfloat16 or wider, within the bound.
No kernel may reach another device: no remote copies, remote signals or barrier semaphores. Data moves between devices by JAX's collectives and lax.ppermute only.
A program may use at most 192 MiB of HBM per device.

```python
import jax
import jax.numpy as jnp
from jax import lax

HEADS = 12
HEAD_DIM = 64
D = 768
FF = 3072
SEQ = 256
LAT_CAP = 2
GROUP_SIZE = 4
HOLDERS = 32
SLOTS = 64
TOKENS = 16384


def draw_counts(key, part):
    own_key = jax.random.fold_in(key, 17)
    size_key, perm_key = jax.random.split(own_key)
    groups = HOLDERS // GROUP_SIZE
    doubled = jax.random.randint(size_key, (groups, 1), 1, GROUP_SIZE // 2 + 1)
    perm_keys = jax.random.split(perm_key, groups)
    places = jax.vmap(lambda one_key: jax.random.permutation(one_key, GROUP_SIZE))(perm_keys)
    values = jnp.where(places < doubled, LAT_CAP, jnp.where(places < 2 * doubled, 0, 1))
    return values.reshape(HOLDERS).astype(jnp.int32)


def levels(key, extent, shards, smallest, largest):
    def one(position, shards_of):
        steps = jax.random.uniform(jax.random.fold_in(jax.random.fold_in(key, 6), position), (shards_of,), jnp.float32, smallest / len(shards), largest / len(shards))
        return jnp.repeat(jnp.exp(steps), extent[position] // shards_of).reshape((-1,) + (1,) * (len(extent) - position - 1))

    loudness = one(*shards[0])
    for cut in shards[1:]:
        loudness = loudness * one(*cut)
    return loudness


def normal_values(key, shape, deviation, most, cuts=(), kind=jnp.bfloat16):
    loudness = levels(key, shape, cuts, -0.22, 0.18) if cuts else 1.0
    entries = jax.random.normal(key, shape, jnp.float32) * deviation * loudness
    return jnp.minimum(jnp.maximum(entries, -most), most).astype(kind)


def setup_inputs(seed: int = 0) -> dict:
    splits = jax.random.split(jax.random.key(seed), 15)
    tokens = normal_values(splits[0], (TOKENS, D), 1.0, 6.0, ((0, 32),))
    condition = normal_values(splits[1], (SLOTS, D), 1.0, 5.0, ((0, 32),))
    counts = draw_counts(jax.random.fold_in(splits[14], 71), 0)
    cotangent = normal_values(splits[3], (TOKENS, D), 1.0, 6.0, ((0, 32),))
    ada_weight = normal_values(splits[4], (D, 6 * D), D ** -0.5, 0.21875, ((0, 4),))
    ada_bias = normal_values(splits[5], (6 * D,), 0.5, 3.0, ((0, 4),))
    qkv_weight = normal_values(splits[6], (D, 3 * D), D ** -0.5, 0.21875, ((0, 4),))
    qv_bias = normal_values(splits[7], (2 * D,), 0.5, 3.0, ((0, 4),))
    proj_weight = normal_values(splits[8], (D, D), (D // 16) ** -0.5, 0.875, ((0, 4),))
    proj_bias = normal_values(splits[9], (D,), 0.5, 3.0, ((0, 4),))
    fc1_weight = normal_values(splits[10], (D, FF), D ** -0.5, 0.21875, ((0, 4),))
    fc1_bias = normal_values(splits[11], (FF,), 0.5, 3.0, ((0, 4),))
    fc2_weight = normal_values(splits[12], (FF, D), FF ** -0.5, 0.109375, ((0, 4),))
    fc2_bias = normal_values(splits[13], (D,), 0.5, 3.0, ((0, 4),))
    return {"tokens": tokens, "condition": condition, "counts": counts, "cotangent": cotangent, "ada_weight": ada_weight, "ada_bias": ada_bias, "qkv_weight": qkv_weight, "qv_bias": qv_bias, "proj_weight": proj_weight, "proj_bias": proj_bias, "fc1_weight": fc1_weight, "fc1_bias": fc1_bias, "fc2_weight": fc2_weight, "fc2_bias": fc2_bias}


EPS = 1e-06
GELU_C = 0.7978845608028654
GELU_A = 0.044715

def normalize(values):
    center = values - lax.optimization_barrier(jnp.mean(values, axis=-1, keepdims=True))
    inv_std = lax.rsqrt(lax.optimization_barrier(jnp.mean(center * center, axis=-1, keepdims=True)) + EPS)
    return (center * inv_std, inv_std)

def norm_back(grad_hat, normed, inv_std):
    return inv_std * (grad_hat - lax.optimization_barrier(jnp.mean(grad_hat, axis=-1, keepdims=True)) - normed * lax.optimization_barrier(jnp.mean(grad_hat * normed, axis=-1, keepdims=True)))

def gelu_pair(pre_act):
    tanh_arg = GELU_C * (pre_act + GELU_A * pre_act * pre_act * pre_act)
    tanh_val = jnp.tanh(tanh_arg)
    activated = 0.5 * pre_act * (1.0 + tanh_val)
    derivative = 0.5 * (1.0 + tanh_val) + 0.5 * pre_act * (1.0 - tanh_val * tanh_val) * GELU_C * (1.0 + 3.0 * GELU_A * pre_act * pre_act)
    return (activated, derivative)

def contract_rows(left, right):
    return lax.dot_general(left, right, (((0,), (0,)), ((), ())), preferred_element_type=jnp.float32)

def times_trans(left, right):
    return lax.dot_general(left, right, (((1,), (1,)), ((), ())), preferred_element_type=jnp.float32)

def batched(form, left, right):
    return jnp.einsum(form, left.astype(jnp.float32), right.astype(jnp.float32))

def head_split(rows):
    return rows.reshape(rows.shape[0], HEADS, HEAD_DIM)

def attention_probs(queries, key_rows, log_total):
    scores = batched('qhd,khd->hqk', head_split(queries), head_split(key_rows)) * HEAD_DIM ** (-0.5)
    if log_total is None:
        row_max = lax.optimization_barrier(jnp.max(scores, axis=-1, keepdims=True))
        log_total = row_max + jnp.log(lax.optimization_barrier(jnp.sum(jnp.exp(scores - row_max), axis=-1, keepdims=True)))
    return (jnp.exp(scores - log_total), log_total)

def forward_latent(tok_rows, cond_row, attn_params, mlp_params):
    ada_w, ada_b, qkv_w, qv_b, proj_w, proj_b = attn_params
    fc1_w, fc1_b, fc2_w, fc2_b = mlp_params
    width = tok_rows.shape[1]
    silu_cond = jax.nn.silu(cond_row.astype(jnp.float32)).astype(jnp.bfloat16)
    modulation = jnp.dot(silu_cond[None, :], ada_w, preferred_element_type=jnp.float32)[0] + ada_b.astype(jnp.float32)
    shift_one, scale_one, gate_one, shift_two, scale_two, gate_two = jnp.split(modulation, 6)
    resid_in = tok_rows.astype(jnp.float32)
    normed_one, inv_one = normalize(resid_in)
    hidden_one = (normed_one * (1.0 + scale_one) + shift_one).astype(jnp.bfloat16)
    projected = jnp.dot(hidden_one, qkv_w, preferred_element_type=jnp.float32)
    bias_wide = qv_b.astype(jnp.float32)
    queries = (projected[:, :width] + bias_wide[:width]).astype(jnp.bfloat16)
    key_rows = projected[:, width:2 * width].astype(jnp.bfloat16)
    value_rows = (projected[:, 2 * width:] + bias_wide[width:]).astype(jnp.bfloat16)
    attn_probs, log_total = attention_probs(queries, key_rows, None)
    probs_low = attn_probs.astype(jnp.bfloat16)
    mixed = batched('hqk,khd->qhd', probs_low, head_split(value_rows)).reshape(-1, width).astype(jnp.bfloat16)
    branch_one = jnp.dot(mixed, proj_w, preferred_element_type=jnp.float32) + proj_b.astype(jnp.float32)
    resid_mid = resid_in + gate_one * branch_one
    normed_two, inv_two = normalize(resid_mid)
    hidden_two = (normed_two * (1.0 + scale_two) + shift_two).astype(jnp.bfloat16)
    pre_act = jnp.dot(hidden_two, fc1_w, preferred_element_type=jnp.float32) + fc1_b.astype(jnp.float32)
    activated, derivative = gelu_pair(pre_act)
    act_low = activated.astype(jnp.bfloat16)
    branch_two = jnp.dot(act_low, fc2_w, preferred_element_type=jnp.float32) + fc2_b.astype(jnp.float32)
    block_rows = (resid_mid + gate_two * branch_two).astype(jnp.bfloat16)
    saved = (silu_cond, modulation, normed_one, inv_one, hidden_one, queries, key_rows, value_rows, log_total, mixed, branch_one, normed_two, inv_two, hidden_two, pre_act, act_low, branch_two)
    return (block_rows, saved)

def mlp_backward(cot_rows, saved, mlp_params):
    fc1_w, fc1_b, fc2_w, fc2_b = mlp_params
    modulation = saved[1]
    normed_two, inv_two, hidden_two, pre_act, act_low, branch_two = saved[11:17]
    shift_one, scale_one, gate_one, shift_two, scale_two, gate_two = jnp.split(modulation, 6)
    cot_wide = cot_rows.astype(jnp.float32)
    grad_branch_two = gate_two * cot_wide
    grad_gate_two = lax.optimization_barrier(jnp.sum(cot_wide * branch_two, axis=0))
    low_two = grad_branch_two.astype(jnp.bfloat16)
    grad_fc2_w = contract_rows(act_low, low_two)
    grad_fc2_b = lax.optimization_barrier(jnp.sum(grad_branch_two, axis=0))
    activated, derivative = gelu_pair(pre_act)
    grad_pre = times_trans(low_two, fc2_w) * derivative
    low_pre = grad_pre.astype(jnp.bfloat16)
    grad_fc1_w = contract_rows(hidden_two, low_pre)
    grad_fc1_b = lax.optimization_barrier(jnp.sum(grad_pre, axis=0))
    grad_hidden_two = times_trans(low_pre, fc1_w)
    grad_shift_two = lax.optimization_barrier(jnp.sum(grad_hidden_two, axis=0))
    grad_scale_two = lax.optimization_barrier(jnp.sum(grad_hidden_two * normed_two, axis=0))
    grad_mid = cot_wide + norm_back(grad_hidden_two * (1.0 + scale_two), normed_two, inv_two)
    return (grad_mid, (grad_shift_two, grad_scale_two, grad_gate_two), (grad_fc1_w, grad_fc1_b, grad_fc2_w, grad_fc2_b))

def attn_backward(grad_mid, mod_two, saved, cond_row, attn_params):
    ada_w, ada_b, qkv_w, qv_b, proj_w, proj_b = attn_params
    modulation, normed_one, inv_one, hidden_one, queries, key_rows, value_rows, log_total, mixed, branch_one = saved[1:11]
    shift_one, scale_one, gate_one, shift_two, scale_two, gate_two = jnp.split(modulation, 6)
    width = grad_mid.shape[1]
    grad_branch_one = gate_one * grad_mid
    grad_gate_one = lax.optimization_barrier(jnp.sum(grad_mid * branch_one, axis=0))
    low_one = grad_branch_one.astype(jnp.bfloat16)
    grad_proj_w = contract_rows(mixed, low_one)
    grad_proj_b = lax.optimization_barrier(jnp.sum(grad_branch_one, axis=0))
    grad_mixed = times_trans(low_one, proj_w).astype(jnp.bfloat16)
    attn_probs, log_total = attention_probs(queries, key_rows, log_total)
    probs_low = attn_probs.astype(jnp.bfloat16)
    grad_heads = head_split(grad_mixed)
    grad_values = batched('hqk,qhd->khd', probs_low, grad_heads).reshape(-1, width)
    grad_probs = batched('qhd,khd->hqk', grad_heads, head_split(value_rows))
    row_dot = lax.optimization_barrier(jnp.sum(attn_probs * grad_probs, axis=-1, keepdims=True))
    grad_scores = (attn_probs * (grad_probs - row_dot) * HEAD_DIM ** (-0.5)).astype(jnp.bfloat16)
    grad_queries = batched('hqk,khd->qhd', grad_scores, head_split(key_rows)).reshape(-1, width)
    grad_keys = batched('hqk,qhd->khd', grad_scores, head_split(queries)).reshape(-1, width)
    grad_qkv = jnp.concatenate([grad_queries, grad_keys, grad_values], axis=1).astype(jnp.bfloat16)
    grad_qv_b = jnp.concatenate([lax.optimization_barrier(jnp.sum(grad_queries, axis=0)), lax.optimization_barrier(jnp.sum(grad_values, axis=0))])
    grad_qkv_w = contract_rows(hidden_one, grad_qkv)
    grad_hidden_one = times_trans(grad_qkv, qkv_w)
    grad_shift_one = lax.optimization_barrier(jnp.sum(grad_hidden_one, axis=0))
    grad_scale_one = lax.optimization_barrier(jnp.sum(grad_hidden_one * normed_one, axis=0))
    grad_rows = grad_mid + norm_back(grad_hidden_one * (1.0 + scale_one), normed_one, inv_one)
    grad_mod = jnp.concatenate([grad_shift_one, grad_scale_one, grad_gate_one, mod_two[0], mod_two[1], mod_two[2]]).astype(jnp.bfloat16)
    grad_silu = times_trans(grad_mod[None, :], ada_w)[0]
    cond_wide = cond_row.astype(jnp.float32)
    logistic = jax.nn.sigmoid(cond_wide)
    grad_cond = grad_silu * logistic * (1.0 + cond_wide * (1.0 - logistic))
    return (grad_rows, grad_cond, grad_mod, (grad_qkv_w, grad_qv_b, grad_proj_w, grad_proj_b))

def reference(tokens, condition, counts, cotangent, ada_weight, ada_bias, qkv_weight, qv_bias, proj_weight, proj_bias, fc1_weight, fc1_bias, fc2_weight, fc2_bias):
    attn_params = (ada_weight, ada_bias, qkv_weight, qv_bias, proj_weight, proj_bias)
    mlp_params = (fc1_weight, fc1_bias, fc2_weight, fc2_bias)
    tok_all = tokens.reshape(SLOTS, SEQ, D)
    cot_all = cotangent.reshape(SLOTS, SEQ, D)
    slot_ids = jnp.arange(SLOTS, dtype=jnp.int32)
    alive_all = counts[slot_ids // LAT_CAP] > slot_ids % LAT_CAP
    grad_init = tuple((jnp.zeros(w.shape, jnp.float32) for w in (qkv_weight, qv_bias, proj_weight, proj_bias, fc1_weight, fc1_bias, fc2_weight, fc2_bias)))

    def working(operands):
        block_rows, saved = forward_latent(operands[0], operands[1], attn_params, mlp_params)
        grad_mid, mod_two, mlp_grads = mlp_backward(operands[2], saved, mlp_params)
        grad_rows, grad_cond, grad_mod, attn_grads = attn_backward(grad_mid, mod_two, saved, operands[1], attn_params)
        return (block_rows, grad_rows, grad_cond, saved[0], grad_mod, attn_grads + mlp_grads)

    def resting(operands):
        return (jnp.zeros((SEQ, D), jnp.bfloat16), jnp.zeros((SEQ, D), jnp.float32), jnp.zeros((D,), jnp.float32), jnp.zeros((D,), jnp.bfloat16), jnp.zeros((6 * D,), jnp.bfloat16), tuple((jnp.zeros(w.shape, jnp.float32) for w in grad_init)))

    def one_slot(totals, inputs):
        tok_rows, cond_row, cot_rows, alive = inputs
        outcome = lax.cond(alive, working, resting, (tok_rows, cond_row, cot_rows))
        totals = tuple((left + right for left, right in zip(totals, outcome[5])))
        return (totals, outcome[:5])
    totals, stacked = lax.scan(one_slot, grad_init, (tok_all, condition, cot_all, alive_all))
    block_all, grad_rows_all, grad_cond_all, silu_all, mod_all = stacked
    grad_ada_w = contract_rows(silu_all, mod_all)
    grad_ada_b = lax.optimization_barrier(jnp.sum(mod_all.astype(jnp.float32), axis=0))
    return (block_all.reshape(TOKENS, D), grad_rows_all.reshape(TOKENS, D), grad_cond_all, grad_ada_w, grad_ada_b, totals[0], totals[1], totals[2], totals[3], totals[4], totals[5], totals[6], totals[7])
```

```python
import functools

import jax
import jax.numpy as jnp
from jax import lax
from jax.experimental import pallas as pl
from jax.experimental.pallas import tpu as pltpu
from jax.sharding import PartitionSpec as P

HEADS = 12
HEAD_DIM = 64
EPS = 1e-06
GELU_C = 0.7978845608028654
GELU_A = 0.044715
F32 = jnp.float32
BF16 = jnp.bfloat16
VMEM_LIMIT = 56 * 1024 * 1024


def normalize(values):
    center = values - jnp.mean(values, axis=-1, keepdims=True)
    inv_std = lax.rsqrt(jnp.mean(center * center, axis=-1, keepdims=True) + EPS)
    return (center * inv_std, inv_std)


def norm_back(grad_hat, normed, inv_std):
    return inv_std * (
        grad_hat
        - jnp.mean(grad_hat, axis=-1, keepdims=True)
        - normed * jnp.mean(grad_hat * normed, axis=-1, keepdims=True)
    )


def gelu_pair(pre_act):
    tanh_arg = GELU_C * (pre_act + GELU_A * pre_act * pre_act * pre_act)
    tanh_val = jnp.tanh(tanh_arg)
    activated = 0.5 * pre_act * (1.0 + tanh_val)
    derivative = 0.5 * (1.0 + tanh_val) + 0.5 * pre_act * (1.0 - tanh_val * tanh_val) * GELU_C * (
        1.0 + 3.0 * GELU_A * pre_act * pre_act
    )
    return (activated, derivative)


def dot_nn(left, right):
    return lax.dot_general(left, right, (((1,), (0,)), ((), ())), preferred_element_type=F32)


def dot_nt(left, right):
    return lax.dot_general(left, right, (((1,), (1,)), ((), ())), preferred_element_type=F32)


def dot_tn(left, right):
    return lax.dot_general(left, right, (((0,), (0,)), ((), ())), preferred_element_type=F32)


def pair_masks(rows):
    lane = lax.broadcasted_iota(jnp.int32, (rows, 2 * HEAD_DIM), 1)
    return lane < HEAD_DIM


def head_probs(query_pair, key_pair, first, head):
    keep = first if head == 0 else jnp.logical_not(first)
    query_head = jnp.where(keep, query_pair, jnp.zeros_like(query_pair))
    scores = dot_nt(query_head, key_pair) * HEAD_DIM ** (-0.5)
    row_max = jnp.max(scores, axis=-1, keepdims=True)
    exped = jnp.exp(scores - row_max)
    return exped * (1.0 / jnp.sum(exped, axis=-1, keepdims=True))


def attn_fwd_kernel(qkv_ref, mixed_ref):
    rows = qkv_ref.shape[0]
    width = mixed_ref.shape[1]
    first = pair_masks(rows)
    for pair in range(HEADS // 2):
        cols = pl.ds(pair * 128, 128)
        query_pair = qkv_ref[:, cols]
        key_pair = qkv_ref[:, pl.ds(width + pair * 128, 128)]
        value_pair = qkv_ref[:, pl.ds(2 * width + pair * 128, 128)]
        parts = []
        for head in range(2):
            probs_low = head_probs(query_pair, key_pair, first, head).astype(BF16)
            parts.append(dot_nn(probs_low, value_pair))
        mixed_ref[:, cols] = jnp.where(first, parts[0], parts[1]).astype(BF16)


def attn_fwd(qkv, slots):
    seq = qkv.shape[0] // slots
    width = qkv.shape[1] // 3
    return pl.pallas_call(
        attn_fwd_kernel,
        grid=(slots,),
        in_specs=[pl.BlockSpec((seq, 3 * width), lambda s: (s, 0))],
        out_specs=pl.BlockSpec((seq, width), lambda s: (s, 0)),
        out_shape=jax.ShapeDtypeStruct((slots * seq, width), BF16),
        compiler_params=pltpu.CompilerParams(vmem_limit_bytes=VMEM_LIMIT),
    )(qkv)


def attn_bwd_kernel(qkv_ref, grad_ref, out_ref, bias_ref):
    rows = qkv_ref.shape[0]
    width = grad_ref.shape[1]
    first = pair_masks(rows)
    for pair in range(HEADS // 2):
        query_cols = pl.ds(pair * 128, 128)
        key_cols = pl.ds(width + pair * 128, 128)
        value_cols = pl.ds(2 * width + pair * 128, 128)
        query_pair = qkv_ref[:, query_cols]
        key_pair = qkv_ref[:, key_cols]
        value_pair = qkv_ref[:, value_cols]
        grad_pair = grad_ref[:, query_cols]
        grads = []
        for head in range(2):
            keep = first if head == 0 else jnp.logical_not(first)
            probs = head_probs(query_pair, key_pair, first, head)
            grad_head = jnp.where(keep, grad_pair, jnp.zeros_like(grad_pair))
            grad_probs = dot_nt(grad_head, value_pair)
            row_dot = jnp.sum(probs * grad_probs, axis=-1, keepdims=True)
            grad_scores = (probs * (grad_probs - row_dot) * HEAD_DIM ** (-0.5)).astype(BF16)
            grads.append(
                (
                    dot_nn(grad_scores, key_pair),
                    dot_tn(grad_scores, query_pair),
                    dot_tn(probs.astype(BF16), grad_pair),
                )
            )
        grad_query, grad_key, grad_value = (
            jnp.where(first, left, right) for left, right in zip(grads[0], grads[1])
        )
        out_ref[:, query_cols] = grad_query.astype(BF16)
        out_ref[:, key_cols] = grad_key.astype(BF16)
        out_ref[:, value_cols] = grad_value.astype(BF16)
        bias_ref[0, :, query_cols] = jnp.sum(grad_query, axis=0, keepdims=True)
        bias_ref[0, :, key_cols] = jnp.sum(grad_value, axis=0, keepdims=True)


def attn_bwd(qkv, grad_mixed, slots):
    seq = qkv.shape[0] // slots
    width = qkv.shape[1] // 3
    return pl.pallas_call(
        attn_bwd_kernel,
        grid=(slots,),
        in_specs=[
            pl.BlockSpec((seq, 3 * width), lambda s: (s, 0)),
            pl.BlockSpec((seq, width), lambda s: (s, 0)),
        ],
        out_specs=[
            pl.BlockSpec((seq, 3 * width), lambda s: (s, 0)),
            pl.BlockSpec((1, 1, 2 * width), lambda s: (s, 0, 0)),
        ],
        out_shape=[
            jax.ShapeDtypeStruct((slots * seq, 3 * width), BF16),
            jax.ShapeDtypeStruct((slots, 1, 2 * width), F32),
        ],
        compiler_params=pltpu.CompilerParams(vmem_limit_bytes=VMEM_LIMIT),
    )(qkv, grad_mixed)


class Axis:
    def __init__(self, name, size):
        self.name = name
        self.size = size
        self.index = lax.axis_index(name)
        self.bits = [1 << k for k in range(size.bit_length() - 1)]

    def swap(self, value, bit):
        return lax.ppermute(value, self.name, [(i, i ^ bit) for i in range(self.size)])

    def high(self, bit):
        return (self.index & bit) != 0


def ordered(high, mine, other, axis=0):
    return jnp.where(
        high, jnp.concatenate([other, mine], axis), jnp.concatenate([mine, other], axis)
    )


def gather_ordered(value, axis):
    value = value[None]
    for bit in axis.bits:
        value = ordered(axis.high(bit), value, axis.swap(value, bit))
    return value


def gather_any_order(value, steps):
    for axis, bit in steps:
        value = jnp.concatenate([value, axis.swap(value, bit)], 0)
    return value


def halves(value, high, dim):
    size = value.shape[dim] // 2
    offset = high.astype(jnp.int32) * size
    keep = lax.dynamic_slice_in_dim(value, offset, size, dim)
    send = lax.dynamic_slice_in_dim(value, size - offset, size, dim)
    return keep, send


def scatter_sum(value, axis, wire):
    for bit in reversed(axis.bits):
        keep, send = halves(value, axis.high(bit), 0)
        value = keep + axis.swap(send.astype(wire), bit).astype(F32)
    return value[0]


def gather_weight(piece, shard, rep):
    pieces = {0: piece}
    half_rows = piece.shape[0] // 2
    for bit in reversed(shard.bits):
        for offset in list(pieces):
            held = pieces[offset]
            if bit == 1 or rep.size == 1:
                pieces[offset ^ bit] = shard.swap(held, bit)
            else:
                mine = lax.dynamic_slice_in_dim(
                    held, rep.high(1).astype(jnp.int32) * half_rows, half_rows, 0
                )
                near = shard.swap(mine, bit)
                far = rep.swap(near, 1)
                pieces[offset ^ bit] = ordered(rep.high(1), near, far)
    rows = piece.shape[0]
    whole = jnp.zeros((rows * shard.size, piece.shape[1]), piece.dtype)
    for offset, held in pieces.items():
        whole = lax.dynamic_update_slice(whole, held, ((shard.index ^ offset) * rows, 0))
    return whole


def reduce_weight(total, shard, rep):
    total = total.reshape((shard.size // 2, 2, -1, total.shape[1]))
    keep, send = halves(total, shard.high(1), 1)
    value = (keep + shard.swap(send.astype(BF16), 1).astype(F32))[:, 0]
    for bit in reversed(shard.bits[1:]):
        keep, send = halves(value, shard.high(bit), 0)
        value = keep + shard.swap(send.astype(BF16), bit).astype(F32)
    value = value[0]
    dims = []
    for bit in rep.bits:
        dim = 1 if value.shape[0] % 32 and value.shape[1] % 256 == 0 else 0
        dims.append(dim)
        keep, send = halves(value, rep.high(bit), dim)
        value = keep + rep.swap(send.astype(BF16), bit).astype(F32)
    value = value.astype(BF16)
    for bit, dim in zip(reversed(rep.bits), reversed(dims)):
        value = ordered(rep.high(bit), value, rep.swap(value, bit), dim)
    return value.astype(F32)


def per_device(
    shard_size,
    rep_size,
    tokens,
    condition,
    counts,
    cotangent,
    ada_weight,
    ada_bias,
    qkv_weight,
    qv_bias,
    proj_weight,
    proj_bias,
    fc1_weight,
    fc1_bias,
    fc2_weight,
    fc2_bias,
):
    shard = Axis("shard", shard_size)
    rep = Axis("rep", rep_size)
    slots, width = condition.shape
    seq = tokens.shape[0] // slots
    rows = slots * seq
    depth = ada_weight.shape[0]
    live = lax.iota(jnp.int32, slots) < counts[0]

    biases = jnp.concatenate([ada_bias, qv_bias, proj_bias, fc1_bias, fc2_bias])
    packed = jnp.concatenate([condition.reshape(-1), biases])
    packed = jnp.pad(packed, (0, -packed.shape[0] % 128)).reshape(-1, 128)
    group = gather_ordered(packed, shard).reshape(shard.size, -1)
    group_cond = group[:, : slots * width].reshape(shard.size * slots, width)
    wide = []
    start = slots * width
    for bias in (ada_bias, qv_bias, proj_bias, fc1_bias, fc2_bias):
        wide.append(group[:, start : start + bias.shape[0]].reshape(-1).astype(F32))
        start += bias.shape[0]
    ada_b, qv_b, proj_b, fc1_b, fc2_b = wide

    qkv_w = gather_weight(qkv_weight, shard, rep)
    proj_w = gather_weight(proj_weight, shard, rep)
    fc1_w = gather_weight(fc1_weight, shard, rep)
    fc2_w = gather_weight(fc2_weight, shard, rep)

    silu_group = jax.nn.silu(group_cond.astype(F32)).astype(BF16)
    my_cols = lax.dynamic_slice_in_dim(silu_group, shard.index * depth, depth, 1)
    mod_part = dot_nn(my_cols, ada_weight).reshape(shard.size, slots, -1)
    modulation = scatter_sum(mod_part, shard, F32) + ada_b
    shift_one, scale_one, gate_one, shift_two, scale_two, gate_two = (
        part[:, None, :] for part in jnp.split(modulation, 6, axis=1)
    )

    def flat(value):
        return value.reshape(rows, value.shape[-1])

    def per_slot(value):
        return value.reshape(slots, seq, value.shape[-1])

    resid_in = per_slot(tokens).astype(F32)
    normed_one, inv_one = normalize(resid_in)
    hidden_one = flat((normed_one * (1.0 + scale_one) + shift_one).astype(BF16))
    zero = jnp.zeros((width,), F32)
    qkv_b = jnp.concatenate([qv_b[:width], zero, qv_b[width:]])
    qkv = (dot_nn(hidden_one, qkv_w) + qkv_b).astype(BF16)
    mixed = attn_fwd(qkv, slots)
    branch_one = per_slot(dot_nn(mixed, proj_w) + proj_b)
    resid_mid = resid_in + gate_one * branch_one
    normed_two, inv_two = normalize(resid_mid)
    hidden_two = flat((normed_two * (1.0 + scale_two) + shift_two).astype(BF16))
    pre_act = dot_nn(hidden_two, fc1_w) + fc1_b
    activated, derivative = gelu_pair(pre_act)
    act_low = activated.astype(BF16)
    branch_two = per_slot(dot_nn(act_low, fc2_w) + fc2_b)
    block = resid_mid + gate_two * branch_two
    block_out = flat(jnp.where(live[:, None, None], block, 0.0).astype(BF16))

    cot_wide = jnp.where(live[:, None, None], per_slot(cotangent).astype(F32), 0.0)
    grad_branch_two = gate_two * cot_wide
    low_two = flat(grad_branch_two.astype(BF16))
    grad_gate_two = jnp.sum(cot_wide * branch_two, axis=1)
    grad_fc2_b = jnp.sum(grad_branch_two, axis=(0, 1))
    grad_fc2_w = reduce_weight(dot_tn(act_low, low_two), shard, rep)
    grad_pre = dot_nt(low_two, fc2_w) * derivative
    low_pre = grad_pre.astype(BF16)
    grad_fc1_b = jnp.sum(grad_pre, axis=0)
    grad_fc1_w = reduce_weight(dot_tn(hidden_two, low_pre), shard, rep)
    grad_hidden_two = per_slot(dot_nt(low_pre, fc1_w))
    grad_shift_two = jnp.sum(grad_hidden_two, axis=1)
    grad_scale_two = jnp.sum(grad_hidden_two * normed_two, axis=1)
    grad_mid = cot_wide + norm_back(grad_hidden_two * (1.0 + scale_two), normed_two, inv_two)

    grad_branch_one = gate_one * grad_mid
    grad_gate_one = jnp.sum(grad_mid * branch_one, axis=1)
    low_one = flat(grad_branch_one.astype(BF16))
    grad_proj_b = jnp.sum(grad_branch_one, axis=(0, 1))
    grad_proj_w = reduce_weight(dot_tn(mixed, low_one), shard, rep)
    grad_mixed = dot_nt(low_one, proj_w).astype(BF16)
    grad_qkv, qv_sums = attn_bwd(qkv, grad_mixed, slots)
    grad_qv_b = jnp.sum(qv_sums[:, 0], axis=0)
    grad_qkv_w = reduce_weight(dot_tn(hidden_one, grad_qkv), shard, rep)
    grad_hidden_one = per_slot(dot_nt(grad_qkv, qkv_w))
    grad_shift_one = jnp.sum(grad_hidden_one, axis=1)
    grad_scale_one = jnp.sum(grad_hidden_one * normed_one, axis=1)
    grad_tokens = flat(
        grad_mid + norm_back(grad_hidden_one * (1.0 + scale_one), normed_one, inv_one)
    )
    grad_mod = jnp.concatenate(
        [grad_shift_one, grad_scale_one, grad_gate_one, grad_shift_two, grad_scale_two, grad_gate_two],
        axis=1,
    ).astype(BF16)

    group_mod = gather_ordered(grad_mod, shard).reshape(shard.size * slots, -1)
    grad_silu = gather_ordered(dot_nt(group_mod, ada_weight), shard)
    grad_silu = lax.dynamic_slice_in_dim(grad_silu, shard.index * slots, slots, 1)
    grad_silu = jnp.swapaxes(grad_silu, 0, 1).reshape(slots, width)
    cond_wide = condition.astype(F32)
    logistic = jax.nn.sigmoid(cond_wide)
    grad_cond = grad_silu * logistic * (1.0 + cond_wide * (1.0 - logistic))

    steps = [(rep, bit) for bit in reversed(rep.bits)] + [(shard, bit) for bit in reversed(shard.bits)]
    silu_own = jax.nn.silu(cond_wide).astype(BF16)
    silu_all = gather_any_order(silu_own, steps)
    mod_all = gather_any_order(grad_mod, steps)
    silu_cols = lax.dynamic_slice_in_dim(silu_all, shard.index * depth, depth, 1)
    grad_ada_w = dot_tn(silu_cols, mod_all)
    ada_b_all = jnp.sum(mod_all.astype(F32), axis=0)
    grad_ada_b = lax.dynamic_slice_in_dim(
        ada_b_all, shard.index * ada_bias.shape[0], ada_bias.shape[0], 0
    )

    bias_grads = jnp.concatenate(
        [v.reshape(shard.size, -1) for v in (grad_qv_b, grad_proj_b, grad_fc1_b, grad_fc2_b)], axis=1
    )
    bias_sum = scatter_sum(bias_grads, shard, F32).reshape(-1, 128)
    for bit in rep.bits:
        bias_sum = bias_sum + rep.swap(bias_sum, bit)
    bias_sum = bias_sum.reshape(-1)
    bias_out = []
    start = 0
    for bias in (qv_bias, proj_bias, fc1_bias, fc2_bias):
        bias_out.append(bias_sum[start : start + bias.shape[0]])
        start += bias.shape[0]

    return (
        block_out,
        grad_tokens,
        grad_cond,
        grad_ada_w,
        grad_ada_b,
        grad_qkv_w,
        bias_out[0],
        grad_proj_w,
        bias_out[1],
        grad_fc1_w,
        bias_out[2],
        grad_fc2_w,
        bias_out[3],
    )


def solution(mesh):
    rows = P(("rep", "shard"), None)
    weights = (P("shard", None), P("shard"))
    return jax.shard_map(
        functools.partial(per_device, mesh.shape["shard"], mesh.shape["rep"]),
        mesh=mesh,
        in_specs=(rows, rows, P(("rep", "shard")), rows) + weights * 5,
        out_specs=(rows, rows, rows) + weights * 5,
        check_vma=False,
    )
```

```python
import functools

import jax
import jax.numpy as jnp
from jax import lax
from jax.experimental import pallas as pl
from jax.experimental.pallas import tpu as pltpu
from jax.sharding import PartitionSpec as P

HEADS = 12
HEAD_DIM = 64
EPS = 1e-06
GELU_C = 0.7978845608028654
GELU_A = 0.044715
F32 = jnp.float32
BF16 = jnp.bfloat16
VMEM_LIMIT = 56 * 1024 * 1024


def norm_back(grad_hat, normed, inv_std):
    return inv_std * (
        grad_hat
        - jnp.mean(grad_hat, axis=-1, keepdims=True)
        - normed * jnp.mean(grad_hat * normed, axis=-1, keepdims=True)
    )


def gelu_pair(pre_act):
    square = pre_act * pre_act
    tanh_val = jnp.tanh(pre_act * (GELU_C + GELU_C * GELU_A * square))
    half = 0.5 + 0.5 * tanh_val
    activated = pre_act * half
    derivative = half + activated * (1.0 - tanh_val) * (GELU_C + 3.0 * GELU_C * GELU_A * square)
    return (activated, derivative)


def dot_nn(left, right):
    return lax.dot_general(left, right, (((1,), (0,)), ((), ())), preferred_element_type=F32)


def dot_nt(left, right):
    return lax.dot_general(left, right, (((1,), (1,)), ((), ())), preferred_element_type=F32)


def dot_tn(left, right):
    return lax.dot_general(left, right, (((0,), (0,)), ((), ())), preferred_element_type=F32)


def specs(count, space=pltpu.VMEM):
    return [pl.BlockSpec(memory_space=space)] * count


def shape(dims, dtype):
    return jax.ShapeDtypeStruct(dims, dtype)


COST_SHARE = 0.0


def params(flops=0, bytes_moved=0, exps=0):
    return dict(
        compiler_params=pltpu.CompilerParams(vmem_limit_bytes=VMEM_LIMIT),
        cost_estimate=pl.CostEstimate(
            flops=int(COST_SHARE * flops),
            bytes_accessed=int(COST_SHARE * bytes_moved),
            transcendentals=int(COST_SHARE * exps),
        ),
    )


def high_bit(spot_ref, number, bit):
    return lax.rem(lax.div(spot_ref[number], jnp.int32(bit)), jnp.int32(2))


def piece_copies(refs, offsets, spot_ref, whole, sems):
    copies = []
    for k, (ref, offset) in enumerate(zip(refs, offsets)):
        count = ref.shape[0]
        place = whole.at[pl.ds(pl.multiple_of((spot_ref[0] ^ offset) * count, 16), count), :]
        copies.append(pltpu.make_async_copy(ref, place, sems.at[k]))
    return copies


def row_norm(value):
    center = value - jnp.mean(value, axis=-1, keepdims=True)
    inv_std = lax.rsqrt(jnp.mean(center * center, axis=-1, keepdims=True) + EPS)
    return center * inv_std, inv_std


def mod_part(mod_ref, slot, part, width):
    return mod_ref[slot : slot + 1, part * width : (part + 1) * width]


def qkv_kernel(offsets, slots, *refs):
    count = len(offsets)
    spot_ref, tok_ref, mod_ref, bias_ref = refs[:4]
    pieces = refs[4 : 4 + count]
    hidden_ref, qkv_ref, whole, sems = refs[4 + count :]
    copies = piece_copies(pieces, offsets, spot_ref, whole, sems)
    for copy in copies:
        copy.start()
    rows, width = tok_ref.shape
    seq = rows // slots
    for slot in range(slots):
        at = pl.ds(slot * seq, seq)
        normed, _ = row_norm(tok_ref[at, :].astype(F32))
        scale = 1.0 + mod_part(mod_ref, slot, 1, width)
        hidden_ref[at, :] = (normed * scale + mod_part(mod_ref, slot, 0, width)).astype(BF16)
    for copy in copies:
        copy.wait()
    for part in range(3):
        cols = pl.ds(part * width, width)
        qkv_ref[:, cols] = (
            dot_nn(hidden_ref[...], whole[:, cols]) + bias_ref[:, cols]
        ).astype(BF16)


def qkv_call(spot, tokens, modulation, bias, weight, slots):
    rows, width = tokens.shape
    pieces, offsets = weight
    return pl.pallas_call(
        functools.partial(qkv_kernel, offsets, slots),
        in_specs=specs(1, pltpu.SMEM) + specs(3) + specs(len(pieces), pl.ANY),
        out_specs=specs(2),
        out_shape=[shape((rows, width), BF16), shape((rows, 3 * width), BF16)],
        scratch_shapes=[
            pltpu.VMEM((width, 3 * width), BF16),
            pltpu.SemaphoreType.DMA((len(pieces),)),
        ],
        name="qkv_fwd",
        **params(6 * rows * width * width, 10 * rows * width + 6 * width * width),
    )(spot, tokens, modulation, bias, *pieces)


def pair_masks(rows):
    lane = lax.broadcasted_iota(jnp.int32, (rows, 2 * HEAD_DIM), 1)
    return lane < HEAD_DIM


def head_probs(query_pair, key_pair, first, head):
    keep = first if head == 0 else jnp.logical_not(first)
    query_head = jnp.where(keep, query_pair, jnp.zeros_like(query_pair))
    scores = dot_nt(query_head, key_pair) * HEAD_DIM ** (-0.5)
    row_max = jnp.max(scores, axis=-1, keepdims=True)
    exped = jnp.exp(scores - row_max)
    return exped * (1.0 / jnp.sum(exped, axis=-1, keepdims=True))


def attn_kernel(offsets, *refs):
    count = len(offsets)
    spot_ref, qkv_ref, tok_ref, cot_ref, mod_ref, bias_ref = refs[:6]
    pieces = refs[6 : 6 + count]
    mixed_ref, branch_ref, hidden_ref, low_ref, whole, sems = refs[6 + count :]
    rows, width = tok_ref.shape
    copies = piece_copies(pieces, offsets, spot_ref, whole, sems)

    @pl.when(pl.program_id(0) == 0)
    def _():
        for copy in copies:
            copy.start()

    first = pair_masks(rows)
    for pair in range(HEADS // 2):
        cols = pl.ds(pair * 128, 128)
        query_pair = qkv_ref[:, cols]
        key_pair = qkv_ref[:, pl.ds(width + pair * 128, 128)]
        value_pair = qkv_ref[:, pl.ds(2 * width + pair * 128, 128)]
        parts = []
        for head in range(2):
            probs_low = head_probs(query_pair, key_pair, first, head).astype(BF16)
            parts.append(dot_nn(probs_low, value_pair))
        mixed_ref[:, cols] = jnp.where(first, parts[0], parts[1]).astype(BF16)

    @pl.when(pl.program_id(0) == 0)
    def _():
        for copy in copies:
            copy.wait()

    mod = mod_ref[0]
    branch = dot_nn(mixed_ref[...], whole[...]) + bias_ref[...]
    branch_ref[...] = branch
    normed, _ = row_norm(tok_ref[...].astype(F32) + mod_part(mod, 0, 2, width) * branch)
    scale = 1.0 + mod_part(mod, 0, 4, width)
    hidden_ref[...] = (normed * scale + mod_part(mod, 0, 3, width)).astype(BF16)
    low_ref[...] = (mod_part(mod, 0, 5, width) * cot_ref[...].astype(F32)).astype(BF16)


def attn_call(spot, qkv, tokens, cot, modulation, bias, weight, slots):
    rows, width = tokens.shape
    seq = rows // slots
    pieces, offsets = weight
    by_slot = pl.BlockSpec((seq, width), lambda s: (s, 0))
    return pl.pallas_call(
        functools.partial(attn_kernel, offsets),
        grid=(slots,),
        in_specs=specs(1, pltpu.SMEM)
        + [
            pl.BlockSpec((seq, 3 * width), lambda s: (s, 0)),
            by_slot,
            by_slot,
            pl.BlockSpec((1, 1, 6 * width), lambda s: (s, 0, 0)),
            pl.BlockSpec((1, width), lambda s: (0, 0)),
        ]
        + specs(len(pieces), pl.ANY),
        out_specs=[by_slot] * 4,
        out_shape=[
            shape((rows, width), BF16),
            shape((rows, width), F32),
            shape((rows, width), BF16),
            shape((rows, width), BF16),
        ],
        scratch_shapes=[
            pltpu.VMEM((width, width), BF16),
            pltpu.SemaphoreType.DMA((len(pieces),)),
        ],
        name="attn_fwd",
        **params(
            2 * rows * width * width + 4 * rows * width * seq * 4,
            24 * rows * width,
            rows * seq * HEADS,
        ),
    )(spot, qkv, tokens, cot, modulation[:, None, :], bias, *pieces)


FF_BLOCK = 512


def gelu_kernel(offsets, *refs):
    count = len(offsets)
    spot_ref, hidden_ref, bias_ref = refs[:3]
    pieces = refs[3 : 3 + count]
    act_ref, deriv_ref, whole, sems = refs[3 + count :]
    step = pl.program_id(0)

    @pl.when(step == 0)
    def _():
        copies = piece_copies(pieces, offsets, spot_ref, whole, sems)
        for copy in copies:
            copy.start()
        for copy in copies:
            copy.wait()

    cols = pl.ds(pl.multiple_of(step * FF_BLOCK, FF_BLOCK), FF_BLOCK)
    pre_act = dot_nn(hidden_ref[...], whole[:, cols]) + bias_ref[...]
    activated, derivative = gelu_pair(pre_act)
    act_ref[...] = activated.astype(BF16)
    deriv_ref[...] = derivative


def gelu_call(spot, hidden, bias, weight):
    rows, width = hidden.shape
    pieces, offsets = weight
    hidden_units = bias.shape[1]
    block = pl.BlockSpec((rows, FF_BLOCK), lambda j: (0, j))
    return pl.pallas_call(
        functools.partial(gelu_kernel, offsets),
        grid=(hidden_units // FF_BLOCK,),
        in_specs=specs(1, pltpu.SMEM)
        + [
            pl.BlockSpec((rows, width), lambda j: (0, 0)),
            pl.BlockSpec((1, FF_BLOCK), lambda j: (0, j)),
        ]
        + specs(len(pieces), pl.ANY),
        out_specs=[block, block],
        out_shape=[shape((rows, hidden_units), BF16), shape((rows, hidden_units), F32)],
        scratch_shapes=[
            pltpu.VMEM((width, hidden_units), BF16),
            pltpu.SemaphoreType.DMA((len(pieces),)),
        ],
        name="fc1_gelu",
        **params(
            2 * rows * width * hidden_units, 8 * rows * hidden_units, rows * hidden_units
        ),
    )(spot, hidden, bias, *pieces)


def out_kernel(offsets, slots, *refs):
    count = len(offsets)
    spot_ref, live_ref, act_ref, tok_ref, branch_ref, cot_ref, mod_ref, bias_ref = refs[:8]
    pieces = refs[8 : 8 + count]
    block_ref, gate_ref, whole, sems = refs[8 + count :]
    copies = piece_copies(pieces, offsets, spot_ref, whole, sems)
    for copy in copies:
        copy.start()
    for copy in copies:
        copy.wait()
    rows, width = tok_ref.shape
    seq = rows // slots
    for slot in range(slots):
        at = pl.ds(slot * seq, seq)
        branch_two = dot_nn(act_ref[at, :], whole[...]) + bias_ref[...]
        gate_ref[slot : slot + 1, :] = jnp.sum(
            cot_ref[at, :].astype(F32) * branch_two, axis=0, keepdims=True
        )
        mid = tok_ref[at, :].astype(F32) + mod_part(mod_ref, slot, 2, width) * branch_ref[at, :]
        block = mid + mod_part(mod_ref, slot, 5, width) * branch_two
        block_ref[at, :] = jnp.where(live_ref[0] > slot, block, 0.0).astype(BF16)


def out_call(spot, counts, act_low, tokens, branch_one, cot, modulation, bias, weight, slots):
    rows, width = tokens.shape
    hidden_units = act_low.shape[1]
    pieces, offsets = weight
    return pl.pallas_call(
        functools.partial(out_kernel, offsets, slots),
        in_specs=specs(2, pltpu.SMEM) + specs(6) + specs(len(pieces), pl.ANY),
        out_specs=specs(2),
        out_shape=[shape((rows, width), BF16), shape((slots, width), F32)],
        scratch_shapes=[
            pltpu.VMEM((hidden_units, width), BF16),
            pltpu.SemaphoreType.DMA((len(pieces),)),
        ],
        name="fc2_fwd",
        **params(2 * rows * width * hidden_units, 2 * (rows + width) * hidden_units),
    )(spot, counts, act_low, tokens, branch_one, cot, modulation, bias, *pieces)


def mlp_bwd_kernel(offsets, slots, *refs):
    count = len(offsets)
    spot_ref, low_ref, deriv_ref, tok_ref, branch_ref, cot_ref, mod_ref = refs[:7]
    one_pieces = refs[7 : 7 + count]
    two_pieces = refs[7 + count : 7 + 2 * count]
    (low_pre_ref, fc1_b_ref, mid_ref, low_one_ref, sums_ref, one, two, acc, sems_one, sems_two) = refs[
        7 + 2 * count :
    ]
    step = pl.program_id(0)
    copies_two = piece_copies(two_pieces, offsets, spot_ref, two, sems_two)
    copies_one = piece_copies(one_pieces, offsets, spot_ref, one, sems_one)

    @pl.when(step == 0)
    def _():
        for copy in copies_two + copies_one:
            copy.start()
        acc[...] = jnp.zeros_like(acc)
        for copy in copies_two:
            copy.wait()

    ff = pl.ds(pl.multiple_of(step * FF_BLOCK, FF_BLOCK), FF_BLOCK)
    grad_pre = dot_nt(low_ref[...], two[ff, :]) * deriv_ref[...]
    fc1_b_ref[...] = jnp.sum(grad_pre, axis=0, keepdims=True)
    low_pre = grad_pre.astype(BF16)
    low_pre_ref[...] = low_pre

    @pl.when(step == 0)
    def _():
        for copy in copies_one:
            copy.wait()

    acc[...] += dot_nt(low_pre, one[:, ff])

    @pl.when(step == pl.num_programs(0) - 1)
    def _():
        rows, width = tok_ref.shape
        seq = rows // slots
        for slot in range(slots):
            at = pl.ds(slot * seq, seq)
            branch = branch_ref[at, :]
            cot = cot_ref[at, :].astype(F32)
            gate_one = mod_part(mod_ref, slot, 2, width)
            normed, inv_std = row_norm(tok_ref[at, :].astype(F32) + gate_one * branch)
            grad_hidden = acc[at, :]
            scale = 1.0 + mod_part(mod_ref, slot, 4, width)
            grad_mid = cot + norm_back(grad_hidden * scale, normed, inv_std)
            mid_ref[at, :] = grad_mid
            grad_branch = gate_one * grad_mid
            low_one_ref[at, :] = grad_branch.astype(BF16)

            def put(part, value):
                sums_ref[part, slot : slot + 1, :] = jnp.sum(value, axis=0, keepdims=True)

            put(0, grad_mid * branch)
            put(1, grad_hidden)
            put(2, grad_hidden * normed)
            put(3, grad_branch)
            put(4, mod_part(mod_ref, slot, 5, width) * cot)


def mlp_bwd_call(spot, low_two, derivative, tokens, branch_one, cot, modulation, one, two, slots):
    rows, width = tokens.shape
    hidden_units = derivative.shape[1]
    block = pl.BlockSpec((rows, FF_BLOCK), lambda j: (0, j))
    whole = pl.BlockSpec((rows, width), lambda j: (0, 0))
    return pl.pallas_call(
        functools.partial(mlp_bwd_kernel, one[1], slots),
        grid=(hidden_units // FF_BLOCK,),
        in_specs=specs(1, pltpu.SMEM)
        + [whole, block, whole, whole, whole, pl.BlockSpec((slots, 6 * width), lambda j: (0, 0))]
        + specs(len(one[0]) + len(two[0]), pl.ANY),
        out_specs=[
            block,
            pl.BlockSpec((1, FF_BLOCK), lambda j: (0, j)),
            whole,
            whole,
            pl.BlockSpec((5, slots, width), lambda j: (0, 0, 0)),
        ],
        out_shape=[
            shape((rows, hidden_units), BF16),
            shape((1, hidden_units), F32),
            shape((rows, width), F32),
            shape((rows, width), BF16),
            shape((5, slots, width), F32),
        ],
        scratch_shapes=[
            pltpu.VMEM((width, hidden_units), BF16),
            pltpu.VMEM((hidden_units, width), BF16),
            pltpu.VMEM((rows, width), F32),
            pltpu.SemaphoreType.DMA((len(one[0]),)),
            pltpu.SemaphoreType.DMA((len(two[0]),)),
        ],
        name="mlp_bwd",
        **params(4 * rows * width * hidden_units, 6 * rows * hidden_units + 4 * width * hidden_units),
    )(spot, low_two, derivative, tokens, branch_one, cot, modulation, *one[0], *two[0])


def attn_bwd_kernel(qkv_ref, grad_ref, out_ref, bias_ref):
    rows = qkv_ref.shape[0]
    width = grad_ref.shape[1]
    first = pair_masks(rows)
    for pair in range(HEADS // 2):
        query_cols = pl.ds(pair * 128, 128)
        key_cols = pl.ds(width + pair * 128, 128)
        value_cols = pl.ds(2 * width + pair * 128, 128)
        query_pair = qkv_ref[:, query_cols]
        key_pair = qkv_ref[:, key_cols]
        value_pair = qkv_ref[:, value_cols]
        grad_pair = grad_ref[:, query_cols]
        grads = []
        for head in range(2):
            keep = first if head == 0 else jnp.logical_not(first)
            probs = head_probs(query_pair, key_pair, first, head)
            grad_head = jnp.where(keep, grad_pair, jnp.zeros_like(grad_pair))
            grad_probs = dot_nt(grad_head, value_pair)
            row_dot = jnp.sum(probs * grad_probs, axis=-1, keepdims=True)
            grad_scores = (probs * (grad_probs - row_dot) * HEAD_DIM ** (-0.5)).astype(BF16)
            grads.append(
                (
                    dot_nn(grad_scores, key_pair),
                    dot_tn(grad_scores, query_pair),
                    dot_tn(probs.astype(BF16), grad_pair),
                )
            )
        grad_query, grad_key, grad_value = (
            jnp.where(first, left, right) for left, right in zip(grads[0], grads[1])
        )
        out_ref[:, query_cols] = grad_query.astype(BF16)
        out_ref[:, key_cols] = grad_key.astype(BF16)
        out_ref[:, value_cols] = grad_value.astype(BF16)
        bias_ref[0, :, query_cols] = jnp.sum(grad_query, axis=0, keepdims=True)
        bias_ref[0, :, key_cols] = jnp.sum(grad_value, axis=0, keepdims=True)


def attn_bwd_call(qkv, grad_mixed, slots):
    rows, width = grad_mixed.shape
    seq = rows // slots
    return pl.pallas_call(
        attn_bwd_kernel,
        grid=(slots,),
        in_specs=[
            pl.BlockSpec((seq, 3 * width), lambda s: (s, 0)),
            pl.BlockSpec((seq, width), lambda s: (s, 0)),
        ],
        out_specs=[
            pl.BlockSpec((seq, 3 * width), lambda s: (s, 0)),
            pl.BlockSpec((1, 1, 2 * width), lambda s: (s, 0, 0)),
        ],
        out_shape=[
            shape((rows, 3 * width), BF16),
            shape((slots, 1, 2 * width), F32),
        ],
        name="attn_bwd",
        **params(20 * rows * width * seq, 16 * rows * width, rows * seq * HEADS),
    )(qkv, grad_mixed)


def mixed_bwd_kernel(offsets, *refs):
    count = len(offsets)
    spot_ref, low_ref = refs[:2]
    pieces = refs[2 : 2 + count]
    out_ref, whole, sems = refs[2 + count :]
    copies = piece_copies(pieces, offsets, spot_ref, whole, sems)
    for copy in copies:
        copy.start()
    for copy in copies:
        copy.wait()
    out_ref[...] = dot_nt(low_ref[...], whole[...]).astype(BF16)


def mixed_bwd_call(spot, low_one, weight):
    rows, width = low_one.shape
    pieces, offsets = weight
    return pl.pallas_call(
        functools.partial(mixed_bwd_kernel, offsets),
        in_specs=specs(1, pltpu.SMEM) + specs(1) + specs(len(pieces), pl.ANY),
        out_specs=pl.BlockSpec(memory_space=pltpu.VMEM),
        out_shape=shape((rows, width), BF16),
        scratch_shapes=[
            pltpu.VMEM((width, width), BF16),
            pltpu.SemaphoreType.DMA((len(pieces),)),
        ],
        name="proj_bwd",
        **params(2 * rows * width * width, 4 * rows * width + 2 * width * width),
    )(spot, low_one, *pieces)


def input_bwd_kernel(offsets, slots, *refs):
    count = len(offsets)
    spot_ref, grad_ref, tok_ref, mid_ref, mod_ref, sums_ref, gate_ref, cond_ref = refs[:8]
    pieces = refs[8 : 8 + count]
    out_ref, mod_out, whole, sems = refs[8 + count :]
    copies = piece_copies(pieces, offsets, spot_ref, whole, sems)
    for copy in copies:
        copy.start()
    for copy in copies:
        copy.wait()
    rows, width = tok_ref.shape
    seq = rows // slots

    def put(slot, part, value):
        mod_out[slot : slot + 1, part * width : (part + 1) * width] = value.astype(BF16)

    for slot in range(slots):
        at = pl.ds(slot * seq, seq)
        row = slice(slot, slot + 1)
        grad_hidden = dot_nt(grad_ref[at, :], whole[...])
        normed, inv_std = row_norm(tok_ref[at, :].astype(F32))
        scale = 1.0 + mod_part(mod_ref, slot, 1, width)
        out_ref[at, :] = mid_ref[at, :] + norm_back(grad_hidden * scale, normed, inv_std)
        put(slot, 0, jnp.sum(grad_hidden, axis=0, keepdims=True))
        put(slot, 1, jnp.sum(grad_hidden * normed, axis=0, keepdims=True))
        for part in range(3):
            put(slot, 2 + part, sums_ref[part, row, :])
        put(slot, 5, gate_ref[row, :])
        cond = cond_ref[row, :].astype(F32)
        put(slot, 6, cond * (1.0 / (1.0 + jnp.exp(-cond))))


def input_bwd_call(spot, grad_qkv, tokens, grad_mid, modulation, sums, gate_sums, condition, weight, slots):
    rows, width = tokens.shape
    pieces, offsets = weight
    return pl.pallas_call(
        functools.partial(input_bwd_kernel, offsets, slots),
        in_specs=specs(1, pltpu.SMEM) + specs(7) + specs(len(pieces), pl.ANY),
        out_specs=specs(2),
        out_shape=[shape((rows, width), F32), shape((slots, 7 * width), BF16)],
        scratch_shapes=[
            pltpu.VMEM((width, 3 * width), BF16),
            pltpu.SemaphoreType.DMA((len(pieces),)),
        ],
        name="qkv_bwd",
        **params(6 * rows * width * width, 16 * rows * width + 6 * width * width),
    )(spot, grad_qkv, tokens, grad_mid, modulation, sums, gate_sums, condition, *pieces)


def split_store(core, total, depth, keep_ref, send_ref, cols):
    for far in range(total.shape[0] // (2 * depth)):
        even = total[2 * far * depth : (2 * far + 1) * depth]
        odd = total[(2 * far + 1) * depth : (2 * far + 2) * depth]
        keep_ref[far, :, cols] = jnp.where(core == 0, even, odd)
        send_ref[far, :, cols] = jnp.where(core == 0, odd, even).astype(BF16)


def wide_grad_kernel(spot_ref, left_ref, right_ref, keep_ref, send_ref):
    total = dot_tn(left_ref[...], right_ref[...])
    split_store(spot_ref[0] & 1, total, keep_ref.shape[1], keep_ref, send_ref, slice(None))


def wide_grad(spot, left, right, shards, name):
    rows, in_dim = left.shape
    out_dim = right.shape[1]
    depth = in_dim // shards
    block = 512 if out_dim % 512 == 0 else 256
    per_step = shards // 2 if in_dim <= 768 else 1
    out_block = pl.BlockSpec((per_step, depth, block), lambda i, j: (i, 0, j))
    dims = (shards // 2, depth, out_dim)
    return pl.pallas_call(
        wide_grad_kernel,
        grid=(shards // 2 // per_step, out_dim // block),
        in_specs=specs(1, pltpu.SMEM)
        + [
            pl.BlockSpec((rows, 2 * depth * per_step), lambda i, j: (0, i)),
            pl.BlockSpec((rows, block), lambda i, j: (0, j)),
        ],
        out_specs=[out_block, out_block],
        out_shape=[shape(dims, F32), shape(dims, BF16)],
        name=name,
        **params(2 * rows * in_dim * out_dim, 3 * in_dim * out_dim + 2 * rows * (in_dim + out_dim)),
    )(spot, left, right)


EXTRA = 256


def bias_rows(count):
    return [(start, min(EXTRA, count - start)) for start in range(0, count, EXTRA)]


def attn_grad_kernel(shards, *refs):
    spot_ref, hidden_ref, qkv_ref, mixed_ref, low_ref, qv_ref, sums_ref, fc1_ref = refs[:8]
    keep_a, send_a, keep_b, send_b, extra = refs[8:]
    depth = keep_a.shape[1]
    width = hidden_ref.shape[1]
    core = spot_ref[0] & 1
    for part, (keep_ref, send_ref) in enumerate([(keep_a, send_a)] * 2 + [(keep_b, send_b)]):
        total = dot_tn(hidden_ref[...], qkv_ref[:, pl.ds(part * width, width)])
        split_store(core, total, depth, keep_ref, send_ref, pl.ds(part % 2 * width, width))
    total = dot_tn(mixed_ref[...], low_ref[...])
    split_store(core, total, depth, keep_b, send_b, pl.ds(width, width))
    extra[...] = jnp.zeros_like(extra)
    biases = (
        jnp.sum(qv_ref[...], axis=0),
        jnp.sum(sums_ref[3], axis=0, keepdims=True),
        fc1_ref[...],
        jnp.sum(sums_ref[4], axis=0, keepdims=True),
    )
    for place in range(shards):
        row = place * depth
        for bias in biases:
            count = bias.shape[1] // shards
            for start, size in bias_rows(count):
                first = place * count + start
                extra[row : row + 1, :size] = bias[:, first : first + size]
                row += 1
    split_store(core, extra[...], depth, keep_b, send_b, pl.ds(2 * width, EXTRA))


def attn_grad(spot, hidden, grad_qkv, mixed, low_one, qv_sums, sums, fc1_sums, shards):
    rows, width = hidden.shape
    first = (shards // 2, width // shards, 2 * width)
    second = (shards // 2, width // shards, 2 * width + EXTRA)
    outs = pl.pallas_call(
        functools.partial(attn_grad_kernel, shards),
        in_specs=specs(1, pltpu.SMEM) + specs(7),
        out_specs=specs(4),
        out_shape=[shape(first, F32), shape(first, BF16), shape(second, F32), shape(second, BF16)],
        scratch_shapes=[pltpu.VMEM((width, EXTRA), F32)],
        name="attn_weight_grads",
        **params(8 * rows * width * width, 12 * width * width + 14 * rows * width),
    )(spot, hidden, grad_qkv, mixed, low_one, qv_sums, sums, fc1_sums)
    return outs[:2], outs[2:]


def round_kernel(kinds, spot_ref, *refs):
    ins = list(refs[: sum(kind[1] for kind in kinds)])
    outs = list(refs[len(ins) :])
    for kind, count in kinds:
        args, ins = ins[:count], ins[count:]
        if kind == "halve":
            keep_out, send_out, outs = outs[0], outs[1], outs[2:]
            keep_out[...] = args[0][...] + args[2][...].astype(F32)
            send_out[...] = (args[1][...] + args[3][...].astype(F32)).astype(BF16)
        elif kind == "merge":
            keep_out, send_out, outs = outs[0], outs[1], outs[2:]
            half = keep_out.shape[2] // 2
            for part in range(2):
                mine, other, sent_mine, sent_other = args[4 * part : 4 * part + 4]
                cols = slice(part * half, (part + 1) * half)
                keep_out[:, :, cols] = mine[...] + sent_mine[...].astype(F32)
                send_out[:, :, cols] = (other[...] + sent_other[...].astype(F32)).astype(BF16)
        elif kind == "add":
            out, outs = outs[0], outs[1:]
            out[...] = (args[0][...].astype(F32) + args[1][...].astype(F32)).astype(BF16)
        else:
            out, outs = outs[0], outs[1:]
            rows = args[0].shape[1]
            out[:, :rows, :] = args[0][...]
            out[:, rows:, :] = args[1][...]


def round_call(spot, jobs):
    split = 2
    for job in jobs:
        cols = job["args"][0].shape[2] // (1 if job.get("part") is None else 2)
        if job["kind"] == "merge" or cols % 256:
            split = 1
    in_specs, args, out_specs, out_shape = [], [], [], []

    def halves_of(value, axis, bit, dim, base, dims, chunk):
        def spec(other):
            def place(j, spot_ref):
                half = high_bit(spot_ref, axis.number, bit)
                half = 1 - half if other else half
                return (half, 0, base + j) if dim == 0 else (0, half, base + j)

            return pl.BlockSpec((dims[0], dims[1], chunk), place)

        in_specs.extend([spec(False), spec(True)])
        args.extend([value, value])

    def plain(dims):
        return pl.BlockSpec((dims[0], dims[1], dims[2] // split), lambda j, spot_ref: (0, 0, j))

    kinds = []
    for job in jobs:
        values = job["args"]
        kind = job["kind"]
        dims = list(values[0].shape)
        before = len(args)
        if kind in ("halve", "merge"):
            axis, bit, dim = job["step"]
            dims[dim] //= 2
            part = job.get("part")
            if part is not None:
                dims[2] //= 2
            chunk = dims[2] // split
            base = 0 if part is None else part * split
            for value in values:
                halves_of(value, axis, bit, dim, base, dims, chunk)
            if kind == "merge":
                dims[2] *= 2
            out_specs += [plain(dims)] * 2
            out_shape += [shape(tuple(dims), F32), shape(tuple(dims), BF16)]
        else:
            in_specs += [plain(value.shape) for value in values]
            args += values
            if kind == "cat":
                dims[1] += values[1].shape[1]
            out_specs.append(plain(dims))
            out_shape.append(shape(tuple(dims), BF16))
        kinds.append((kind, len(args) - before))
    outs = pl.pallas_call(
        functools.partial(round_kernel, kinds),
        grid_spec=pltpu.PrefetchScalarGridSpec(
            num_scalar_prefetch=1, grid=(split,), in_specs=in_specs, out_specs=out_specs
        ),
        out_shape=out_shape,
        name="sum_round",
        **params(0, 0),
    )(spot, *args)
    outs = list(outs)
    results = []
    for kind, _ in kinds:
        count = 2 if kind in ("halve", "merge") else 1
        results.append(outs[:count])
        outs = outs[count:]
    return results


def first_row(spot_ref, terms, flips):
    row = 0
    for (number, bit, size), flip in zip(terms, flips):
        half = high_bit(spot_ref, number, bit)
        row = row + (1 - half if flip else half) * size
    return row


def row_places(spot_ref, refs, terms, flips, count):
    parts = []
    for ref in refs:
        parts += [(ref, slice(k * count, (k + 1) * count)) for k in range(ref.shape[1] // count)]
    for (ref, rows), flip in zip(parts, flips):
        at = first_row(spot_ref, terms, flip)
        if not isinstance(at, int):
            at = pl.multiple_of(at, 16)
        yield ref, rows, pl.ds(at, count)


def place_kernel(terms, flips, count, spot_ref, *refs):
    out_ref = refs[-1]
    for ref, rows, at in row_places(spot_ref, refs[:-1], terms, flips, count):
        out_ref[at, :] = ref[0, rows, :].astype(F32)


def place_rows(spot, done, rows):
    pieces, terms, flips, count = done
    cols = pieces[0].shape[2]
    return pl.pallas_call(
        functools.partial(place_kernel, terms, flips, count),
        in_specs=specs(1, pltpu.SMEM) + specs(len(pieces)),
        out_specs=pl.BlockSpec(memory_space=pltpu.VMEM),
        out_shape=shape((rows, cols), F32),
        name="place_rows",
        **params(0, rows * cols * 6),
    )(spot, *pieces)


def place_attn_kernel(plans, parts, biases, spot_ref, *refs):
    qkv_out, proj_out, *bias_outs, head = refs[2 * parts :]
    width = proj_out.shape[1]
    for ref, rows, at in row_places(spot_ref, refs[:parts], *plans[0]):
        qkv_out[at, : 2 * width] = ref[0, rows, :].astype(F32)
    for ref, rows, at in row_places(spot_ref, refs[parts : 2 * parts], *plans[1]):
        qkv_out[at, 2 * width :] = ref[0, rows, :width].astype(F32)
        proj_out[at, :] = ref[0, rows, width : 2 * width].astype(F32)
        head[at, :] = ref[0, rows, 2 * width :].astype(F32)
    row = 0
    for count, out in zip(biases, bias_outs):
        for start, size in bias_rows(count):
            out[:, start : start + size] = head[row : row + 1, :size]
            row += 1


def place_attn(spot, first, second, rows, width, biases):
    parts = len(first[0])
    return pl.pallas_call(
        functools.partial(place_attn_kernel, (first[1:], second[1:]), parts, biases),
        in_specs=specs(1, pltpu.SMEM) + specs(2 * parts),
        out_specs=specs(2 + len(biases)),
        out_shape=[shape((rows, 3 * width), F32), shape((rows, width), F32)]
        + [shape((1, count), F32) for count in biases],
        scratch_shapes=[pltpu.VMEM((rows, EXTRA), F32)],
        name="place_attn",
        **params(0, rows * width * 24),
    )(spot, *first[0], *second[0])


def cond_kernel(shards, spot_ref, grad_ref, cond_ref, out_ref):
    slots, width = cond_ref.shape
    depth = width // shards
    group = shards * slots
    for place in range(shards):
        total = jnp.zeros((slots, depth), F32)
        for offset in range(shards):
            first = offset * group + offset * slots
            part = grad_ref[first : first + slots, :]
            total = total + jnp.where((spot_ref[0] ^ offset) == place, part, 0.0)
        cond = cond_ref[:, place * depth : (place + 1) * depth].astype(F32)
        logistic = 1.0 / (1.0 + jnp.exp(-cond))
        out_ref[:, place * depth : (place + 1) * depth] = (
            total * logistic * (1.0 + cond * (1.0 - logistic))
        )


def cond_call(spot, grads, condition, shards):
    return pl.pallas_call(
        functools.partial(cond_kernel, shards),
        in_specs=specs(1, pltpu.SMEM) + specs(2),
        out_specs=pl.BlockSpec(memory_space=pltpu.VMEM),
        out_shape=shape(condition.shape, F32),
        name="grad_condition",
        **params(),
    )(spot, grads, condition)


def after(value, *others):
    return lax.optimization_barrier((value,) + others)[0]


class Axis:
    def __init__(self, name, size, number):
        self.name = name
        self.size = size
        self.number = number
        self.index = lax.axis_index(name)
        self.bits = [1 << k for k in range(size.bit_length() - 1)]

    def swap(self, value, bit):
        return lax.ppermute(value, self.name, [(i, i ^ bit) for i in range(self.size)])

    def high(self, bit):
        return (self.index & bit) != 0


def ordered(high, mine, other, axis=0):
    return jnp.where(
        high, jnp.concatenate([other, mine], axis), jnp.concatenate([mine, other], axis)
    )


def gather_ordered(value, axis):
    value = value[None]
    for bit in axis.bits:
        value = ordered(axis.high(bit), value, axis.swap(value, bit))
    return value


class Gather:
    def __init__(self, piece, shard):
        self.shard = shard
        self.own = piece
        self.swapped = [(shard.swap(piece, 1), 1)]

    def near(self, *gate):
        self.held = [(self.own, 0)]
        for bit in reversed(self.shard.bits[1:]):
            for value, offset in list(self.held):
                self.held.append((self.shard.swap(after(value, *gate), bit), offset ^ bit))
        return self.held[-1][0]

    def pieces(self, *gate):
        for value, offset in self.held[1:]:
            self.swapped.append((self.shard.swap(after(value, *gate), 1), offset ^ 1))
        held = self.held + self.swapped
        return [value for value, _ in held], tuple(offset for _, offset in held)


def plan(order, rows):
    stages = []
    back = []
    for at, (axis, bit) in enumerate(order):
        if axis.name == "shard":
            stages.append((axis, bit, 0))
        elif rows // 2 % 16 == 0 and at < len(order) - 1:
            rows //= 2
            stages.append((axis, bit, 1))
            back.insert(0, (axis, bit, rows))
        else:
            stages.append((axis, bit, None))
    return stages, back


class Reduction:
    def __init__(self, keep, operand, sent, stages, back):
        self.keep = keep
        self.operand = (operand,)
        self.sent = (sent,)
        self.stages, self.back = stages, back
        self.at = 0
        self.steps = len(stages) + len(back)

    def running(self):
        return self.at < self.steps

    def jobs(self):
        if self.at < len(self.stages):
            dim = self.stages[self.at][2]
            if dim is not None:
                return [dict(kind="halve", args=[self.keep, self.sent[0]], step=self.stages[self.at])]
        if self.at <= len(self.stages):
            return [dict(kind="add", args=[self.keep, self.sent[0]])]
        return [dict(kind="cat", args=[self.whole, self.sent[0]])]

    def commit(self, results):
        if self.at < len(self.stages):
            axis, bit, _ = self.stages[self.at]
            self.keep, operand = results[0][0], results[0][-1]
        else:
            axis, bit, _ = self.back[self.at - len(self.stages)]
            operand = self.whole = results[0][0]
        self.operand = (operand,)
        self.sent = (axis.swap(operand, bit),)
        self.at += 1

    def finish(self):
        terms = [(axis.number, bit, size) for axis, bit, size in self.back]
        flips = [(False,) * len(terms)]
        for k in range(len(terms)):
            flips += [flip[:k] + (True,) + flip[k + 1 :] for flip in flips]
        if self.back:
            pieces = [self.whole, self.sent[0]]
        else:
            total = self.keep.astype(F32) + self.sent[0].astype(F32)
            pieces = [total.astype(BF16)]
        count = sum(piece.shape[1] for piece in pieces) // len(flips)
        return pieces, terms, flips, count


def one_way(pair, shard, order):
    keep, send = pair
    return Reduction(keep, send, shard.swap(send, 1), *plan(order, keep.shape[1]))


class TwoWay:
    def __init__(self, pair, shard, rep):
        self.keeps, send = pair[0], pair[1]
        self.operand = (send,)
        self.sent = (shard.swap(send, 1),)
        inner = [(shard, bit, 0) for bit in reversed(shard.bits[1:])]
        near = (rep, 1, 1)
        self.orders = (inner + [near], [near] + inner)
        rows = self.keeps.shape[1] // 2
        self.stages, self.back = plan([(rep, bit) for bit in rep.bits[1:]], rows)
        self.back = self.back + [(rep, 1, rows)]
        self.round = 0
        self.inner = None

    def running(self):
        return self.inner is None or self.inner.running()

    def jobs(self):
        if self.inner is not None:
            self.inner.sent = self.sent
            return self.inner.jobs()
        if self.round == len(self.orders[0]):
            args = [self.keeps[0], self.sent[0], self.keeps[1], self.sent[1]]
            return [dict(kind="merge", args=args, step=self.stages[0])]
        jobs = []
        for part, order in enumerate(self.orders):
            if self.round == 0:
                jobs.append(dict(args=[self.keeps, self.sent[0]], part=part))
            else:
                jobs.append(dict(args=[self.keeps[part], self.sent[part]]))
            jobs[part].update(kind="halve", step=order[self.round])
        return jobs

    def commit(self, results):
        if self.inner is None and self.round < len(self.orders[0]):
            self.keeps = [keep for keep, _ in results]
            self.operand = tuple(operand for _, operand in results)
            steps = [order[self.round] for order in self.orders]
            self.sent = tuple(
                axis.swap(operand, bit) for (axis, bit, _), operand in zip(steps, self.operand)
            )
            self.round += 1
            return
        if self.inner is None:
            self.inner = Reduction(None, None, None, self.stages, self.back)
        self.inner.commit(results)
        self.operand, self.sent = self.inner.operand, self.inner.sent

    def finish(self):
        self.inner.sent = self.sent
        return self.inner.finish()


def two_way(pair, shard, rep):
    rows = pair[0].shape[1]
    if len(rep.bits) > 1 and rows // 4 % 16 == 0 and shard.size > 2:
        return TwoWay(pair, shard, rep)
    order = [(shard, bit) for bit in reversed(shard.bits[1:])] + [(rep, bit) for bit in rep.bits]
    return one_way(pair, shard, order)


class Chain:
    def __init__(self, value, steps):
        self.value = value
        self.todo = list(steps)
        self.send_next()

    def running(self):
        return self.join is not None

    def send_next(self):
        self.operand = (self.value,)
        axis, bit, self.join = self.todo.pop(0)
        self.sent = (axis.swap(self.value, bit),)

    def jobs(self):
        return []

    def commit(self, results):
        self.value = self.join(self.value, self.sent[0])
        self.join = None
        if self.todo:
            self.send_next()


def together(spot, chains, *values):
    got = lax.optimization_barrier((tuple(chain.sent for chain in chains), values))
    jobs = []
    shares = []
    for chain, sent in zip(chains, got[0]):
        chain.sent = sent
        shares.append(chain.jobs() if chain.running() else [])
        jobs += shares[-1]
    results = round_call(spot, jobs) if jobs else []
    for chain, share in zip(chains, shares):
        if chain.running():
            chain.commit(results[: len(share)])
            results = results[len(share) :]
    return got[1][0] if len(values) == 1 else got[1]


def launched(value, *chains):
    return after(value, *[operand for chain in chains for operand in chain.operand])


def per_device(
    shard_size,
    rep_size,
    tokens,
    condition,
    counts,
    cotangent,
    ada_weight,
    ada_bias,
    qkv_weight,
    qv_bias,
    proj_weight,
    proj_bias,
    fc1_weight,
    fc1_bias,
    fc2_weight,
    fc2_bias,
):
    shard = Axis("shard", shard_size, 0)
    rep = Axis("rep", rep_size, 1)
    spot = jnp.stack([shard.index, rep.index]).astype(jnp.int32)
    slots, width = condition.shape
    seq = tokens.shape[0] // slots
    rows = slots * seq
    depth = ada_weight.shape[0]

    qkv_gather = Gather(qkv_weight, shard)
    proj_gather = Gather(proj_weight, shard)
    fc1_gather = Gather(fc1_weight, shard)
    fc2_gather = Gather(fc2_weight, shard)

    slots_here = condition
    for bit in shard.bits:
        slots_here = jnp.concatenate([slots_here, shard.swap(slots_here, bit)], 0)
    near = proj_gather.near(qkv_gather.near())
    silu_group = jax.nn.silu(slots_here.astype(F32)).astype(BF16)
    my_cols = lax.dynamic_slice_in_dim(silu_group, shard.index * depth, depth, 1)
    own_bias = lax.dynamic_update_slice(
        jnp.zeros((6 * width,), F32), ada_bias.astype(F32), (shard.index * ada_bias.shape[0],)
    )
    modulation = dot_nn(my_cols, ada_weight) + own_bias[None]
    for bit in reversed(shard.bits):
        half = modulation.shape[0] // 2
        modulation = modulation[:half] + shard.swap(modulation[half:], bit)

    bias_list = (qv_bias, proj_bias, fc1_bias, fc2_bias)
    packed = jnp.concatenate([after(qv_bias, slots_here), *bias_list[1:]])
    packed = jnp.pad(packed, (0, -packed.shape[0] % 128)).reshape(-1, 128)
    group = gather_ordered(packed, shard).reshape(shard.size, -1)
    wide = []
    start = 0
    for bias in bias_list:
        wide.append(group[:, start : start + bias.shape[0]].reshape(1, -1).astype(F32))
        start += bias.shape[0]
    qv_b, proj_b, fc1_b, fc2_b = wide

    live_rows = lax.broadcasted_iota(jnp.int32, (rows, 1), 0) < counts[0] * seq
    cot = jnp.where(live_rows, cotangent, jnp.zeros_like(cotangent))

    near_one = fc1_gather.near(near)
    qkv_w = qkv_gather.pieces()
    proj_w = proj_gather.pieces()
    qkv_b = jnp.concatenate([qv_b[:, :width], jnp.zeros((1, width), F32), qv_b[:, width:]], axis=1)
    hidden_one, qkv = qkv_call(spot, tokens, after(modulation, near), qkv_b, qkv_w, slots)
    mixed, branch_one, hidden_two, low_two = attn_call(spot,
        qkv, tokens, cot, modulation, proj_b, proj_w, slots
    )
    fc2_gather.near(near_one, hidden_two)
    fc1_w = fc1_gather.pieces()
    act_low, derivative = gelu_call(spot, hidden_two, fc1_b, fc1_w)

    shard_steps = [(shard, bit) for bit in reversed(shard.bits[1:])]
    low_bits = [(rep, bit) for bit in rep.bits[:1]]
    high_bits = [(rep, bit) for bit in rep.bits[1:]]
    keep, send = wide_grad(spot, act_low, low_two, shard.size, "fc2_grad")
    fc2_w = fc2_gather.pieces(send)
    fc2_sum = two_way((keep, after(send, fc2_gather.held[-1][0])), shard, rep)
    block_out, gate_sums = out_call(spot,
        counts, launched(act_low, fc2_sum), tokens, branch_one, cot, modulation, fc2_b, fc2_w, slots
    )
    block_out, gate_sums = together(spot, [fc2_sum], block_out, gate_sums)
    low_pre, grad_fc1_b, grad_mid, low_one, sums = mlp_bwd_call(spot,
        launched(low_two, fc2_sum), derivative, tokens, branch_one, cot, modulation, fc1_w, fc2_w, slots
    )
    low_pre = together(spot, [fc2_sum], low_pre)
    keep, send = wide_grad(spot, hidden_two, launched(low_pre, fc2_sum), shard.size, "fc1_grad")
    keep, send, low_one = together(spot, [fc2_sum], keep, send, low_one)
    fc1_sum = two_way((keep, send), shard, rep)
    grad_mixed = mixed_bwd_call(spot, launched(low_one, fc1_sum, fc2_sum), proj_w)
    grad_mixed = together(spot, [fc1_sum, fc2_sum], grad_mixed)
    grad_qkv, qv_sums = attn_bwd_call(qkv, launched(grad_mixed, fc1_sum, fc2_sum), slots)
    grad_qkv, qv_sums = together(spot, [fc1_sum, fc2_sum], grad_qkv, qv_sums)
    first, second = attn_grad(
        spot,
        hidden_one,
        launched(grad_qkv, fc1_sum, fc2_sum),
        mixed,
        low_one,
        qv_sums,
        sums,
        grad_fc1_b,
        shard.size,
    )
    first, second, grad_qkv = together(spot, [fc1_sum, fc2_sum], first, second, grad_qkv)
    first_sum = one_way(first, shard, shard_steps + high_bits[:-1] + low_bits + high_bits[-1:])
    second_sum = one_way(second, shard, low_bits + shard_steps + high_bits)
    grad_tokens, slot_values = input_bwd_call(spot,
        launched(grad_qkv, first_sum, second_sum, fc1_sum, fc2_sum),
        tokens,
        grad_mid,
        modulation,
        sums,
        gate_sums,
        condition,
        qkv_w,
        slots,
    )
    sums_list = [first_sum, second_sum, fc1_sum, fc2_sum]
    grad_tokens, slot_values = together(spot, sums_list, grad_tokens, slot_values)

    def append(mine, other):
        return jnp.concatenate([mine, other], 0)

    every = [(rep, bit, append) for bit in reversed(rep.bits)]
    every += [(shard, bit, append) for bit in reversed(shard.bits)]
    all_slots = Chain(slot_values, every)

    def to_silu(mine, other):
        return dot_nt(append(mine, other), ada_weight)

    there = [(shard, bit, append) for bit in shard.bits[:-1]]
    there += [(shard, shard.bits[-1], to_silu)]
    there += [(shard, bit, append) for bit in shard.bits]
    to_cond = Chain(slot_values[:, : 6 * width], there)

    chains = [first_sum, second_sum, fc1_sum, fc2_sum, all_slots, to_cond]
    active = [chain for chain in chains if chain.running()]
    while active:
        together(spot, active)
        active = [chain for chain in chains if chain.running()]

    grad_cond = cond_call(spot, to_cond.value, condition, shard.size)

    mod_all = all_slots.value[:, : 6 * width]
    silu_cols = lax.dynamic_slice_in_dim(all_slots.value, 6 * width + shard.index * depth, depth, 1)
    grad_ada_w = dot_tn(silu_cols, mod_all)
    ada_b_all = jnp.sum(mod_all.astype(F32), axis=0)
    grad_ada_b = lax.dynamic_slice_in_dim(
        ada_b_all, shard.index * ada_bias.shape[0], ada_bias.shape[0], 0
    )

    grad_fc2_w = place_rows(spot, fc2_sum.finish(), fc2_weight.shape[0])
    grad_fc1_w = place_rows(spot, fc1_sum.finish(), fc1_weight.shape[0])
    bias_sizes = tuple(bias.shape[0] for bias in bias_list)
    grad_qkv_w, grad_proj_w, *bias_out = place_attn(
        spot, first_sum.finish(), second_sum.finish(), depth, width, bias_sizes
    )
    bias_out = [value.reshape(-1) for value in bias_out]

    return (
        block_out,
        grad_tokens,
        grad_cond,
        grad_ada_w,
        grad_ada_b,
        grad_qkv_w,
        bias_out[0],
        grad_proj_w,
        bias_out[1],
        grad_fc1_w,
        bias_out[2],
        grad_fc2_w,
        bias_out[3],
    )


def solution(mesh):
    rows = P(("rep", "shard"), None)
    weights = (P("shard", None), P("shard"))
    return jax.shard_map(
        functools.partial(per_device, mesh.shape["shard"], mesh.shape["rep"]),
        mesh=mesh,
        in_specs=(rows, rows, P(("rep", "shard")), rows) + weights * 5,
        out_specs=(rows, rows, rows) + weights * 5,
        check_vma=False,
    )
```

```python
import functools

import jax
import jax.numpy as jnp
from jax import lax
from jax.experimental import pallas as pl
from jax.experimental.pallas import tpu as pltpu
from jax.sharding import PartitionSpec as P

HEADS = 12
HEAD_DIM = 64
EPS = 1e-06
GELU_C = 0.7978845608028654
GELU_A = 0.044715
F32 = jnp.float32
BF16 = jnp.bfloat16
VMEM_LIMIT = 56 * 1024 * 1024


def norm_back(grad_hat, normed, inv_std):
    return inv_std * (
        grad_hat
        - jnp.mean(grad_hat, axis=-1, keepdims=True)
        - normed * jnp.mean(grad_hat * normed, axis=-1, keepdims=True)
    )


def gelu_pair(pre_act):
    square = pre_act * pre_act
    tanh_val = jnp.tanh(pre_act * (GELU_C + GELU_C * GELU_A * square))
    half = 0.5 + 0.5 * tanh_val
    activated = pre_act * half
    derivative = half + activated * (1.0 - tanh_val) * (GELU_C + 3.0 * GELU_C * GELU_A * square)
    return (activated, derivative)


def dot_nn(left, right):
    return lax.dot_general(left, right, (((1,), (0,)), ((), ())), preferred_element_type=F32)


def dot_nt(left, right):
    return lax.dot_general(left, right, (((1,), (1,)), ((), ())), preferred_element_type=F32)


def dot_tn(left, right):
    return lax.dot_general(left, right, (((0,), (0,)), ((), ())), preferred_element_type=F32)


def specs(count, space=pltpu.VMEM):
    return [pl.BlockSpec(memory_space=space)] * count


def shape(dims, dtype):
    return jax.ShapeDtypeStruct(dims, dtype)


COST_SHARE = 0.0


def params(flops=0, bytes_moved=0, exps=0):
    return dict(
        compiler_params=pltpu.CompilerParams(vmem_limit_bytes=VMEM_LIMIT),
        cost_estimate=pl.CostEstimate(
            flops=int(COST_SHARE * flops),
            bytes_accessed=int(COST_SHARE * bytes_moved),
            transcendentals=int(COST_SHARE * exps),
        ),
    )


def high_bit(spot_ref, number, bit):
    return lax.rem(lax.div(spot_ref[number], jnp.int32(bit)), jnp.int32(2))


def piece_copies(refs, offsets, spot_ref, whole, sems):
    copies = []
    for k, (ref, (offset, part, rows)) in enumerate(zip(refs, offsets)):
        first = (spot_ref[0] ^ offset) * rows
        if part is not None:
            half = high_bit(spot_ref, 1, 1)
            first = first + (half if part == "near" else 1 - half) * (rows // 2)
        place = whole.at[pl.ds(pl.multiple_of(first, 16), ref.shape[0]), :]
        copies.append(pltpu.make_async_copy(ref, place, sems.at[k]))
    return copies


def row_norm(value):
    center = value - jnp.mean(value, axis=-1, keepdims=True)
    inv_std = lax.rsqrt(jnp.mean(center * center, axis=-1, keepdims=True) + EPS)
    return center * inv_std, inv_std


def mod_part(mod_ref, slot, part, width):
    return mod_ref[slot : slot + 1, part * width : (part + 1) * width]


def qkv_kernel(offsets, slots, *refs):
    count = len(offsets)
    spot_ref, tok_ref, mod_ref, bias_ref = refs[:4]
    pieces = refs[4 : 4 + count]
    hidden_ref, qkv_ref, whole, sems = refs[4 + count :]
    copies = piece_copies(pieces, offsets, spot_ref, whole, sems)
    for copy in copies:
        copy.start()
    rows, width = tok_ref.shape
    seq = rows // slots
    for slot in range(slots):
        at = pl.ds(slot * seq, seq)
        normed, _ = row_norm(tok_ref[at, :].astype(F32))
        scale = 1.0 + mod_part(mod_ref, slot, 1, width)
        hidden_ref[at, :] = (normed * scale + mod_part(mod_ref, slot, 0, width)).astype(BF16)
    for copy in copies:
        copy.wait()
    for part in range(3):
        cols = pl.ds(part * width, width)
        qkv_ref[:, cols] = (
            dot_nn(hidden_ref[...], whole[:, cols]) + bias_ref[:, cols]
        ).astype(BF16)


def qkv_call(spot, tokens, modulation, bias, weight, slots):
    rows, width = tokens.shape
    pieces, offsets = weight
    return pl.pallas_call(
        functools.partial(qkv_kernel, offsets, slots),
        in_specs=specs(1, pltpu.SMEM) + specs(3) + specs(len(pieces), pl.ANY),
        out_specs=specs(2),
        out_shape=[shape((rows, width), BF16), shape((rows, 3 * width), BF16)],
        scratch_shapes=[
            pltpu.VMEM((width, 3 * width), BF16),
            pltpu.SemaphoreType.DMA((len(pieces),)),
        ],
        name="qkv_fwd",
        **params(6 * rows * width * width, 10 * rows * width + 6 * width * width),
    )(spot, tokens, modulation, bias, *pieces)


def pair_masks(rows):
    lane = lax.broadcasted_iota(jnp.int32, (rows, 2 * HEAD_DIM), 1)
    return lane < HEAD_DIM


def attn_kernel(offsets, *refs):
    count = len(offsets)
    spot_ref, qkv_ref, tok_ref, cot_ref, mod_ref, bias_ref = refs[:6]
    pieces = refs[6 : 6 + count]
    mixed_ref, branch_ref, hidden_ref, low_ref, whole, sems = refs[6 + count :]
    rows, width = tok_ref.shape
    copies = piece_copies(pieces, offsets, spot_ref, whole, sems)

    @pl.when(pl.program_id(0) == 0)
    def _():
        for copy in copies:
            copy.start()

    first = pair_masks(rows)
    for pair in range(HEADS // 2):
        cols = pl.ds(pair * 128, 128)
        query_pair = qkv_ref[:, cols]
        key_pair = qkv_ref[:, pl.ds(width + pair * 128, 128)]
        value_pair = qkv_ref[:, pl.ds(2 * width + pair * 128, 128)]
        parts = []
        none = jnp.zeros_like(query_pair)
        for head in range(2):
            keep = first if head == 0 else jnp.logical_not(first)
            scores = dot_nt(key_pair, jnp.where(keep, query_pair, none)) * HEAD_DIM ** (-0.5)
            exped = jnp.exp(scores - jnp.max(scores, axis=0, keepdims=True))
            probs = exped * (1.0 / jnp.sum(exped, axis=0, keepdims=True))
            parts.append(dot_tn(probs.astype(BF16), value_pair))
        mixed_ref[:, cols] = jnp.where(first, parts[0], parts[1]).astype(BF16)

    @pl.when(pl.program_id(0) == 0)
    def _():
        for copy in copies:
            copy.wait()

    mod = mod_ref[0]
    branch = dot_nn(mixed_ref[...], whole[...]) + bias_ref[...]
    branch_ref[...] = branch
    normed, _ = row_norm(tok_ref[...].astype(F32) + mod_part(mod, 0, 2, width) * branch)
    scale = 1.0 + mod_part(mod, 0, 4, width)
    hidden_ref[...] = (normed * scale + mod_part(mod, 0, 3, width)).astype(BF16)
    low_ref[...] = (mod_part(mod, 0, 5, width) * cot_ref[...].astype(F32)).astype(BF16)


def attn_call(spot, qkv, tokens, cot, modulation, bias, weight, slots):
    rows, width = tokens.shape
    seq = rows // slots
    pieces, offsets = weight
    by_slot = pl.BlockSpec((seq, width), lambda s: (s, 0))
    return pl.pallas_call(
        functools.partial(attn_kernel, offsets),
        grid=(slots,),
        in_specs=specs(1, pltpu.SMEM)
        + [
            pl.BlockSpec((seq, 3 * width), lambda s: (s, 0)),
            by_slot,
            by_slot,
            pl.BlockSpec((1, 1, 6 * width), lambda s: (s, 0, 0)),
            pl.BlockSpec((1, width), lambda s: (0, 0)),
        ]
        + specs(len(pieces), pl.ANY),
        out_specs=[by_slot] * 4,
        out_shape=[
            shape((rows, width), BF16),
            shape((rows, width), F32),
            shape((rows, width), BF16),
            shape((rows, width), BF16),
        ],
        scratch_shapes=[
            pltpu.VMEM((width, width), BF16),
            pltpu.SemaphoreType.DMA((len(pieces),)),
        ],
        name="attn_fwd",
        **params(
            2 * rows * width * width + 4 * rows * width * seq * 4,
            24 * rows * width,
            rows * seq * HEADS,
        ),
    )(spot, qkv, tokens, cot, modulation[:, None, :], bias, *pieces)


FF_BLOCK = 768


def gelu_kernel(offsets, *refs):
    count = len(offsets)
    spot_ref, hidden_ref, bias_ref = refs[:3]
    pieces = refs[3 : 3 + count]
    act_ref, deriv_ref, whole, sems = refs[3 + count :]
    step = pl.program_id(0)

    @pl.when(step == 0)
    def _():
        copies = piece_copies(pieces, offsets, spot_ref, whole, sems)
        for copy in copies:
            copy.start()
        for copy in copies:
            copy.wait()

    cols = pl.ds(pl.multiple_of(step * FF_BLOCK, FF_BLOCK), FF_BLOCK)
    pre_act = dot_nn(hidden_ref[...], whole[:, cols]) + bias_ref[...]
    activated, derivative = gelu_pair(pre_act)
    act_ref[...] = activated.astype(BF16)
    deriv_ref[...] = derivative


def gelu_call(spot, hidden, bias, weight):
    rows, width = hidden.shape
    pieces, offsets = weight
    hidden_units = bias.shape[1]
    block = pl.BlockSpec((rows, FF_BLOCK), lambda j: (0, j))
    return pl.pallas_call(
        functools.partial(gelu_kernel, offsets),
        grid=(hidden_units // FF_BLOCK,),
        in_specs=specs(1, pltpu.SMEM)
        + [
            pl.BlockSpec((rows, width), lambda j: (0, 0)),
            pl.BlockSpec((1, FF_BLOCK), lambda j: (0, j)),
        ]
        + specs(len(pieces), pl.ANY),
        out_specs=[block, block],
        out_shape=[shape((rows, hidden_units), BF16), shape((rows, hidden_units), F32)],
        scratch_shapes=[
            pltpu.VMEM((width, hidden_units), BF16),
            pltpu.SemaphoreType.DMA((len(pieces),)),
        ],
        name="fc1_gelu",
        **params(
            2 * rows * width * hidden_units, 8 * rows * hidden_units, rows * hidden_units
        ),
    )(spot, hidden, bias, *pieces)


def out_kernel(offsets, slots, *refs):
    count = len(offsets)
    spot_ref, live_ref, act_ref, tok_ref, branch_ref, cot_ref, mod_ref, bias_ref = refs[:8]
    pieces = refs[8 : 8 + count]
    block_ref, gate_ref, whole, sems = refs[8 + count :]
    copies = piece_copies(pieces, offsets, spot_ref, whole, sems)
    for copy in copies:
        copy.start()
    for copy in copies:
        copy.wait()
    rows, width = tok_ref.shape
    seq = rows // slots
    for slot in range(slots):
        at = pl.ds(slot * seq, seq)
        branch_two = dot_nn(act_ref[at, :], whole[...]) + bias_ref[...]
        gate_ref[slot : slot + 1, :] = jnp.sum(
            cot_ref[at, :].astype(F32) * branch_two, axis=0, keepdims=True
        )
        mid = tok_ref[at, :].astype(F32) + mod_part(mod_ref, slot, 2, width) * branch_ref[at, :]
        block = mid + mod_part(mod_ref, slot, 5, width) * branch_two
        block_ref[at, :] = jnp.where(live_ref[0] > slot, block, 0.0).astype(BF16)


def out_call(spot, counts, act_low, tokens, branch_one, cot, modulation, bias, weight, slots):
    rows, width = tokens.shape
    hidden_units = act_low.shape[1]
    pieces, offsets = weight
    return pl.pallas_call(
        functools.partial(out_kernel, offsets, slots),
        in_specs=specs(2, pltpu.SMEM) + specs(6) + specs(len(pieces), pl.ANY),
        out_specs=specs(2),
        out_shape=[shape((rows, width), BF16), shape((slots, width), F32)],
        scratch_shapes=[
            pltpu.VMEM((hidden_units, width), BF16),
            pltpu.SemaphoreType.DMA((len(pieces),)),
        ],
        name="fc2_fwd",
        **params(2 * rows * width * hidden_units, 2 * (rows + width) * hidden_units),
    )(spot, counts, act_low, tokens, branch_one, cot, modulation, bias, *pieces)


def mlp_bwd_kernel(one_offsets, two_offsets, slots, *refs):
    count, both = len(one_offsets), len(one_offsets) + len(two_offsets)
    spot_ref, low_ref, deriv_ref, tok_ref, branch_ref, cot_ref, mod_ref = refs[:7]
    one_pieces = refs[7 : 7 + count]
    two_pieces = refs[7 + count : 7 + both]
    (low_pre_ref, fc1_b_ref, mid_ref, low_one_ref, sums_ref, one, two, acc, sems_one, sems_two) = refs[
        7 + both :
    ]
    step = pl.program_id(0)
    copies_two = piece_copies(two_pieces, two_offsets, spot_ref, two, sems_two)
    copies_one = piece_copies(one_pieces, one_offsets, spot_ref, one, sems_one)

    @pl.when(step == 0)
    def _():
        for copy in copies_two + copies_one:
            copy.start()
        acc[...] = jnp.zeros_like(acc)
        for copy in copies_two:
            copy.wait()

    ff = pl.ds(pl.multiple_of(step * FF_BLOCK, FF_BLOCK), FF_BLOCK)
    grad_pre = dot_nt(low_ref[...], two[ff, :]) * deriv_ref[...]
    fc1_b_ref[...] = jnp.sum(grad_pre, axis=0, keepdims=True)
    low_pre = grad_pre.astype(BF16)
    low_pre_ref[...] = low_pre

    @pl.when(step == 0)
    def _():
        for copy in copies_one:
            copy.wait()

    acc[...] += dot_nt(low_pre, one[:, ff])

    @pl.when(step == pl.num_programs(0) - 1)
    def _():
        rows, width = tok_ref.shape
        seq = rows // slots
        for slot in range(slots):
            at = pl.ds(slot * seq, seq)
            branch = branch_ref[at, :]
            cot = cot_ref[at, :].astype(F32)
            gate_one = mod_part(mod_ref, slot, 2, width)
            normed, inv_std = row_norm(tok_ref[at, :].astype(F32) + gate_one * branch)
            grad_hidden = acc[at, :]
            scale = 1.0 + mod_part(mod_ref, slot, 4, width)
            grad_mid = cot + norm_back(grad_hidden * scale, normed, inv_std)
            mid_ref[at, :] = grad_mid
            grad_branch = gate_one * grad_mid
            low_one_ref[at, :] = grad_branch.astype(BF16)

            def put(part, value):
                sums_ref[part, slot : slot + 1, :] = jnp.sum(value, axis=0, keepdims=True)

            put(0, grad_mid * branch)
            put(1, grad_hidden)
            put(2, grad_hidden * normed)
            put(3, grad_branch)
            put(4, mod_part(mod_ref, slot, 5, width) * cot)


def mlp_bwd_call(spot, low_two, derivative, tokens, branch_one, cot, modulation, one, two, slots):
    rows, width = tokens.shape
    hidden_units = derivative.shape[1]
    block = pl.BlockSpec((rows, FF_BLOCK), lambda j: (0, j))
    whole = pl.BlockSpec((rows, width), lambda j: (0, 0))
    return pl.pallas_call(
        functools.partial(mlp_bwd_kernel, one[1], two[1], slots),
        grid=(hidden_units // FF_BLOCK,),
        in_specs=specs(1, pltpu.SMEM)
        + [whole, block, whole, whole, whole, pl.BlockSpec((slots, 6 * width), lambda j: (0, 0))]
        + specs(len(one[0]) + len(two[0]), pl.ANY),
        out_specs=[
            block,
            pl.BlockSpec((1, FF_BLOCK), lambda j: (0, j)),
            whole,
            whole,
            pl.BlockSpec((5, slots, width), lambda j: (0, 0, 0)),
        ],
        out_shape=[
            shape((rows, hidden_units), BF16),
            shape((1, hidden_units), F32),
            shape((rows, width), F32),
            shape((rows, width), BF16),
            shape((5, slots, width), F32),
        ],
        scratch_shapes=[
            pltpu.VMEM((width, hidden_units), BF16),
            pltpu.VMEM((hidden_units, width), BF16),
            pltpu.VMEM((rows, width), F32),
            pltpu.SemaphoreType.DMA((len(one[0]),)),
            pltpu.SemaphoreType.DMA((len(two[0]),)),
        ],
        name="mlp_bwd",
        **params(4 * rows * width * hidden_units, 6 * rows * hidden_units + 4 * width * hidden_units),
    )(spot, low_two, derivative, tokens, branch_one, cot, modulation, *one[0], *two[0])


def attn_bwd_kernel(qkv_ref, grad_ref, out_ref, bias_ref):
    rows = qkv_ref.shape[0]
    width = grad_ref.shape[1]
    first = pair_masks(rows)
    for pair in range(HEADS // 2):
        query_cols = pl.ds(pair * 128, 128)
        key_cols = pl.ds(width + pair * 128, 128)
        value_cols = pl.ds(2 * width + pair * 128, 128)
        query_pair = qkv_ref[:, query_cols]
        key_pair = qkv_ref[:, key_cols]
        value_pair = qkv_ref[:, value_cols]
        grad_pair = grad_ref[:, query_cols]
        grads = []
        for head in range(2):
            keep = first if head == 0 else jnp.logical_not(first)
            none = jnp.zeros_like(query_pair)
            scores = dot_nt(key_pair, jnp.where(keep, query_pair, none)) * HEAD_DIM ** (-0.5)
            exped = jnp.exp(scores - jnp.max(scores, axis=0, keepdims=True))
            probs = exped * (1.0 / jnp.sum(exped, axis=0, keepdims=True))
            grad_probs = dot_nt(value_pair, jnp.where(keep, grad_pair, none))
            dots = jnp.sum(probs * grad_probs, axis=0, keepdims=True)
            grad_scores = (probs * (grad_probs - dots) * HEAD_DIM ** (-0.5)).astype(BF16)
            grads.append(
                (
                    dot_tn(grad_scores, key_pair),
                    dot_nn(grad_scores, query_pair),
                    dot_nn(probs.astype(BF16), grad_pair),
                )
            )
        grad_query, grad_key, grad_value = (
            jnp.where(first, left, right) for left, right in zip(grads[0], grads[1])
        )
        out_ref[:, query_cols] = grad_query.astype(BF16)
        out_ref[:, key_cols] = grad_key.astype(BF16)
        out_ref[:, value_cols] = grad_value.astype(BF16)
        bias_ref[0, :, query_cols] = jnp.sum(grad_query, axis=0, keepdims=True)
        bias_ref[0, :, key_cols] = jnp.sum(grad_value, axis=0, keepdims=True)


def attn_bwd_call(qkv, grad_mixed, slots):
    rows, width = grad_mixed.shape
    seq = rows // slots
    return pl.pallas_call(
        attn_bwd_kernel,
        grid=(slots,),
        in_specs=[
            pl.BlockSpec((seq, 3 * width), lambda s: (s, 0)),
            pl.BlockSpec((seq, width), lambda s: (s, 0)),
        ],
        out_specs=[
            pl.BlockSpec((seq, 3 * width), lambda s: (s, 0)),
            pl.BlockSpec((1, 1, 2 * width), lambda s: (s, 0, 0)),
        ],
        out_shape=[
            shape((rows, 3 * width), BF16),
            shape((slots, 1, 2 * width), F32),
        ],
        name="attn_bwd",
        **params(20 * rows * width * seq, 16 * rows * width, rows * seq * HEADS),
    )(qkv, grad_mixed)


def mixed_bwd_kernel(offsets, *refs):
    count = len(offsets)
    spot_ref, low_ref = refs[:2]
    pieces = refs[2 : 2 + count]
    out_ref, whole, sems = refs[2 + count :]
    copies = piece_copies(pieces, offsets, spot_ref, whole, sems)
    for copy in copies:
        copy.start()
    for copy in copies:
        copy.wait()
    out_ref[...] = dot_nt(low_ref[...], whole[...]).astype(BF16)


def mixed_bwd_call(spot, low_one, weight):
    rows, width = low_one.shape
    pieces, offsets = weight
    return pl.pallas_call(
        functools.partial(mixed_bwd_kernel, offsets),
        in_specs=specs(1, pltpu.SMEM) + specs(1) + specs(len(pieces), pl.ANY),
        out_specs=pl.BlockSpec(memory_space=pltpu.VMEM),
        out_shape=shape((rows, width), BF16),
        scratch_shapes=[
            pltpu.VMEM((width, width), BF16),
            pltpu.SemaphoreType.DMA((len(pieces),)),
        ],
        name="proj_bwd",
        **params(2 * rows * width * width, 4 * rows * width + 2 * width * width),
    )(spot, low_one, *pieces)


def input_bwd_kernel(offsets, slots, *refs):
    count = len(offsets)
    spot_ref, grad_ref, tok_ref, mid_ref, mod_ref, sums_ref, gate_ref, cond_ref = refs[:8]
    pieces = refs[8 : 8 + count]
    out_ref, mod_out, whole, sems = refs[8 + count :]
    copies = piece_copies(pieces, offsets, spot_ref, whole, sems)
    for copy in copies:
        copy.start()
    for copy in copies:
        copy.wait()
    rows, width = tok_ref.shape
    seq = rows // slots

    def put(slot, part, value):
        mod_out[slot : slot + 1, part * width : (part + 1) * width] = value.astype(BF16)

    for slot in range(slots):
        at = pl.ds(slot * seq, seq)
        row = slice(slot, slot + 1)
        grad_hidden = dot_nt(grad_ref[at, :], whole[...])
        normed, inv_std = row_norm(tok_ref[at, :].astype(F32))
        scale = 1.0 + mod_part(mod_ref, slot, 1, width)
        out_ref[at, :] = mid_ref[at, :] + norm_back(grad_hidden * scale, normed, inv_std)
        put(slot, 0, jnp.sum(grad_hidden, axis=0, keepdims=True))
        put(slot, 1, jnp.sum(grad_hidden * normed, axis=0, keepdims=True))
        for part in range(3):
            put(slot, 2 + part, sums_ref[part, row, :])
        put(slot, 5, gate_ref[row, :])
        cond = cond_ref[row, :].astype(F32)
        put(slot, 6, cond * (1.0 / (1.0 + jnp.exp(-cond))))


def input_bwd_call(spot, grad_qkv, tokens, grad_mid, modulation, sums, gate_sums, condition, weight, slots):
    rows, width = tokens.shape
    pieces, offsets = weight
    return pl.pallas_call(
        functools.partial(input_bwd_kernel, offsets, slots),
        in_specs=specs(1, pltpu.SMEM) + specs(7) + specs(len(pieces), pl.ANY),
        out_specs=specs(2),
        out_shape=[shape((rows, width), F32), shape((slots, 7 * width), BF16)],
        scratch_shapes=[
            pltpu.VMEM((width, 3 * width), BF16),
            pltpu.SemaphoreType.DMA((len(pieces),)),
        ],
        name="qkv_bwd",
        **params(6 * rows * width * width, 16 * rows * width + 6 * width * width),
    )(spot, grad_qkv, tokens, grad_mid, modulation, sums, gate_sums, condition, *pieces)


def split_store(core, total, depth, keep_ref, send_ref, cols):
    for far in range(total.shape[0] // (2 * depth)):
        even = total[2 * far * depth : (2 * far + 1) * depth]
        odd = total[(2 * far + 1) * depth : (2 * far + 2) * depth]
        keep_ref[far, :, cols] = jnp.where(core == 0, even, odd)
        send_ref[far, :, cols] = jnp.where(core == 0, odd, even).astype(BF16)


def wide_grad_kernel(spot_ref, left_ref, right_ref, keep_ref, send_ref):
    total = dot_tn(left_ref[...], right_ref[...])
    split_store(spot_ref[0] & 1, total, keep_ref.shape[1], keep_ref, send_ref, slice(None))


def wide_grad(spot, left, right, shards, name):
    rows, in_dim = left.shape
    out_dim = right.shape[1]
    depth = in_dim // shards
    block = out_dim // 2 if out_dim > 1024 else out_dim
    per_step = shards // 2 if in_dim <= 768 else 1
    out_block = pl.BlockSpec((per_step, depth, block), lambda i, j: (i, 0, j))
    dims = (shards // 2, depth, out_dim)
    return pl.pallas_call(
        wide_grad_kernel,
        grid=(shards // 2 // per_step, out_dim // block),
        in_specs=specs(1, pltpu.SMEM)
        + [
            pl.BlockSpec((rows, 2 * depth * per_step), lambda i, j: (0, i)),
            pl.BlockSpec((rows, block), lambda i, j: (0, j)),
        ],
        out_specs=[out_block, out_block],
        out_shape=[shape(dims, F32), shape(dims, BF16)],
        name=name,
        **params(2 * rows * in_dim * out_dim, 3 * in_dim * out_dim + 2 * rows * (in_dim + out_dim)),
    )(spot, left, right)


EXTRA = 256


def bias_rows(count):
    return [(start, min(EXTRA, count - start)) for start in range(0, count, EXTRA)]


def attn_grad_kernel(shards, *refs):
    spot_ref, hidden_ref, qkv_ref, mixed_ref, low_ref, qv_ref, sums_ref, fc1_ref = refs[:8]
    keep_a, send_a, keep_b, send_b, extra = refs[8:]
    depth = keep_a.shape[1]
    width = hidden_ref.shape[1]
    core = spot_ref[0] & 1
    total = dot_tn(hidden_ref[...], qkv_ref[...])
    split_store(core, total[:, : 2 * width], depth, keep_a, send_a, slice(None))
    split_store(core, total[:, 2 * width :], depth, keep_b, send_b, pl.ds(0, width))
    total = dot_tn(mixed_ref[...], low_ref[...])
    split_store(core, total, depth, keep_b, send_b, pl.ds(width, width))
    extra[...] = jnp.zeros_like(extra)
    biases = (
        jnp.sum(qv_ref[...], axis=0),
        jnp.sum(sums_ref[3], axis=0, keepdims=True),
        fc1_ref[...],
        jnp.sum(sums_ref[4], axis=0, keepdims=True),
    )
    for place in range(shards):
        row = place * depth
        for bias in biases:
            count = bias.shape[1] // shards
            for start, size in bias_rows(count):
                first = place * count + start
                extra[row : row + 1, :size] = bias[:, first : first + size]
                row += 1
    split_store(core, extra[...], depth, keep_b, send_b, pl.ds(2 * width, EXTRA))


def attn_grad(spot, hidden, grad_qkv, mixed, low_one, qv_sums, sums, fc1_sums, shards):
    rows, width = hidden.shape
    first = (shards // 2, width // shards, 2 * width)
    second = (shards // 2, width // shards, 2 * width + EXTRA)
    outs = pl.pallas_call(
        functools.partial(attn_grad_kernel, shards),
        in_specs=specs(1, pltpu.SMEM) + specs(7),
        out_specs=specs(4),
        out_shape=[shape(first, F32), shape(first, BF16), shape(second, F32), shape(second, BF16)],
        scratch_shapes=[pltpu.VMEM((width, EXTRA), F32)],
        name="attn_weight_grads",
        **params(8 * rows * width * width, 12 * width * width + 14 * rows * width),
    )(spot, hidden, grad_qkv, mixed, low_one, qv_sums, sums, fc1_sums)
    return outs[:2], outs[2:]


def round_kernel(kinds, spot_ref, *refs):
    ins = list(refs[: sum(kind[1] for kind in kinds)])
    outs = list(refs[len(ins) :])
    for kind, count in kinds:
        args, ins = ins[:count], ins[count:]
        if kind == "halve":
            keep_out, send_out, outs = outs[0], outs[1], outs[2:]
            keep_out[...] = args[0][...] + args[2][...].astype(F32)
            send_out[...] = (args[1][...] + args[3][...].astype(F32)).astype(BF16)
        elif kind == "merge":
            keep_out, send_out, outs = outs[0], outs[1], outs[2:]
            half = keep_out.shape[2] // 2
            for part in range(2):
                mine, other, sent_mine, sent_other = args[4 * part : 4 * part + 4]
                cols = slice(part * half, (part + 1) * half)
                keep_out[:, :, cols] = mine[...] + sent_mine[...].astype(F32)
                send_out[:, :, cols] = (other[...] + sent_other[...].astype(F32)).astype(BF16)
        elif kind == "add":
            out, outs = outs[0], outs[1:]
            out[...] = (args[0][...].astype(F32) + args[1][...].astype(F32)).astype(BF16)
        else:
            out, outs = outs[0], outs[1:]
            rows = args[0].shape[1]
            out[:, :rows, :] = args[0][...]
            out[:, rows:, :] = args[1][...]


def round_call(spot, jobs):
    split = 2
    for job in jobs:
        cols = job["args"][0].shape[2] // (1 if job.get("part") is None else 2)
        if job["kind"] == "merge" or cols % 256:
            split = 1
    in_specs, args, out_specs, out_shape = [], [], [], []

    def halves_of(value, axis, bit, dim, base, dims, chunk):
        def spec(other):
            def place(j, spot_ref):
                half = high_bit(spot_ref, axis.number, bit)
                half = 1 - half if other else half
                return (half, 0, base + j) if dim == 0 else (0, half, base + j)

            return pl.BlockSpec((dims[0], dims[1], chunk), place)

        in_specs.extend([spec(False), spec(True)])
        args.extend([value, value])

    def plain(dims):
        return pl.BlockSpec((dims[0], dims[1], dims[2] // split), lambda j, spot_ref: (0, 0, j))

    kinds = []
    for job in jobs:
        values = job["args"]
        kind = job["kind"]
        dims = list(values[0].shape)
        before = len(args)
        if kind in ("halve", "merge"):
            axis, bit, dim = job["step"]
            dims[dim] //= 2
            part = job.get("part")
            if part is not None:
                dims[2] //= 2
            chunk = dims[2] // split
            base = 0 if part is None else part * split
            for value in values:
                halves_of(value, axis, bit, dim, base, dims, chunk)
            if kind == "merge":
                dims[2] *= 2
            out_specs += [plain(dims)] * 2
            out_shape += [shape(tuple(dims), F32), shape(tuple(dims), BF16)]
        else:
            in_specs += [plain(value.shape) for value in values]
            args += values
            if kind == "cat":
                dims[1] += values[1].shape[1]
            out_specs.append(plain(dims))
            out_shape.append(shape(tuple(dims), BF16))
        kinds.append((kind, len(args) - before))
    outs = pl.pallas_call(
        functools.partial(round_kernel, kinds),
        grid_spec=pltpu.PrefetchScalarGridSpec(
            num_scalar_prefetch=1, grid=(split,), in_specs=in_specs, out_specs=out_specs
        ),
        out_shape=out_shape,
        name="sum_round",
        **params(0, 0),
    )(spot, *args)
    outs = list(outs)
    results = []
    for kind, _ in kinds:
        count = 2 if kind in ("halve", "merge") else 1
        results.append(outs[:count])
        outs = outs[count:]
    return results


def first_row(spot_ref, terms, flips):
    row = 0
    for (number, bit, size), flip in zip(terms, flips):
        half = high_bit(spot_ref, number, bit)
        row = row + (1 - half if flip else half) * size
    return row


def row_places(spot_ref, refs, terms, flips, count):
    parts = []
    for ref in refs:
        parts += [(ref, slice(k * count, (k + 1) * count)) for k in range(ref.shape[1] // count)]
    for (ref, rows), flip in zip(parts, flips):
        at = first_row(spot_ref, terms, flip)
        if not isinstance(at, int):
            at = pl.multiple_of(at, 16)
        yield ref, rows, pl.ds(at, count)


def place_kernel(terms, flips, count, spot_ref, *refs):
    out_ref = refs[-1]
    for ref, rows, at in row_places(spot_ref, refs[:-1], terms, flips, count):
        out_ref[at, :] = ref[0, rows, :].astype(F32)


def place_rows(spot, done, rows):
    pieces, terms, flips, count = done
    cols = pieces[0].shape[2]
    return pl.pallas_call(
        functools.partial(place_kernel, terms, flips, count),
        in_specs=specs(1, pltpu.SMEM) + specs(len(pieces)),
        out_specs=pl.BlockSpec(memory_space=pltpu.VMEM),
        out_shape=shape((rows, cols), F32),
        name="place_rows",
        **params(0, rows * cols * 6),
    )(spot, *pieces)


def place_attn_kernel(plans, parts, biases, spot_ref, *refs):
    qkv_out, proj_out, *bias_outs, head = refs[2 * parts :]
    width = proj_out.shape[1]
    for ref, rows, at in row_places(spot_ref, refs[:parts], *plans[0]):
        qkv_out[at, : 2 * width] = ref[0, rows, :].astype(F32)
    for ref, rows, at in row_places(spot_ref, refs[parts : 2 * parts], *plans[1]):
        qkv_out[at, 2 * width :] = ref[0, rows, :width].astype(F32)
        proj_out[at, :] = ref[0, rows, width : 2 * width].astype(F32)
        head[at, :] = ref[0, rows, 2 * width :].astype(F32)
    row = 0
    for count, out in zip(biases, bias_outs):
        for start, size in bias_rows(count):
            out[:, start : start + size] = head[row : row + 1, :size]
            row += 1


def place_attn(spot, first, second, rows, width, biases):
    parts = len(first[0])
    return pl.pallas_call(
        functools.partial(place_attn_kernel, (first[1:], second[1:]), parts, biases),
        in_specs=specs(1, pltpu.SMEM) + specs(2 * parts),
        out_specs=specs(2 + len(biases)),
        out_shape=[shape((rows, 3 * width), F32), shape((rows, width), F32)]
        + [shape((1, count), F32) for count in biases],
        scratch_shapes=[pltpu.VMEM((rows, EXTRA), F32)],
        name="place_attn",
        **params(0, rows * width * 24),
    )(spot, *first[0], *second[0])


def cond_kernel(shards, spot_ref, grad_ref, cond_ref, out_ref):
    slots, width = cond_ref.shape
    depth = width // shards
    group = shards * slots
    for place in range(shards):
        total = jnp.zeros((slots, depth), F32)
        for offset in range(shards):
            first = offset * group + offset * slots
            part = grad_ref[first : first + slots, :]
            total = total + jnp.where((spot_ref[0] ^ offset) == place, part, 0.0)
        cond = cond_ref[:, place * depth : (place + 1) * depth].astype(F32)
        logistic = 1.0 / (1.0 + jnp.exp(-cond))
        out_ref[:, place * depth : (place + 1) * depth] = (
            total * logistic * (1.0 + cond * (1.0 - logistic))
        )


def cond_call(spot, grads, condition, shards):
    return pl.pallas_call(
        functools.partial(cond_kernel, shards),
        in_specs=specs(1, pltpu.SMEM) + specs(2),
        out_specs=pl.BlockSpec(memory_space=pltpu.VMEM),
        out_shape=shape(condition.shape, F32),
        name="grad_condition",
        **params(),
    )(spot, grads, condition)


def after(value, *others):
    return lax.optimization_barrier((value,) + others)[0]


class Axis:
    def __init__(self, name, size, number):
        self.name = name
        self.size = size
        self.number = number
        self.index = lax.axis_index(name)
        self.bits = [1 << k for k in range(size.bit_length() - 1)]

    def swap(self, value, bit):
        return lax.ppermute(value, self.name, [(i, i ^ bit) for i in range(self.size)])

    def high(self, bit):
        return (self.index & bit) != 0


def ordered(high, mine, other, axis=0):
    return jnp.where(
        high, jnp.concatenate([other, mine], axis), jnp.concatenate([mine, other], axis)
    )


def gather_ordered(value, axis):
    dims = value.shape
    value = value[None]
    for bit in reversed(axis.bits):
        other = axis.swap(value, bit)
        high = axis.high(bit)
        value = jnp.stack([jnp.where(high, other, value), jnp.where(high, value, other)], 1)
        value = value.reshape((-1,) + dims)
    return value


class Gather:
    def __init__(self, piece, shard, rep, split):
        self.shard, self.rep = shard, rep
        self.own = piece
        half = piece.shape[0] // 2
        self.split = split is not None and half % 16 == 0 and rep.size > 1
        self.send = piece
        if self.split:
            late = after(piece, split)
            self.send = lax.dynamic_slice_in_dim(late, rep.high(1).astype(jnp.int32) * half, half, 0)
        self.held = [(piece, 0, None)]
        self.fars = []
        self.swapped = []

    def near(self, *gate):
        for bit in reversed(self.shard.bits[1:]):
            for value, offset, part in list(self.held):
                if value is self.own and self.split:
                    value, part = self.send, "near"
                self.held.append((self.shard.swap(after(value, *gate), bit), offset ^ bit, part))
        return self.held[-1][0]

    def far(self, *gate):
        for value, offset, part in self.held:
            if part == "near":
                self.fars.append((self.rep.swap(after(value, *gate), 1), offset, "far"))
        return self.fars[-1][0] if self.fars else self.held[-1][0]

    def swap_own(self, *gate):
        self.swap(self.held[:1], *gate)

    def swap_near(self, *gate):
        self.swap(self.held[1:], *gate)

    def swap_far(self, *gate):
        self.swap(self.fars, *gate)

    def swap(self, held, *gate):
        for value, offset, part in held:
            self.swapped.append((self.shard.swap(after(value, *gate), 1), offset ^ 1, part))

    def pieces(self):
        every = self.held + self.fars + self.swapped
        rows = self.own.shape[0]
        return [value for value, _, _ in every], tuple((offset, part, rows) for _, offset, part in every)


def plan(order, rows):
    stages = []
    back = []
    for at, (axis, bit) in enumerate(order):
        if axis.name == "shard":
            stages.append((axis, bit, 0))
        elif rows // 2 % 16 == 0 and at < len(order) - 1:
            rows //= 2
            stages.append((axis, bit, 1))
            back.insert(0, (axis, bit, rows))
        else:
            stages.append((axis, bit, None))
    return stages, back


class Reduction:
    def __init__(self, keep, operand, sent, stages, back):
        self.keep = keep
        self.operand = (operand,)
        self.sent = (sent,)
        self.stages, self.back = stages, back
        self.at = 0
        self.steps = len(stages) + len(back)

    def running(self):
        return self.at < self.steps

    def jobs(self):
        if self.at < len(self.stages):
            dim = self.stages[self.at][2]
            if dim is not None:
                return [dict(kind="halve", args=[self.keep, self.sent[0]], step=self.stages[self.at])]
        if self.at <= len(self.stages):
            return [dict(kind="add", args=[self.keep, self.sent[0]])]
        return [dict(kind="cat", args=[self.whole, self.sent[0]])]

    def commit(self, results):
        if self.at < len(self.stages):
            axis, bit, _ = self.stages[self.at]
            self.keep, operand = results[0][0], results[0][-1]
        else:
            axis, bit, _ = self.back[self.at - len(self.stages)]
            operand = self.whole = results[0][0]
        self.operand = (operand,)
        self.sent = (axis.swap(operand, bit),)
        self.at += 1

    def finish(self):
        terms = [(axis.number, bit, size) for axis, bit, size in self.back]
        flips = [(False,) * len(terms)]
        for k in range(len(terms)):
            flips += [flip[:k] + (True,) + flip[k + 1 :] for flip in flips]
        if self.back:
            pieces = [self.whole, self.sent[0]]
        else:
            total = self.keep.astype(F32) + self.sent[0].astype(F32)
            pieces = [total.astype(BF16)]
        count = sum(piece.shape[1] for piece in pieces) // len(flips)
        return pieces, terms, flips, count


def one_way(pair, shard, order):
    keep, send = pair
    return Reduction(keep, send, shard.swap(send, 1), *plan(order, keep.shape[1]))


class TwoWay:
    def __init__(self, pair, shard, rep):
        self.keeps, send = pair[0], pair[1]
        self.operand = (send,)
        self.sent = (shard.swap(send, 1),)
        inner = [(shard, bit, 0) for bit in reversed(shard.bits[1:])]
        near = (rep, 1, 1)
        self.orders = (inner + [near], [near] + inner)
        rows = self.keeps.shape[1] // 2
        self.stages, self.back = plan([(rep, bit) for bit in rep.bits[1:]], rows)
        self.back = self.back + [(rep, 1, rows)]
        self.round = 0
        self.inner = None

    def running(self):
        return self.inner is None or self.inner.running()

    def jobs(self):
        if self.inner is not None:
            self.inner.sent = self.sent
            return self.inner.jobs()
        if self.round == len(self.orders[0]):
            args = [self.keeps[0], self.sent[0], self.keeps[1], self.sent[1]]
            return [dict(kind="merge", args=args, step=self.stages[0])]
        jobs = []
        for part, order in enumerate(self.orders):
            if self.round == 0:
                jobs.append(dict(args=[self.keeps, self.sent[0]], part=part))
            else:
                jobs.append(dict(args=[self.keeps[part], self.sent[part]]))
            jobs[part].update(kind="halve", step=order[self.round])
        return jobs

    def commit(self, results):
        if self.inner is None and self.round < len(self.orders[0]):
            self.keeps = [keep for keep, _ in results]
            self.operand = tuple(operand for _, operand in results)
            steps = [order[self.round] for order in self.orders]
            self.sent = tuple(
                axis.swap(operand, bit) for (axis, bit, _), operand in zip(steps, self.operand)
            )
            self.round += 1
            return
        if self.inner is None:
            self.inner = Reduction(None, None, None, self.stages, self.back)
        self.inner.commit(results)
        self.operand, self.sent = self.inner.operand, self.inner.sent

    def finish(self):
        self.inner.sent = self.sent
        return self.inner.finish()


def two_way(pair, shard, rep):
    rows = pair[0].shape[1]
    if len(rep.bits) > 1 and rows // 4 % 16 == 0 and shard.size > 2:
        return TwoWay(pair, shard, rep)
    order = [(shard, bit) for bit in reversed(shard.bits[1:])] + [(rep, bit) for bit in rep.bits]
    return one_way(pair, shard, order)


class Chain:
    def __init__(self, value, steps):
        self.value = value
        self.todo = list(steps)
        self.send_next()

    def running(self):
        return self.join is not None

    def send_next(self):
        self.operand = (self.value,)
        axis, bit, self.join = self.todo.pop(0)
        self.sent = (axis.swap(self.value, bit),)

    def jobs(self):
        return []

    def commit(self, results):
        self.value = self.join(self.value, self.sent[0])
        self.join = None
        if self.todo:
            self.send_next()


def together(spot, chains, *values):
    got = lax.optimization_barrier((tuple(chain.sent for chain in chains), values))
    jobs = []
    shares = []
    for chain, sent in zip(chains, got[0]):
        chain.sent = sent
        shares.append(chain.jobs() if chain.running() else [])
        jobs += shares[-1]
    results = round_call(spot, jobs) if jobs else []
    for chain, share in zip(chains, shares):
        if chain.running():
            chain.commit(results[: len(share)])
            results = results[len(share) :]
    return got[1][0] if len(values) == 1 else got[1]


def rounds(spot, chains, most):
    for _ in range(most):
        running = [chain for chain in chains if chain.running()]
        if not running:
            return
        together(spot, running)


def launched(value, *chains):
    return after(value, *[operand for chain in chains for operand in chain.operand])


def per_device(
    shard_size,
    rep_size,
    tokens,
    condition,
    counts,
    cotangent,
    ada_weight,
    ada_bias,
    qkv_weight,
    qv_bias,
    proj_weight,
    proj_bias,
    fc1_weight,
    fc1_bias,
    fc2_weight,
    fc2_bias,
):
    shard = Axis("shard", shard_size, 0)
    rep = Axis("rep", rep_size, 1)
    spot = jnp.stack([shard.index, rep.index]).astype(jnp.int32)
    slots, width = condition.shape
    seq = tokens.shape[0] // slots
    rows = slots * seq
    depth = ada_weight.shape[0]

    slots_here = condition[None]
    arrived = []
    for bit in reversed(shard.bits):
        arrived.append(shard.swap(slots_here, bit))
        slots_here = jnp.stack([slots_here, arrived[-1]], 1).reshape((-1,) + condition.shape)
    slots_here = slots_here.reshape(-1, width)
    silu_group = jax.nn.silu(slots_here.astype(F32)).astype(BF16)
    my_cols = lax.dynamic_slice_in_dim(silu_group, shard.index * depth, depth, 1)
    ada_late, counts, *bias_list = lax.optimization_barrier(
        (ada_bias, counts, qv_bias, proj_bias, fc1_bias, fc2_bias, arrived[0])
    )[:-1]
    own_bias = lax.dynamic_update_slice(
        jnp.zeros((6 * width,), F32), ada_late.astype(F32), (shard.index * ada_bias.shape[0],)
    )
    modulation = dot_nn(my_cols, ada_weight) + own_bias[None]

    packed = jnp.concatenate(bias_list).astype(F32)
    packed = jnp.pad(packed, (0, 6 * width - packed.shape[0]))[None]
    qkv_gather = Gather(qkv_weight, shard, rep, None)
    near = qkv_gather.near(arrived[0])
    qkv_gather.swap_own(slots_here)
    queued = []
    for bit in reversed(shard.bits):
        half = modulation.shape[0] // 2
        queued.append(jnp.concatenate([modulation[half:], packed], 0))
        came = shard.swap(queued[-1], bit)
        modulation = modulation[:half] + came[:half]
        other, high = came[half:], shard.high(bit)
        packed = jnp.stack([jnp.where(high, other, packed), jnp.where(high, packed, other)], 1)
        packed = packed.reshape(-1, 6 * width)
    proj_gather = Gather(proj_weight, shard, rep, None)
    near_proj = proj_gather.near(queued[0])
    proj_gather.swap_own(slots_here)
    fc1_gather = Gather(fc1_weight, shard, rep, queued[0])
    fc2_gather = Gather(fc2_weight, shard, rep, queued[0])
    near_one = fc1_gather.near(near)
    near_two = fc2_gather.near(near_proj)
    wide = []
    start = 0
    for bias in bias_list:
        wide.append(packed[:, start : start + bias.shape[0]].reshape(1, -1))
        start += bias.shape[0]
    qv_b, proj_b, fc1_b, fc2_b = wide

    live_rows = lax.broadcasted_iota(jnp.int32, (rows, 1), 0) < counts[0] * seq
    cot = jnp.where(live_rows, cotangent, jnp.zeros_like(cotangent))

    qkv_gather.swap_near()
    proj_gather.swap_near()
    qkv_w = qkv_gather.pieces()
    proj_w = proj_gather.pieces()
    qkv_b = jnp.concatenate([qv_b[:, :width], jnp.zeros((1, width), F32), qv_b[:, width:]], axis=1)
    hidden_one, qkv = qkv_call(spot, tokens, modulation, qkv_b, qkv_w, slots)
    far_one = fc1_gather.far(qkv)
    fc1_gather.swap_near(qkv)
    fc1_gather.swap_own(qkv)
    fc2_gather.swap_own(qkv)
    mixed, branch_one, hidden_two, low_two = attn_call(
        spot, after(qkv, near_one), tokens, cot, modulation, proj_b, proj_w, slots
    )
    far_two = fc2_gather.far(hidden_two)
    fc2_gather.swap_near(hidden_two)
    fc1_gather.swap_far(hidden_two)
    fc1_w = fc1_gather.pieces()
    act_low, derivative = gelu_call(spot, after(hidden_two, near_two), fc1_b, fc1_w)
    fc2_gather.swap_far(act_low)
    fc2_w = fc2_gather.pieces()

    shard_steps = [(shard, bit) for bit in reversed(shard.bits[1:])]
    low_bits = [(rep, bit) for bit in rep.bits[:1]]
    high_bits = [(rep, bit) for bit in rep.bits[1:]]
    keep, send = wide_grad(spot, act_low, after(low_two, far_two), shard.size, "fc2_grad")
    fc2_sum = two_way((keep, after(send, *fc2_w[0])), shard, rep)
    block_out, gate_sums = out_call(spot,
        counts, launched(act_low, fc2_sum), tokens, branch_one, cot, modulation, fc2_b, fc2_w, slots
    )
    block_out, gate_sums = together(spot, [fc2_sum], block_out, gate_sums)
    low_pre, grad_fc1_b, grad_mid, low_one, sums = mlp_bwd_call(spot,
        launched(low_two, fc2_sum), derivative, tokens, branch_one, cot, modulation, fc1_w, fc2_w, slots
    )
    low_pre = together(spot, [fc2_sum], low_pre)
    keep, send = wide_grad(spot, hidden_two, launched(low_pre, fc2_sum), shard.size, "fc1_grad")
    keep, send, low_one = together(spot, [fc2_sum], keep, send, low_one)
    fc1_sum = two_way((keep, send), shard, rep)
    grad_mixed = mixed_bwd_call(spot, launched(low_one, fc1_sum, fc2_sum), proj_w)
    grad_mixed = together(spot, [fc1_sum, fc2_sum], grad_mixed)
    grad_qkv, qv_sums = attn_bwd_call(qkv, launched(grad_mixed, fc1_sum, fc2_sum), slots)
    grad_qkv, qv_sums = together(spot, [fc1_sum, fc2_sum], grad_qkv, qv_sums)
    first, second = attn_grad(
        spot,
        hidden_one,
        launched(grad_qkv, fc1_sum, fc2_sum),
        mixed,
        low_one,
        qv_sums,
        sums,
        grad_fc1_b,
        shard.size,
    )
    first, second, grad_qkv = together(spot, [fc1_sum, fc2_sum], first, second, grad_qkv)
    first_sum = one_way(first, shard, shard_steps + low_bits + high_bits)
    first_sum.back.reverse()
    second_sum = one_way(second, shard, low_bits + shard_steps + high_bits)
    grad_tokens, slot_values = input_bwd_call(spot,
        launched(grad_qkv, first_sum, second_sum, fc1_sum, fc2_sum),
        tokens,
        grad_mid,
        modulation,
        sums,
        gate_sums,
        condition,
        qkv_w,
        slots,
    )
    sums_list = [first_sum, second_sum, fc1_sum, fc2_sum]
    grad_tokens, slot_values = together(spot, sums_list, grad_tokens, slot_values)

    def append(mine, other):
        return jnp.concatenate([mine, other], 0)

    group_slots = Chain(slot_values, [(shard, bit, append) for bit in shard.bits])
    rounds(spot, sums_list + [group_slots], len(shard.bits))
    every = [(rep, bit, append) for bit in reversed(rep.bits)]
    all_slots = Chain(group_slots.value, every)
    grad_silu = dot_nt(group_slots.value[:, : 6 * width], ada_weight)
    to_cond = Chain(grad_silu, [(shard, bit, append) for bit in shard.bits])
    rounds(spot, sums_list + [all_slots, to_cond], 100)

    grad_cond = cond_call(spot, to_cond.value, condition, shard.size)

    mod_all = all_slots.value[:, : 6 * width]
    silu_cols = lax.dynamic_slice_in_dim(all_slots.value, 6 * width + shard.index * depth, depth, 1)
    grad_ada_w = dot_tn(silu_cols, mod_all)
    ada_b_all = jnp.sum(mod_all.astype(F32), axis=0)
    grad_ada_b = lax.dynamic_slice_in_dim(
        ada_b_all, shard.index * ada_bias.shape[0], ada_bias.shape[0], 0
    )

    grad_fc2_w = place_rows(spot, fc2_sum.finish(), fc2_weight.shape[0])
    grad_fc1_w = place_rows(spot, fc1_sum.finish(), fc1_weight.shape[0])
    bias_sizes = tuple(bias.shape[0] for bias in bias_list)
    grad_qkv_w, grad_proj_w, *bias_out = place_attn(
        spot, first_sum.finish(), second_sum.finish(), depth, width, bias_sizes
    )
    bias_out = [value.reshape(-1) for value in bias_out]

    return (
        block_out,
        grad_tokens,
        grad_cond,
        grad_ada_w,
        grad_ada_b,
        grad_qkv_w,
        bias_out[0],
        grad_proj_w,
        bias_out[1],
        grad_fc1_w,
        bias_out[2],
        grad_fc2_w,
        bias_out[3],
    )


def solution(mesh):
    rows = P(("rep", "shard"), None)
    weights = (P("shard", None), P("shard"))
    return jax.shard_map(
        functools.partial(per_device, mesh.shape["shard"], mesh.shape["rep"]),
        mesh=mesh,
        in_specs=(rows, rows, P(("rep", "shard")), rows) + weights * 5,
        out_specs=(rows, rows, rows) + weights * 5,
        check_vma=False,
    )
```

```python
import functools

import jax
import jax.numpy as jnp
from jax import lax
from jax.experimental import pallas as pl
from jax.experimental.pallas import tpu as pltpu
from jax.sharding import PartitionSpec as P

HEADS = 12
HEAD_DIM = 64
EPS = 1e-06
GELU_C = 0.7978845608028654
GELU_A = 0.044715
F32 = jnp.float32
BF16 = jnp.bfloat16
VMEM_LIMIT = 56 * 1024 * 1024


def norm_back(grad_hat, normed, inv_std):
    return inv_std * (
        grad_hat
        - jnp.mean(grad_hat, axis=-1, keepdims=True)
        - normed * jnp.mean(grad_hat * normed, axis=-1, keepdims=True)
    )


def gelu_pair(pre_act):
    square = pre_act * pre_act
    tanh_val = jnp.tanh(pre_act * (GELU_C + GELU_C * GELU_A * square))
    half = 0.5 + 0.5 * tanh_val
    activated = pre_act * half
    derivative = half + activated * (1.0 - tanh_val) * (GELU_C + 3.0 * GELU_C * GELU_A * square)
    return (activated, derivative)


def dot_nn(left, right):
    return lax.dot_general(left, right, (((1,), (0,)), ((), ())), preferred_element_type=F32)


def dot_nt(left, right):
    return lax.dot_general(left, right, (((1,), (1,)), ((), ())), preferred_element_type=F32)


def dot_tn(left, right):
    return lax.dot_general(left, right, (((0,), (0,)), ((), ())), preferred_element_type=F32)


def specs(count, space=pltpu.VMEM):
    return [pl.BlockSpec(memory_space=space)] * count


def shape(dims, dtype):
    return jax.ShapeDtypeStruct(dims, dtype)


COST_SHARE = 0.0


def params(flops=0, bytes_moved=0, exps=0):
    return dict(
        compiler_params=pltpu.CompilerParams(vmem_limit_bytes=VMEM_LIMIT),
        cost_estimate=pl.CostEstimate(
            flops=int(COST_SHARE * flops),
            bytes_accessed=int(COST_SHARE * bytes_moved),
            transcendentals=int(COST_SHARE * exps),
        ),
    )


def high_bit(spot_ref, number, bit):
    return lax.rem(lax.div(spot_ref[number], jnp.int32(bit)), jnp.int32(2))


def piece_copies(refs, offsets, spot_ref, whole, sems):
    copies = []
    for k, (ref, (offset, part, rows)) in enumerate(zip(refs, offsets)):
        first = (spot_ref[0] ^ offset) * rows
        if part is not None:
            half = high_bit(spot_ref, 1, 1)
            first = first + (half if part == "near" else 1 - half) * (rows // 2)
        place = whole.at[pl.ds(pl.multiple_of(first, 16), ref.shape[0]), :]
        copies.append(pltpu.make_async_copy(ref, place, sems.at[k]))
    return copies


def row_norm(value):
    center = value - jnp.mean(value, axis=-1, keepdims=True)
    inv_std = lax.rsqrt(jnp.mean(center * center, axis=-1, keepdims=True) + EPS)
    return center * inv_std, inv_std


def mod_part(mod_ref, slot, part, width):
    return mod_ref[slot : slot + 1, part * width : (part + 1) * width]


def qkv_kernel(offsets, slots, *refs):
    count = len(offsets)
    spot_ref, tok_ref, mod_ref, bias_ref = refs[:4]
    pieces = refs[4 : 4 + count]
    hidden_ref, qkv_ref, whole, sems = refs[4 + count :]
    copies = piece_copies(pieces, offsets, spot_ref, whole, sems)
    for copy in copies:
        copy.start()
    rows, width = tok_ref.shape
    seq = rows // slots
    for slot in range(slots):
        at = pl.ds(slot * seq, seq)
        normed, _ = row_norm(tok_ref[at, :].astype(F32))
        scale = 1.0 + mod_part(mod_ref, slot, 1, width)
        hidden_ref[at, :] = (normed * scale + mod_part(mod_ref, slot, 0, width)).astype(BF16)
    for copy in copies:
        copy.wait()
    for part in range(3):
        cols = pl.ds(part * width, width)
        qkv_ref[:, cols] = (
            dot_nn(hidden_ref[...], whole[:, cols]) + bias_ref[:, cols]
        ).astype(BF16)


def qkv_call(spot, tokens, modulation, bias, weight, slots):
    rows, width = tokens.shape
    pieces, offsets = weight
    return pl.pallas_call(
        functools.partial(qkv_kernel, offsets, slots),
        in_specs=specs(1, pltpu.SMEM) + specs(3) + specs(len(pieces), pl.ANY),
        out_specs=specs(2),
        out_shape=[shape((rows, width), BF16), shape((rows, 3 * width), BF16)],
        scratch_shapes=[
            pltpu.VMEM((width, 3 * width), BF16),
            pltpu.SemaphoreType.DMA((len(pieces),)),
        ],
        name="qkv_fwd",
        **params(6 * rows * width * width, 10 * rows * width + 6 * width * width),
    )(spot, tokens, modulation, bias, *pieces)


def pair_masks(rows):
    lane = lax.broadcasted_iota(jnp.int32, (rows, 2 * HEAD_DIM), 1)
    return lane < HEAD_DIM


def attn_kernel(offsets, *refs):
    count = len(offsets)
    spot_ref, qkv_ref, tok_ref, cot_ref, mod_ref, bias_ref = refs[:6]
    pieces = refs[6 : 6 + count]
    mixed_ref, branch_ref, hidden_ref, low_ref, whole, sems = refs[6 + count :]
    rows, width = tok_ref.shape
    copies = piece_copies(pieces, offsets, spot_ref, whole, sems)

    @pl.when(pl.program_id(0) == 0)
    def _():
        for copy in copies:
            copy.start()

    first = pair_masks(rows)
    for pair in range(HEADS // 2):
        cols = pl.ds(pair * 128, 128)
        query_pair = qkv_ref[:, cols]
        key_pair = qkv_ref[:, pl.ds(width + pair * 128, 128)]
        value_pair = qkv_ref[:, pl.ds(2 * width + pair * 128, 128)]
        parts = []
        none = jnp.zeros_like(query_pair)
        for head in range(2):
            keep = first if head == 0 else jnp.logical_not(first)
            scores = dot_nt(key_pair, jnp.where(keep, query_pair, none)) * HEAD_DIM ** (-0.5)
            exped = jnp.exp(scores - jnp.max(scores, axis=0, keepdims=True))
            probs = exped * (1.0 / jnp.sum(exped, axis=0, keepdims=True))
            parts.append(dot_tn(probs.astype(BF16), value_pair))
        mixed_ref[:, cols] = jnp.where(first, parts[0], parts[1]).astype(BF16)

    @pl.when(pl.program_id(0) == 0)
    def _():
        for copy in copies:
            copy.wait()

    mod = mod_ref[0]
    branch = dot_nn(mixed_ref[...], whole[...]) + bias_ref[...]
    branch_ref[...] = branch
    normed, _ = row_norm(tok_ref[...].astype(F32) + mod_part(mod, 0, 2, width) * branch)
    scale = 1.0 + mod_part(mod, 0, 4, width)
    hidden_ref[...] = (normed * scale + mod_part(mod, 0, 3, width)).astype(BF16)
    cot = jnp.where(spot_ref[2] > pl.program_id(0), cot_ref[...].astype(F32), 0.0)
    low_ref[...] = (mod_part(mod, 0, 5, width) * cot).astype(BF16)


def attn_call(spot, qkv, tokens, cot, modulation, bias, weight, slots):
    rows, width = tokens.shape
    seq = rows // slots
    pieces, offsets = weight
    by_slot = pl.BlockSpec((seq, width), lambda s: (s, 0))
    return pl.pallas_call(
        functools.partial(attn_kernel, offsets),
        grid=(slots,),
        in_specs=specs(1, pltpu.SMEM)
        + [
            pl.BlockSpec((seq, 3 * width), lambda s: (s, 0)),
            by_slot,
            by_slot,
            pl.BlockSpec((1, 1, 6 * width), lambda s: (s, 0, 0)),
            pl.BlockSpec((1, width), lambda s: (0, 0)),
        ]
        + specs(len(pieces), pl.ANY),
        out_specs=[by_slot] * 4,
        out_shape=[
            shape((rows, width), BF16),
            shape((rows, width), F32),
            shape((rows, width), BF16),
            shape((rows, width), BF16),
        ],
        scratch_shapes=[
            pltpu.VMEM((width, width), BF16),
            pltpu.SemaphoreType.DMA((len(pieces),)),
        ],
        name="attn_fwd",
        **params(
            2 * rows * width * width + 4 * rows * width * seq * 4,
            24 * rows * width,
            rows * seq * HEADS,
        ),
    )(spot, qkv, tokens, cot, modulation[:, None, :], bias, *pieces)


FF_BLOCK = 768


def gelu_kernel(offsets, *refs):
    count = len(offsets)
    spot_ref, hidden_ref, bias_ref = refs[:3]
    pieces = refs[3 : 3 + count]
    act_ref, deriv_ref, whole, sems = refs[3 + count :]
    step = pl.program_id(0)

    @pl.when(step == 0)
    def _():
        copies = piece_copies(pieces, offsets, spot_ref, whole, sems)
        for copy in copies:
            copy.start()
        for copy in copies:
            copy.wait()

    cols = pl.ds(pl.multiple_of(step * FF_BLOCK, FF_BLOCK), FF_BLOCK)
    pre_act = dot_nn(hidden_ref[...], whole[:, cols]) + bias_ref[...]
    activated, derivative = gelu_pair(pre_act)
    act_ref[...] = activated.astype(BF16)
    deriv_ref[...] = derivative


def gelu_call(spot, hidden, bias, weight):
    rows, width = hidden.shape
    pieces, offsets = weight
    hidden_units = bias.shape[1]
    block = pl.BlockSpec((rows, FF_BLOCK), lambda j: (0, j))
    return pl.pallas_call(
        functools.partial(gelu_kernel, offsets),
        grid=(hidden_units // FF_BLOCK,),
        in_specs=specs(1, pltpu.SMEM)
        + [
            pl.BlockSpec((rows, width), lambda j: (0, 0)),
            pl.BlockSpec((1, FF_BLOCK), lambda j: (0, j)),
        ]
        + specs(len(pieces), pl.ANY),
        out_specs=[block, block],
        out_shape=[shape((rows, hidden_units), BF16), shape((rows, hidden_units), F32)],
        scratch_shapes=[
            pltpu.VMEM((width, hidden_units), BF16),
            pltpu.SemaphoreType.DMA((len(pieces),)),
        ],
        name="fc1_gelu",
        **params(
            2 * rows * width * hidden_units, 8 * rows * hidden_units, rows * hidden_units
        ),
    )(spot, hidden, bias, *pieces)


def out_kernel(offsets, slots, *refs):
    count = len(offsets)
    spot_ref, act_ref, tok_ref, branch_ref, cot_ref, mod_ref, bias_ref = refs[:7]
    pieces = refs[7 : 7 + count]
    block_ref, gate_ref, whole, sems = refs[7 + count :]
    copies = piece_copies(pieces, offsets, spot_ref, whole, sems)
    for copy in copies:
        copy.start()
    for copy in copies:
        copy.wait()
    rows, width = tok_ref.shape
    seq = rows // slots
    for slot in range(slots):
        at = pl.ds(slot * seq, seq)
        branch_two = dot_nn(act_ref[at, :], whole[...]) + bias_ref[...]
        live = spot_ref[2] > slot
        cot = jnp.where(live, cot_ref[at, :].astype(F32), 0.0)
        gate_ref[slot : slot + 1, :] = jnp.sum(cot * branch_two, axis=0, keepdims=True)
        mid = tok_ref[at, :].astype(F32) + mod_part(mod_ref, slot, 2, width) * branch_ref[at, :]
        block = mid + mod_part(mod_ref, slot, 5, width) * branch_two
        block_ref[at, :] = jnp.where(live, block, 0.0).astype(BF16)


def out_call(spot, act_low, tokens, branch_one, cot, modulation, bias, weight, slots):
    rows, width = tokens.shape
    hidden_units = act_low.shape[1]
    pieces, offsets = weight
    return pl.pallas_call(
        functools.partial(out_kernel, offsets, slots),
        in_specs=specs(1, pltpu.SMEM) + specs(6) + specs(len(pieces), pl.ANY),
        out_specs=specs(2),
        out_shape=[shape((rows, width), BF16), shape((slots, width), F32)],
        scratch_shapes=[
            pltpu.VMEM((hidden_units, width), BF16),
            pltpu.SemaphoreType.DMA((len(pieces),)),
        ],
        name="fc2_fwd",
        **params(2 * rows * width * hidden_units, 2 * (rows + width) * hidden_units),
    )(spot, act_low, tokens, branch_one, cot, modulation, bias, *pieces)


def mlp_bwd_kernel(one_offsets, two_offsets, slots, *refs):
    count, both = len(one_offsets), len(one_offsets) + len(two_offsets)
    spot_ref, low_ref, deriv_ref, tok_ref, branch_ref, cot_ref, mod_ref = refs[:7]
    one_pieces = refs[7 : 7 + count]
    two_pieces = refs[7 + count : 7 + both]
    (low_pre_ref, fc1_b_ref, mid_ref, low_one_ref, sums_ref, one, two, acc, sems_one, sems_two) = refs[
        7 + both :
    ]
    step = pl.program_id(0)
    copies_two = piece_copies(two_pieces, two_offsets, spot_ref, two, sems_two)
    copies_one = piece_copies(one_pieces, one_offsets, spot_ref, one, sems_one)

    @pl.when(step == 0)
    def _():
        for copy in copies_two + copies_one:
            copy.start()
        acc[...] = jnp.zeros_like(acc)
        for copy in copies_two:
            copy.wait()

    ff = pl.ds(pl.multiple_of(step * FF_BLOCK, FF_BLOCK), FF_BLOCK)
    grad_pre = dot_nt(low_ref[...], two[ff, :]) * deriv_ref[...]
    fc1_b_ref[...] = jnp.sum(grad_pre, axis=0, keepdims=True)
    low_pre = grad_pre.astype(BF16)
    low_pre_ref[...] = low_pre

    @pl.when(step == 0)
    def _():
        for copy in copies_one:
            copy.wait()

    acc[...] += dot_nt(low_pre, one[:, ff])

    @pl.when(step == pl.num_programs(0) - 1)
    def _():
        rows, width = tok_ref.shape
        seq = rows // slots
        for slot in range(slots):
            at = pl.ds(slot * seq, seq)
            branch = branch_ref[at, :]
            cot = jnp.where(spot_ref[2] > slot, cot_ref[at, :].astype(F32), 0.0)
            gate_one = mod_part(mod_ref, slot, 2, width)
            normed, inv_std = row_norm(tok_ref[at, :].astype(F32) + gate_one * branch)
            grad_hidden = acc[at, :]
            scale = 1.0 + mod_part(mod_ref, slot, 4, width)
            grad_mid = cot + norm_back(grad_hidden * scale, normed, inv_std)
            mid_ref[at, :] = grad_mid
            grad_branch = gate_one * grad_mid
            low_one_ref[at, :] = grad_branch.astype(BF16)

            def put(part, value):
                sums_ref[part, slot : slot + 1, :] = jnp.sum(value, axis=0, keepdims=True)

            put(0, grad_mid * branch)
            put(1, grad_hidden)
            put(2, grad_hidden * normed)
            put(3, grad_branch)
            put(4, mod_part(mod_ref, slot, 5, width) * cot)


def mlp_bwd_call(spot, low_two, derivative, tokens, branch_one, cot, modulation, one, two, slots):
    rows, width = tokens.shape
    hidden_units = derivative.shape[1]
    block = pl.BlockSpec((rows, FF_BLOCK), lambda j: (0, j))
    whole = pl.BlockSpec((rows, width), lambda j: (0, 0))
    return pl.pallas_call(
        functools.partial(mlp_bwd_kernel, one[1], two[1], slots),
        grid=(hidden_units // FF_BLOCK,),
        in_specs=specs(1, pltpu.SMEM)
        + [whole, block, whole, whole, whole, pl.BlockSpec((slots, 6 * width), lambda j: (0, 0))]
        + specs(len(one[0]) + len(two[0]), pl.ANY),
        out_specs=[
            block,
            pl.BlockSpec((1, FF_BLOCK), lambda j: (0, j)),
            whole,
            whole,
            pl.BlockSpec((5, slots, width), lambda j: (0, 0, 0)),
        ],
        out_shape=[
            shape((rows, hidden_units), BF16),
            shape((1, hidden_units), F32),
            shape((rows, width), F32),
            shape((rows, width), BF16),
            shape((5, slots, width), F32),
        ],
        scratch_shapes=[
            pltpu.VMEM((width, hidden_units), BF16),
            pltpu.VMEM((hidden_units, width), BF16),
            pltpu.VMEM((rows, width), F32),
            pltpu.SemaphoreType.DMA((len(one[0]),)),
            pltpu.SemaphoreType.DMA((len(two[0]),)),
        ],
        name="mlp_bwd",
        **params(4 * rows * width * hidden_units, 6 * rows * hidden_units + 4 * width * hidden_units),
    )(spot, low_two, derivative, tokens, branch_one, cot, modulation, *one[0], *two[0])


def attn_bwd_kernel(qkv_ref, grad_ref, out_ref, bias_ref):
    rows = qkv_ref.shape[0]
    width = grad_ref.shape[1]
    first = pair_masks(rows)
    for pair in range(HEADS // 2):
        query_cols = pl.ds(pair * 128, 128)
        key_cols = pl.ds(width + pair * 128, 128)
        value_cols = pl.ds(2 * width + pair * 128, 128)
        query_pair = qkv_ref[:, query_cols]
        key_pair = qkv_ref[:, key_cols]
        value_pair = qkv_ref[:, value_cols]
        grad_pair = grad_ref[:, query_cols]
        grads = []
        for head in range(2):
            keep = first if head == 0 else jnp.logical_not(first)
            none = jnp.zeros_like(query_pair)
            scores = dot_nt(key_pair, jnp.where(keep, query_pair, none)) * HEAD_DIM ** (-0.5)
            exped = jnp.exp(scores - jnp.max(scores, axis=0, keepdims=True))
            probs = exped * (1.0 / jnp.sum(exped, axis=0, keepdims=True))
            grad_probs = dot_nt(value_pair, jnp.where(keep, grad_pair, none))
            dots = jnp.sum(probs * grad_probs, axis=0, keepdims=True)
            grad_scores = (probs * (grad_probs - dots) * HEAD_DIM ** (-0.5)).astype(BF16)
            grads.append(
                (
                    dot_tn(grad_scores, key_pair),
                    dot_nn(grad_scores, query_pair),
                    dot_nn(probs.astype(BF16), grad_pair),
                )
            )
        grad_query, grad_key, grad_value = (
            jnp.where(first, left, right) for left, right in zip(grads[0], grads[1])
        )
        out_ref[:, query_cols] = grad_query.astype(BF16)
        out_ref[:, key_cols] = grad_key.astype(BF16)
        out_ref[:, value_cols] = grad_value.astype(BF16)
        bias_ref[0, :, query_cols] = jnp.sum(grad_query, axis=0, keepdims=True)
        bias_ref[0, :, key_cols] = jnp.sum(grad_value, axis=0, keepdims=True)


def attn_bwd_call(qkv, grad_mixed, slots):
    rows, width = grad_mixed.shape
    seq = rows // slots
    return pl.pallas_call(
        attn_bwd_kernel,
        grid=(slots,),
        in_specs=[
            pl.BlockSpec((seq, 3 * width), lambda s: (s, 0)),
            pl.BlockSpec((seq, width), lambda s: (s, 0)),
        ],
        out_specs=[
            pl.BlockSpec((seq, 3 * width), lambda s: (s, 0)),
            pl.BlockSpec((1, 1, 2 * width), lambda s: (s, 0, 0)),
        ],
        out_shape=[
            shape((rows, 3 * width), BF16),
            shape((slots, 1, 2 * width), F32),
        ],
        name="attn_bwd",
        **params(20 * rows * width * seq, 16 * rows * width, rows * seq * HEADS),
    )(qkv, grad_mixed)


def mixed_bwd_kernel(offsets, *refs):
    count = len(offsets)
    spot_ref, low_ref = refs[:2]
    pieces = refs[2 : 2 + count]
    out_ref, whole, sems = refs[2 + count :]
    copies = piece_copies(pieces, offsets, spot_ref, whole, sems)
    for copy in copies:
        copy.start()
    for copy in copies:
        copy.wait()
    out_ref[...] = dot_nt(low_ref[...], whole[...]).astype(BF16)


def mixed_bwd_call(spot, low_one, weight):
    rows, width = low_one.shape
    pieces, offsets = weight
    return pl.pallas_call(
        functools.partial(mixed_bwd_kernel, offsets),
        in_specs=specs(1, pltpu.SMEM) + specs(1) + specs(len(pieces), pl.ANY),
        out_specs=pl.BlockSpec(memory_space=pltpu.VMEM),
        out_shape=shape((rows, width), BF16),
        scratch_shapes=[
            pltpu.VMEM((width, width), BF16),
            pltpu.SemaphoreType.DMA((len(pieces),)),
        ],
        name="proj_bwd",
        **params(2 * rows * width * width, 4 * rows * width + 2 * width * width),
    )(spot, low_one, *pieces)


def input_bwd_kernel(offsets, slots, *refs):
    count = len(offsets)
    spot_ref, grad_ref, tok_ref, mid_ref, mod_ref, sums_ref, gate_ref, cond_ref = refs[:8]
    pieces = refs[8 : 8 + count]
    out_ref, mod_out, whole, sems = refs[8 + count :]
    copies = piece_copies(pieces, offsets, spot_ref, whole, sems)
    for copy in copies:
        copy.start()
    for copy in copies:
        copy.wait()
    rows, width = tok_ref.shape
    seq = rows // slots

    def put(slot, part, value):
        mod_out[slot : slot + 1, part * width : (part + 1) * width] = value.astype(BF16)

    for slot in range(slots):
        at = pl.ds(slot * seq, seq)
        row = slice(slot, slot + 1)
        grad_hidden = dot_nt(grad_ref[at, :], whole[...])
        normed, inv_std = row_norm(tok_ref[at, :].astype(F32))
        scale = 1.0 + mod_part(mod_ref, slot, 1, width)
        out_ref[at, :] = mid_ref[at, :] + norm_back(grad_hidden * scale, normed, inv_std)
        put(slot, 0, jnp.sum(grad_hidden, axis=0, keepdims=True))
        put(slot, 1, jnp.sum(grad_hidden * normed, axis=0, keepdims=True))
        for part in range(3):
            put(slot, 2 + part, sums_ref[part, row, :])
        put(slot, 5, gate_ref[row, :])
        cond = cond_ref[row, :].astype(F32)
        put(slot, 6, cond * (1.0 / (1.0 + jnp.exp(-cond))))


def input_bwd_call(spot, grad_qkv, tokens, grad_mid, modulation, sums, gate_sums, condition, weight, slots):
    rows, width = tokens.shape
    pieces, offsets = weight
    return pl.pallas_call(
        functools.partial(input_bwd_kernel, offsets, slots),
        in_specs=specs(1, pltpu.SMEM) + specs(7) + specs(len(pieces), pl.ANY),
        out_specs=specs(2),
        out_shape=[shape((rows, width), F32), shape((slots, 7 * width), BF16)],
        scratch_shapes=[
            pltpu.VMEM((width, 3 * width), BF16),
            pltpu.SemaphoreType.DMA((len(pieces),)),
        ],
        name="qkv_bwd",
        **params(6 * rows * width * width, 16 * rows * width + 6 * width * width),
    )(spot, grad_qkv, tokens, grad_mid, modulation, sums, gate_sums, condition, *pieces)


def split_store(core, total, depth, keep_ref, send_ref, cols):
    for far in range(total.shape[0] // (2 * depth)):
        even = total[2 * far * depth : (2 * far + 1) * depth]
        odd = total[(2 * far + 1) * depth : (2 * far + 2) * depth]
        keep_ref[far, :, cols] = jnp.where(core == 0, even, odd)
        send_ref[far, :, cols] = jnp.where(core == 0, odd, even).astype(BF16)


def wide_grad_kernel(spot_ref, left_ref, right_ref, keep_ref, send_ref):
    total = dot_tn(left_ref[...], right_ref[...])
    split_store(spot_ref[0] & 1, total, keep_ref.shape[1], keep_ref, send_ref, slice(None))


def wide_grad(spot, left, right, shards, name):
    rows, in_dim = left.shape
    out_dim = right.shape[1]
    depth = in_dim // shards
    block = out_dim // 2 if out_dim > 1024 else out_dim
    per_step = shards // 2 if in_dim <= 768 else 1
    out_block = pl.BlockSpec((per_step, depth, block), lambda i, j: (i, 0, j))
    dims = (shards // 2, depth, out_dim)
    return pl.pallas_call(
        wide_grad_kernel,
        grid=(shards // 2 // per_step, out_dim // block),
        in_specs=specs(1, pltpu.SMEM)
        + [
            pl.BlockSpec((rows, 2 * depth * per_step), lambda i, j: (0, i)),
            pl.BlockSpec((rows, block), lambda i, j: (0, j)),
        ],
        out_specs=[out_block, out_block],
        out_shape=[shape(dims, F32), shape(dims, BF16)],
        name=name,
        **params(2 * rows * in_dim * out_dim, 3 * in_dim * out_dim + 2 * rows * (in_dim + out_dim)),
    )(spot, left, right)


EXTRA = 256


def bias_rows(count):
    return [(start, min(EXTRA, count - start)) for start in range(0, count, EXTRA)]


def attn_grad_kernel(shards, *refs):
    spot_ref, hidden_ref, qkv_ref, mixed_ref, low_ref, qv_ref, sums_ref, fc1_ref = refs[:8]
    keep_a, send_a, keep_b, send_b, extra = refs[8:]
    depth = keep_a.shape[1]
    width = hidden_ref.shape[1]
    core = spot_ref[0] & 1
    total = dot_tn(hidden_ref[...], qkv_ref[...])
    split_store(core, total[:, : 2 * width], depth, keep_a, send_a, slice(None))
    split_store(core, total[:, 2 * width :], depth, keep_b, send_b, pl.ds(0, width))
    total = dot_tn(mixed_ref[...], low_ref[...])
    split_store(core, total, depth, keep_b, send_b, pl.ds(width, width))
    extra[...] = jnp.zeros_like(extra)
    biases = (
        jnp.sum(qv_ref[...], axis=0),
        jnp.sum(sums_ref[3], axis=0, keepdims=True),
        fc1_ref[...],
        jnp.sum(sums_ref[4], axis=0, keepdims=True),
    )
    for place in range(shards):
        row = place * depth
        for bias in biases:
            count = bias.shape[1] // shards
            for start, size in bias_rows(count):
                first = place * count + start
                extra[row : row + 1, :size] = bias[:, first : first + size]
                row += 1
    split_store(core, extra[...], depth, keep_b, send_b, pl.ds(2 * width, EXTRA))


def attn_grad(spot, hidden, grad_qkv, mixed, low_one, qv_sums, sums, fc1_sums, shards):
    rows, width = hidden.shape
    first = (shards // 2, width // shards, 2 * width)
    second = (shards // 2, width // shards, 2 * width + EXTRA)
    outs = pl.pallas_call(
        functools.partial(attn_grad_kernel, shards),
        in_specs=specs(1, pltpu.SMEM) + specs(7),
        out_specs=specs(4),
        out_shape=[shape(first, F32), shape(first, BF16), shape(second, F32), shape(second, BF16)],
        scratch_shapes=[pltpu.VMEM((width, EXTRA), F32)],
        name="attn_weight_grads",
        **params(8 * rows * width * width, 12 * width * width + 14 * rows * width),
    )(spot, hidden, grad_qkv, mixed, low_one, qv_sums, sums, fc1_sums)
    return outs[:2], outs[2:]


def round_kernel(kinds, spot_ref, *refs):
    ins = list(refs[: sum(kind[1] for kind in kinds)])
    outs = list(refs[len(ins) :])
    for kind, count in kinds:
        args, ins = ins[:count], ins[count:]
        if kind == "halve":
            keep_out, send_out, outs = outs[0], outs[1], outs[2:]
            keep_out[...] = args[0][...] + args[2][...].astype(F32)
            send_out[...] = (args[1][...] + args[3][...].astype(F32)).astype(BF16)
        elif kind == "merge":
            keep_out, send_out, outs = outs[0], outs[1], outs[2:]
            half = keep_out.shape[2] // 2
            for part in range(2):
                mine, other, sent_mine, sent_other = args[4 * part : 4 * part + 4]
                cols = slice(part * half, (part + 1) * half)
                keep_out[:, :, cols] = mine[...] + sent_mine[...].astype(F32)
                send_out[:, :, cols] = (other[...] + sent_other[...].astype(F32)).astype(BF16)
        elif kind == "add":
            out, outs = outs[0], outs[1:]
            out[...] = (args[0][...].astype(F32) + args[1][...].astype(F32)).astype(BF16)
        else:
            out, outs = outs[0], outs[1:]
            rows = args[0].shape[1]
            out[:, :rows, :] = args[0][...]
            out[:, rows:, :] = args[1][...]


SMALL_ROUND = 1 << 20


def round_call(spot, jobs):
    split = 2 if sum(value.size for job in jobs for value in job["args"]) > SMALL_ROUND else 1
    for job in jobs:
        cols = job["args"][0].shape[2] // (1 if job.get("part") is None else 2)
        if job["kind"] == "merge" or cols % 256:
            split = 1
    in_specs, args, out_specs, out_shape = [], [], [], []

    def halves_of(value, axis, bit, dim, base, dims, chunk):
        def spec(other):
            def place(j, spot_ref):
                half = high_bit(spot_ref, axis.number, bit)
                half = 1 - half if other else half
                return (half, 0, base + j) if dim == 0 else (0, half, base + j)

            return pl.BlockSpec((dims[0], dims[1], chunk), place)

        in_specs.extend([spec(False), spec(True)])
        args.extend([value, value])

    def plain(dims):
        return pl.BlockSpec((dims[0], dims[1], dims[2] // split), lambda j, spot_ref: (0, 0, j))

    kinds = []
    for job in jobs:
        values = job["args"]
        kind = job["kind"]
        dims = list(values[0].shape)
        before = len(args)
        if kind in ("halve", "merge"):
            axis, bit, dim = job["step"]
            dims[dim] //= 2
            part = job.get("part")
            if part is not None:
                dims[2] //= 2
            chunk = dims[2] // split
            base = 0 if part is None else part * split
            for value in values:
                halves_of(value, axis, bit, dim, base, dims, chunk)
            if kind == "merge":
                dims[2] *= 2
            out_specs += [plain(dims)] * 2
            out_shape += [shape(tuple(dims), F32), shape(tuple(dims), BF16)]
        else:
            in_specs += [plain(value.shape) for value in values]
            args += values
            if kind == "cat":
                dims[1] += values[1].shape[1]
            out_specs.append(plain(dims))
            out_shape.append(shape(tuple(dims), BF16))
        kinds.append((kind, len(args) - before))
    outs = pl.pallas_call(
        functools.partial(round_kernel, kinds),
        grid_spec=pltpu.PrefetchScalarGridSpec(
            num_scalar_prefetch=1, grid=(split,), in_specs=in_specs, out_specs=out_specs
        ),
        out_shape=out_shape,
        name="sum_round",
        **params(0, 0),
    )(spot, *args)
    outs = list(outs)
    results = []
    for kind, _ in kinds:
        count = 2 if kind in ("halve", "merge") else 1
        results.append(outs[:count])
        outs = outs[count:]
    return results


def first_row(spot_ref, terms, flips):
    row = 0
    for (number, bit, size), flip in zip(terms, flips):
        half = high_bit(spot_ref, number, bit)
        row = row + (1 - half if flip else half) * size
    return row


def row_places(spot_ref, refs, terms, flips, count):
    parts = []
    for ref in refs:
        parts += [(ref, slice(k * count, (k + 1) * count)) for k in range(ref.shape[1] // count)]
    for (ref, rows), flip in zip(parts, flips):
        at = first_row(spot_ref, terms, flip)
        if not isinstance(at, int):
            at = pl.multiple_of(at, 16)
        yield ref, rows, pl.ds(at, count)


def place_kernel(terms, flips, count, spot_ref, *refs):
    out_ref = refs[-1]
    for ref, rows, at in row_places(spot_ref, refs[:-1], terms, flips, count):
        out_ref[at, :] = ref[0, rows, :].astype(F32)


def place_rows(spot, done, rows):
    pieces, terms, flips, count = done
    cols = pieces[0].shape[2]
    return pl.pallas_call(
        functools.partial(place_kernel, terms, flips, count),
        in_specs=specs(1, pltpu.SMEM) + specs(len(pieces)),
        out_specs=pl.BlockSpec(memory_space=pltpu.VMEM),
        out_shape=shape((rows, cols), F32),
        name="place_rows",
        **params(0, rows * cols * 6),
    )(spot, *pieces)


def place_attn_kernel(plans, parts, biases, spot_ref, *refs):
    qkv_out, proj_out, *bias_outs, head = refs[2 * parts :]
    width = proj_out.shape[1]
    for ref, rows, at in row_places(spot_ref, refs[:parts], *plans[0]):
        qkv_out[at, : 2 * width] = ref[0, rows, :].astype(F32)
    for ref, rows, at in row_places(spot_ref, refs[parts : 2 * parts], *plans[1]):
        qkv_out[at, 2 * width :] = ref[0, rows, :width].astype(F32)
        proj_out[at, :] = ref[0, rows, width : 2 * width].astype(F32)
        head[at, :] = ref[0, rows, 2 * width :].astype(F32)
    row = 0
    for count, out in zip(biases, bias_outs):
        for start, size in bias_rows(count):
            out[start : start + size] = head[row, :size]
            row += 1


def place_attn(spot, first, second, rows, width, biases):
    parts = len(first[0])
    return pl.pallas_call(
        functools.partial(place_attn_kernel, (first[1:], second[1:]), parts, biases),
        in_specs=specs(1, pltpu.SMEM) + specs(2 * parts),
        out_specs=specs(2 + len(biases)),
        out_shape=[shape((rows, 3 * width), F32), shape((rows, width), F32)]
        + [shape((count,), F32) for count in biases],
        scratch_shapes=[pltpu.VMEM((rows, EXTRA), F32)],
        name="place_attn",
        **params(0, rows * width * 24),
    )(spot, *first[0], *second[0])


def cond_kernel(shards, spot_ref, grad_ref, cond_ref, out_ref):
    slots, width = cond_ref.shape
    depth = width // shards
    group = shards * slots
    for place in range(shards):
        total = jnp.zeros((slots, depth), F32)
        for offset in range(shards):
            first = offset * group + offset * slots
            part = grad_ref[first : first + slots, :]
            total = total + jnp.where((spot_ref[0] ^ offset) == place, part, 0.0)
        cond = cond_ref[:, place * depth : (place + 1) * depth].astype(F32)
        logistic = 1.0 / (1.0 + jnp.exp(-cond))
        out_ref[:, place * depth : (place + 1) * depth] = (
            total * logistic * (1.0 + cond * (1.0 - logistic))
        )


def cond_call(spot, grads, condition, shards):
    return pl.pallas_call(
        functools.partial(cond_kernel, shards),
        in_specs=specs(1, pltpu.SMEM) + specs(2),
        out_specs=pl.BlockSpec(memory_space=pltpu.VMEM),
        out_shape=shape(condition.shape, F32),
        name="grad_condition",
        **params(),
    )(spot, grads, condition)


def after(value, *others):
    return lax.optimization_barrier((value,) + others)[0]


class Axis:
    def __init__(self, name, size, number):
        self.name = name
        self.size = size
        self.number = number
        self.index = lax.axis_index(name)
        self.bits = [1 << k for k in range(size.bit_length() - 1)]

    def swap(self, value, bit):
        return lax.ppermute(value, self.name, [(i, i ^ bit) for i in range(self.size)])

    def high(self, bit):
        return (self.index & bit) != 0


def ordered(high, mine, other, axis=0):
    return jnp.where(
        high, jnp.concatenate([other, mine], axis), jnp.concatenate([mine, other], axis)
    )


def gather_ordered(value, axis):
    dims = value.shape
    value = value[None]
    for bit in reversed(axis.bits):
        other = axis.swap(value, bit)
        high = axis.high(bit)
        value = jnp.stack([jnp.where(high, other, value), jnp.where(high, value, other)], 1)
        value = value.reshape((-1,) + dims)
    return value


class Gather:
    def __init__(self, piece, shard, rep, split):
        self.shard, self.rep = shard, rep
        self.own = piece
        half = piece.shape[0] // 2
        self.split = split is not None and half % 16 == 0 and rep.size > 1
        self.send = piece
        if self.split:
            late = after(piece, split)
            self.send = lax.dynamic_slice_in_dim(late, rep.high(1).astype(jnp.int32) * half, half, 0)
        self.held = [(piece, 0, None)]
        self.fars = []
        self.swapped = []

    def near(self, *gate):
        for bit in reversed(self.shard.bits[1:]):
            for value, offset, part in list(self.held):
                if value is self.own and self.split:
                    value, part = self.send, "near"
                self.held.append((self.shard.swap(after(value, *gate), bit), offset ^ bit, part))
        return self.held[-1][0]

    def far(self, *gate):
        for value, offset, part in self.held:
            if part == "near":
                self.fars.append((self.rep.swap(after(value, *gate), 1), offset, "far"))
        return self.fars[-1][0] if self.fars else self.held[-1][0]

    def swap_own(self, *gate):
        self.swap(self.held[:1], *gate)

    def swap_near(self, *gate):
        self.swap(self.held[1:], *gate)

    def swap_far(self, *gate):
        self.swap(self.fars, *gate)

    def swap(self, held, *gate):
        for value, offset, part in held:
            self.swapped.append((self.shard.swap(after(value, *gate), 1), offset ^ 1, part))

    def pieces(self):
        every = self.held + self.fars + self.swapped
        rows = self.own.shape[0]
        return [value for value, _, _ in every], tuple((offset, part, rows) for _, offset, part in every)


def plan(order, rows):
    stages = []
    back = []
    for at, (axis, bit) in enumerate(order):
        if axis.name == "shard":
            stages.append((axis, bit, 0))
        elif rows // 2 % 16 == 0 and at < len(order) - 1:
            rows //= 2
            stages.append((axis, bit, 1))
            back.insert(0, (axis, bit, rows))
        else:
            stages.append((axis, bit, None))
    return stages, back


class Reduction:
    def __init__(self, keep, operand, sent, stages, back):
        self.keep = keep
        self.operand = (operand,)
        self.sent = (sent,)
        self.stages, self.back = stages, back
        self.at = 0
        self.steps = len(stages) + len(back)

    def running(self):
        return self.at < self.steps

    def jobs(self):
        if self.at < len(self.stages):
            dim = self.stages[self.at][2]
            if dim is not None:
                return [dict(kind="halve", args=[self.keep, self.sent[0]], step=self.stages[self.at])]
        if self.at <= len(self.stages):
            return [dict(kind="add", args=[self.keep, self.sent[0]])]
        return [dict(kind="cat", args=[self.whole, self.sent[0]])]

    def commit(self, results):
        if self.at < len(self.stages):
            axis, bit, _ = self.stages[self.at]
            self.keep, operand = results[0][0], results[0][-1]
        else:
            axis, bit, _ = self.back[self.at - len(self.stages)]
            operand = self.whole = results[0][0]
        self.operand = (operand,)
        self.sent = (axis.swap(operand, bit),)
        self.at += 1

    def finish(self):
        terms = [(axis.number, bit, size) for axis, bit, size in self.back]
        flips = [(False,) * len(terms)]
        for k in range(len(terms)):
            flips += [flip[:k] + (True,) + flip[k + 1 :] for flip in flips]
        if self.back:
            pieces = [self.whole, self.sent[0]]
        else:
            total = self.keep.astype(F32) + self.sent[0].astype(F32)
            pieces = [total.astype(BF16)]
        count = sum(piece.shape[1] for piece in pieces) // len(flips)
        return pieces, terms, flips, count


def one_way(pair, shard, order):
    keep, send = pair
    return Reduction(keep, send, shard.swap(send, 1), *plan(order, keep.shape[1]))


class TwoWay:
    def __init__(self, pair, shard, rep):
        self.keeps, send = pair[0], pair[1]
        self.operand = (send,)
        self.sent = (shard.swap(send, 1),)
        inner = [(shard, bit, 0) for bit in reversed(shard.bits[1:])]
        near = (rep, 1, 1)
        self.orders = (inner + [near], [near] + inner)
        rows = self.keeps.shape[1] // 2
        self.stages, self.back = plan([(rep, bit) for bit in rep.bits[1:]], rows)
        self.back = self.back + [(rep, 1, rows)]
        self.round = 0
        self.inner = None

    def running(self):
        return self.inner is None or self.inner.running()

    def jobs(self):
        if self.inner is not None:
            self.inner.sent = self.sent
            return self.inner.jobs()
        if self.round == len(self.orders[0]):
            args = [self.keeps[0], self.sent[0], self.keeps[1], self.sent[1]]
            return [dict(kind="merge", args=args, step=self.stages[0])]
        jobs = []
        for part, order in enumerate(self.orders):
            if self.round == 0:
                jobs.append(dict(args=[self.keeps, self.sent[0]], part=part))
            else:
                jobs.append(dict(args=[self.keeps[part], self.sent[part]]))
            jobs[part].update(kind="halve", step=order[self.round])
        return jobs

    def commit(self, results):
        if self.inner is None and self.round < len(self.orders[0]):
            self.keeps = [keep for keep, _ in results]
            self.operand = tuple(operand for _, operand in results)
            steps = [order[self.round] for order in self.orders]
            self.sent = tuple(
                axis.swap(operand, bit) for (axis, bit, _), operand in zip(steps, self.operand)
            )
            self.round += 1
            return
        if self.inner is None:
            self.inner = Reduction(None, None, None, self.stages, self.back)
        self.inner.commit(results)
        self.operand, self.sent = self.inner.operand, self.inner.sent

    def finish(self):
        self.inner.sent = self.sent
        return self.inner.finish()


def two_way(pair, shard, rep):
    rows = pair[0].shape[1]
    if len(rep.bits) > 1 and rows // 4 % 16 == 0 and shard.size > 2:
        return TwoWay(pair, shard, rep)
    order = [(shard, bit) for bit in reversed(shard.bits[1:])] + [(rep, bit) for bit in rep.bits]
    return one_way(pair, shard, order)


class Chain:
    def __init__(self, value, steps):
        self.value = value
        self.todo = list(steps)
        self.send_next()

    def running(self):
        return self.join is not None

    def send_next(self):
        self.operand = (self.value,)
        axis, bit, self.join = self.todo.pop(0)
        self.sent = (axis.swap(self.value, bit),)

    def jobs(self):
        return []

    def commit(self, results):
        self.value = self.join(self.value, self.sent[0])
        self.join = None
        if self.todo:
            self.send_next()


def together(spot, chains, *values):
    got = lax.optimization_barrier((tuple(chain.sent for chain in chains), values))
    jobs = []
    shares = []
    for chain, sent in zip(chains, got[0]):
        chain.sent = sent
        shares.append(chain.jobs() if chain.running() else [])
        jobs += shares[-1]
    results = round_call(spot, jobs) if jobs else []
    for chain, share in zip(chains, shares):
        if chain.running():
            chain.commit(results[: len(share)])
            results = results[len(share) :]
    return got[1][0] if len(values) == 1 else got[1]


def rounds(spot, chains, most):
    for _ in range(most):
        running = [chain for chain in chains if chain.running()]
        if not running:
            return
        together(spot, running)


def launched(value, *chains):
    return after(value, *[operand for chain in chains for operand in chain.operand])


def per_device(
    shard_size,
    rep_size,
    tokens,
    condition,
    counts,
    cotangent,
    ada_weight,
    ada_bias,
    qkv_weight,
    qv_bias,
    proj_weight,
    proj_bias,
    fc1_weight,
    fc1_bias,
    fc2_weight,
    fc2_bias,
):
    shard = Axis("shard", shard_size, 0)
    rep = Axis("rep", rep_size, 1)
    spot = jnp.stack([shard.index, rep.index]).astype(jnp.int32)
    slots, width = condition.shape
    seq = tokens.shape[0] // slots
    rows = slots * seq
    depth = ada_weight.shape[0]

    slots_here = condition[None]
    arrived = []
    for bit in reversed(shard.bits):
        arrived.append(shard.swap(slots_here, bit))
        slots_here = jnp.stack([slots_here, arrived[-1]], 1).reshape((-1,) + condition.shape)
    slots_here = slots_here.reshape(-1, width)
    silu_group = jax.nn.silu(slots_here.astype(F32)).astype(BF16)
    my_cols = lax.dynamic_slice_in_dim(silu_group, shard.index * depth, depth, 1)
    ada_late, counts, *bias_list = lax.optimization_barrier(
        (ada_bias, counts, qv_bias, proj_bias, fc1_bias, fc2_bias, slots_here)
    )[:-1]
    own_bias = lax.dynamic_update_slice(
        jnp.zeros((6 * width,), F32), ada_late.astype(F32), (shard.index * ada_bias.shape[0],)
    )
    modulation = dot_nn(my_cols, ada_weight) + own_bias[None]

    packed = jnp.concatenate(bias_list).astype(F32)
    packed = jnp.pad(packed, (0, 6 * width - packed.shape[0]))[None]
    qkv_gather = Gather(qkv_weight, shard, rep, condition)
    near = qkv_gather.near(arrived[0])
    qkv_gather.far()
    qkv_gather.swap_own(slots_here)
    queued = []
    partial = []
    for bit in reversed(shard.bits):
        half = modulation.shape[0] // 2
        send = jnp.concatenate([modulation[half:], packed], 0)
        queued.append(send if queued else after(send, near))
        came = shard.swap(queued[-1], bit)
        partial.append(came)
        modulation = modulation[:half] + came[:half]
        other, high = came[half:], shard.high(bit)
        packed = jnp.stack([jnp.where(high, other, packed), jnp.where(high, packed, other)], 1)
        packed = packed.reshape(-1, 6 * width)
    proj_gather = Gather(proj_weight, shard, rep, None)
    near_proj = proj_gather.near(queued[0])
    proj_gather.swap_own(slots_here)
    fc1_gather = Gather(fc1_weight, shard, rep, queued[0])
    fc2_gather = Gather(fc2_weight, shard, rep, queued[0])
    near_one = fc1_gather.near(partial[0])
    near_two = fc2_gather.near(near_proj)
    wide = []
    start = 0
    for bias in bias_list:
        wide.append(packed[:, start : start + bias.shape[0]].reshape(1, -1))
        start += bias.shape[0]
    qv_b, proj_b, fc1_b, fc2_b = wide

    spot = jnp.concatenate([spot, counts])
    cot = cotangent

    qkv_gather.swap_near()
    qkv_gather.swap_far()
    proj_gather.swap_near()
    qkv_w = qkv_gather.pieces()
    proj_w = proj_gather.pieces()
    qkv_b = jnp.concatenate([qv_b[:, :width], jnp.zeros((1, width), F32), qv_b[:, width:]], axis=1)
    hidden_one, qkv = qkv_call(spot, tokens, modulation, qkv_b, qkv_w, slots)
    far_one = fc1_gather.far(qkv)
    fc1_gather.swap_near(qkv)
    fc1_gather.swap_own(qkv)
    fc2_gather.swap_own(qkv)
    mixed, branch_one, hidden_two, low_two = attn_call(
        spot, after(qkv, near_one), tokens, cot, modulation, proj_b, proj_w, slots
    )
    far_two = fc2_gather.far(hidden_two)
    fc2_gather.swap_near(hidden_two)
    fc1_gather.swap_far(hidden_two)
    fc1_w = fc1_gather.pieces()
    act_low, derivative = gelu_call(spot, after(hidden_two, near_two), fc1_b, fc1_w)
    fc2_gather.swap_far(act_low)
    fc2_w = fc2_gather.pieces()

    shard_steps = [(shard, bit) for bit in reversed(shard.bits[1:])]
    low_bits = [(rep, bit) for bit in rep.bits[:1]]
    high_bits = [(rep, bit) for bit in rep.bits[1:]]
    keep, send = wide_grad(spot, act_low, after(low_two, far_two), shard.size, "fc2_grad")
    fc2_sum = two_way((keep, after(send, *fc2_w[0])), shard, rep)
    block_out, gate_sums = out_call(
        spot, launched(act_low, fc2_sum), tokens, branch_one, cot, modulation, fc2_b, fc2_w, slots
    )
    block_out, gate_sums = together(spot, [fc2_sum], block_out, gate_sums)
    low_pre, grad_fc1_b, grad_mid, low_one, sums = mlp_bwd_call(spot,
        launched(low_two, fc2_sum), derivative, tokens, branch_one, cot, modulation, fc1_w, fc2_w, slots
    )
    low_pre = together(spot, [fc2_sum], low_pre)
    keep, send = wide_grad(spot, hidden_two, launched(low_pre, fc2_sum), shard.size, "fc1_grad")
    keep, send, low_one = together(spot, [fc2_sum], keep, send, low_one)
    fc1_sum = two_way((keep, send), shard, rep)
    grad_mixed = mixed_bwd_call(spot, launched(low_one, fc1_sum, fc2_sum), proj_w)
    grad_mixed = together(spot, [fc1_sum, fc2_sum], grad_mixed)
    grad_qkv, qv_sums = attn_bwd_call(qkv, launched(grad_mixed, fc1_sum, fc2_sum), slots)
    grad_qkv, qv_sums = together(spot, [fc1_sum, fc2_sum], grad_qkv, qv_sums)
    first, second = attn_grad(
        spot,
        hidden_one,
        launched(grad_qkv, fc1_sum, fc2_sum),
        mixed,
        low_one,
        qv_sums,
        sums,
        grad_fc1_b,
        shard.size,
    )
    first, second, grad_qkv = together(spot, [fc1_sum, fc2_sum], first, second, grad_qkv)
    first_sum = one_way(first, shard, shard_steps + low_bits + high_bits)
    first_sum.back.reverse()
    second_sum = one_way(second, shard, low_bits + shard_steps + high_bits)
    grad_tokens, slot_values = input_bwd_call(spot,
        launched(grad_qkv, first_sum, second_sum, fc1_sum, fc2_sum),
        tokens,
        grad_mid,
        modulation,
        sums,
        gate_sums,
        condition,
        qkv_w,
        slots,
    )
    sums_list = [first_sum, second_sum, fc1_sum] + ([fc2_sum] if fc2_sum.running() else [])
    grad_tokens, slot_values = together(spot, sums_list, grad_tokens, slot_values)

    def append(mine, other):
        return jnp.concatenate([mine, other], 0)

    group_slots = Chain(slot_values, [(shard, bit, append) for bit in shard.bits])
    rounds(spot, sums_list + [group_slots], len(shard.bits))
    every = [(rep, bit, append) for bit in reversed(rep.bits)]
    all_slots = Chain(group_slots.value, every)
    grad_silu = dot_nt(group_slots.value[:, : 6 * width], ada_weight)
    to_cond = Chain(grad_silu, [(shard, bit, append) for bit in shard.bits])
    rounds(spot, sums_list + [all_slots, to_cond], 100)

    grad_cond = cond_call(spot, to_cond.value, condition, shard.size)

    mod_all = all_slots.value[:, : 6 * width]
    silu_cols = lax.dynamic_slice_in_dim(all_slots.value, 6 * width + shard.index * depth, depth, 1)
    grad_ada_w = dot_tn(silu_cols, mod_all)
    ada_b_all = jnp.sum(mod_all.astype(F32), axis=0)
    grad_ada_b = lax.dynamic_slice_in_dim(
        ada_b_all, shard.index * ada_bias.shape[0], ada_bias.shape[0], 0
    )

    grad_fc2_w = place_rows(spot, fc2_sum.finish(), fc2_weight.shape[0])
    grad_fc1_w = place_rows(spot, fc1_sum.finish(), fc1_weight.shape[0])
    bias_sizes = tuple(bias.shape[0] for bias in bias_list)
    grad_qkv_w, grad_proj_w, *bias_out = place_attn(
        spot, first_sum.finish(), second_sum.finish(), depth, width, bias_sizes
    )

    return (
        block_out,
        grad_tokens,
        grad_cond,
        grad_ada_w,
        grad_ada_b,
        grad_qkv_w,
        bias_out[0],
        grad_proj_w,
        bias_out[1],
        grad_fc1_w,
        bias_out[2],
        grad_fc2_w,
        bias_out[3],
    )


def solution(mesh):
    rows = P(("rep", "shard"), None)
    weights = (P("shard", None), P("shard"))
    return jax.shard_map(
        functools.partial(per_device, mesh.shape["shard"], mesh.shape["rep"]),
        mesh=mesh,
        in_specs=(rows, rows, P(("rep", "shard")), rows) + weights * 5,
        out_specs=(rows, rows, rows) + weights * 5,
        check_vma=False,
    )
```

```python
import functools

import jax
import jax.numpy as jnp
from jax import lax
from jax.experimental import pallas as pl
from jax.experimental.pallas import tpu as pltpu
from jax.sharding import PartitionSpec as P

HEADS = 12
HEAD_DIM = 64
EPS = 1e-06
GELU_C = 0.7978845608028654
GELU_A = 0.044715
F32 = jnp.float32
BF16 = jnp.bfloat16
VMEM_LIMIT = 56 * 1024 * 1024


def norm_back(grad_hat, normed, inv_std):
    return inv_std * (
        grad_hat
        - jnp.mean(grad_hat, axis=-1, keepdims=True)
        - normed * jnp.mean(grad_hat * normed, axis=-1, keepdims=True)
    )


def gelu_pair(pre_act):
    square = pre_act * pre_act
    tanh_val = jnp.tanh(pre_act * (GELU_C + GELU_C * GELU_A * square))
    half = 0.5 + 0.5 * tanh_val
    activated = pre_act * half
    derivative = half + activated * (1.0 - tanh_val) * (GELU_C + 3.0 * GELU_C * GELU_A * square)
    return (activated, derivative)


def dot_nn(left, right):
    return lax.dot_general(left, right, (((1,), (0,)), ((), ())), preferred_element_type=F32)


def dot_nt(left, right):
    return lax.dot_general(left, right, (((1,), (1,)), ((), ())), preferred_element_type=F32)


def dot_tn(left, right):
    return lax.dot_general(left, right, (((0,), (0,)), ((), ())), preferred_element_type=F32)


def specs(count, space=pltpu.VMEM):
    return [pl.BlockSpec(memory_space=space)] * count


def shape(dims, dtype):
    return jax.ShapeDtypeStruct(dims, dtype)


COST_SHARE = 0.0


def params(flops=0, bytes_moved=0, exps=0):
    return dict(
        compiler_params=pltpu.CompilerParams(vmem_limit_bytes=VMEM_LIMIT),
        cost_estimate=pl.CostEstimate(
            flops=int(COST_SHARE * flops),
            bytes_accessed=int(COST_SHARE * bytes_moved),
            transcendentals=int(COST_SHARE * exps),
        ),
    )


def high_bit(spot_ref, number, bit):
    return lax.rem(lax.div(spot_ref[number], jnp.int32(bit)), jnp.int32(2))


def piece_copies(refs, offsets, spot_ref, whole, sems):
    copies = []
    for k, (ref, (offset, part, rows)) in enumerate(zip(refs, offsets)):
        first = (spot_ref[0] ^ offset) * rows
        if part is not None:
            half = high_bit(spot_ref, 1, 1)
            first = first + (half if part == "near" else 1 - half) * (rows // 2)
        place = whole.at[pl.ds(pl.multiple_of(first, 16), ref.shape[0]), :]
        copies.append(pltpu.make_async_copy(ref, place, sems.at[k]))
    return copies


def row_norm(value):
    center = value - jnp.mean(value, axis=-1, keepdims=True)
    inv_std = lax.rsqrt(jnp.mean(center * center, axis=-1, keepdims=True) + EPS)
    return center * inv_std, inv_std


def mod_part(mod_ref, slot, part, width):
    return mod_ref[slot : slot + 1, part * width : (part + 1) * width]


def qkv_kernel(offsets, slots, *refs):
    count = len(offsets)
    spot_ref, tok_ref, mod_ref, bias_ref = refs[:4]
    pieces = refs[4 : 4 + count]
    hidden_ref, qkv_ref, whole, sems = refs[4 + count :]
    copies = piece_copies(pieces, offsets, spot_ref, whole, sems)
    for copy in copies:
        copy.start()
    rows, width = tok_ref.shape
    seq = rows // slots
    for slot in range(slots):
        at = pl.ds(slot * seq, seq)
        normed, _ = row_norm(tok_ref[at, :].astype(F32))
        scale = 1.0 + mod_part(mod_ref, slot, 1, width)
        hidden_ref[at, :] = (normed * scale + mod_part(mod_ref, slot, 0, width)).astype(BF16)
    for copy in copies:
        copy.wait()
    for part in range(3):
        cols = pl.ds(part * width, width)
        qkv_ref[:, cols] = (
            dot_nn(hidden_ref[...], whole[:, cols]) + bias_ref[:, cols]
        ).astype(BF16)


def qkv_call(spot, tokens, modulation, bias, weight, slots):
    rows, width = tokens.shape
    pieces, offsets = weight
    return pl.pallas_call(
        functools.partial(qkv_kernel, offsets, slots),
        in_specs=specs(1, pltpu.SMEM) + specs(3) + specs(len(pieces), pl.ANY),
        out_specs=specs(2),
        out_shape=[shape((rows, width), BF16), shape((rows, 3 * width), BF16)],
        scratch_shapes=[
            pltpu.VMEM((width, 3 * width), BF16),
            pltpu.SemaphoreType.DMA((len(pieces),)),
        ],
        name="qkv_fwd",
        **params(6 * rows * width * width, 10 * rows * width + 6 * width * width),
    )(spot, tokens, modulation, bias, *pieces)


def pair_masks(rows):
    lane = lax.broadcasted_iota(jnp.int32, (rows, 2 * HEAD_DIM), 1)
    return lane < HEAD_DIM


def attn_kernel(offsets, *refs):
    count = len(offsets)
    spot_ref, qkv_ref, tok_ref, cot_ref, mod_ref, bias_ref = refs[:6]
    pieces = refs[6 : 6 + count]
    mixed_ref, branch_ref, hidden_ref, low_ref, whole, sems = refs[6 + count :]
    rows, width = tok_ref.shape
    copies = piece_copies(pieces, offsets, spot_ref, whole, sems)

    @pl.when(pl.program_id(0) == 0)
    def _():
        for copy in copies:
            copy.start()

    first = pair_masks(rows)
    for pair in range(HEADS // 2):
        cols = pl.ds(pair * 128, 128)
        query_pair = qkv_ref[:, cols]
        key_pair = qkv_ref[:, pl.ds(width + pair * 128, 128)]
        value_pair = qkv_ref[:, pl.ds(2 * width + pair * 128, 128)]
        parts = []
        none = jnp.zeros_like(query_pair)
        for head in range(2):
            keep = first if head == 0 else jnp.logical_not(first)
            scores = dot_nt(key_pair, jnp.where(keep, query_pair, none)) * HEAD_DIM ** (-0.5)
            exped = jnp.exp(scores - jnp.max(scores, axis=0, keepdims=True))
            probs = exped * (1.0 / jnp.sum(exped, axis=0, keepdims=True))
            parts.append(dot_tn(probs.astype(BF16), value_pair))
        mixed_ref[:, cols] = jnp.where(first, parts[0], parts[1]).astype(BF16)

    @pl.when(pl.program_id(0) == 0)
    def _():
        for copy in copies:
            copy.wait()

    mod = mod_ref[0]
    branch = dot_nn(mixed_ref[...], whole[...]) + bias_ref[...]
    branch_ref[...] = branch
    normed, _ = row_norm(tok_ref[...].astype(F32) + mod_part(mod, 0, 2, width) * branch)
    scale = 1.0 + mod_part(mod, 0, 4, width)
    hidden_ref[...] = (normed * scale + mod_part(mod, 0, 3, width)).astype(BF16)
    cot = jnp.where(spot_ref[2] > pl.program_id(0), cot_ref[...].astype(F32), 0.0)
    low_ref[...] = (mod_part(mod, 0, 5, width) * cot).astype(BF16)


def attn_call(spot, qkv, tokens, cot, modulation, bias, weight, slots):
    rows, width = tokens.shape
    seq = rows // slots
    pieces, offsets = weight
    by_slot = pl.BlockSpec((seq, width), lambda s: (s, 0))
    return pl.pallas_call(
        functools.partial(attn_kernel, offsets),
        grid=(slots,),
        in_specs=specs(1, pltpu.SMEM)
        + [
            pl.BlockSpec((seq, 3 * width), lambda s: (s, 0)),
            by_slot,
            by_slot,
            pl.BlockSpec((1, 1, 6 * width), lambda s: (s, 0, 0)),
            pl.BlockSpec((1, width), lambda s: (0, 0)),
        ]
        + specs(len(pieces), pl.ANY),
        out_specs=[by_slot] * 4,
        out_shape=[
            shape((rows, width), BF16),
            shape((rows, width), F32),
            shape((rows, width), BF16),
            shape((rows, width), BF16),
        ],
        scratch_shapes=[
            pltpu.VMEM((width, width), BF16),
            pltpu.SemaphoreType.DMA((len(pieces),)),
        ],
        name="attn_fwd",
        **params(
            2 * rows * width * width + 4 * rows * width * seq * 4,
            24 * rows * width,
            rows * seq * HEADS,
        ),
    )(spot, qkv, tokens, cot, modulation[:, None, :], bias, *pieces)


FF_BLOCK = 768


def gelu_kernel(offsets, *refs):
    count = len(offsets)
    spot_ref, hidden_ref, bias_ref = refs[:3]
    pieces = refs[3 : 3 + count]
    act_ref, deriv_ref, whole, sems = refs[3 + count :]
    step = pl.program_id(0)

    @pl.when(step == 0)
    def _():
        copies = piece_copies(pieces, offsets, spot_ref, whole, sems)
        for copy in copies:
            copy.start()
        for copy in copies:
            copy.wait()

    cols = pl.ds(pl.multiple_of(step * FF_BLOCK, FF_BLOCK), FF_BLOCK)
    pre_act = dot_nn(hidden_ref[...], whole[:, cols]) + bias_ref[...]
    activated, derivative = gelu_pair(pre_act)
    act_ref[...] = activated.astype(BF16)
    deriv_ref[...] = derivative


def gelu_call(spot, hidden, bias, weight):
    rows, width = hidden.shape
    pieces, offsets = weight
    hidden_units = bias.shape[1]
    block = pl.BlockSpec((rows, FF_BLOCK), lambda j: (0, j))
    return pl.pallas_call(
        functools.partial(gelu_kernel, offsets),
        grid=(hidden_units // FF_BLOCK,),
        in_specs=specs(1, pltpu.SMEM)
        + [
            pl.BlockSpec((rows, width), lambda j: (0, 0)),
            pl.BlockSpec((1, FF_BLOCK), lambda j: (0, j)),
        ]
        + specs(len(pieces), pl.ANY),
        out_specs=[block, block],
        out_shape=[shape((rows, hidden_units), BF16), shape((rows, hidden_units), F32)],
        scratch_shapes=[
            pltpu.VMEM((width, hidden_units), BF16),
            pltpu.SemaphoreType.DMA((len(pieces),)),
        ],
        name="fc1_gelu",
        **params(
            2 * rows * width * hidden_units, 8 * rows * hidden_units, rows * hidden_units
        ),
    )(spot, hidden, bias, *pieces)


def out_kernel(offsets, slots, *refs):
    count = len(offsets)
    spot_ref, act_ref, tok_ref, branch_ref, cot_ref, mod_ref, bias_ref = refs[:7]
    pieces = refs[7 : 7 + count]
    block_ref, gate_ref, whole, sems = refs[7 + count :]
    slot = pl.program_id(0)
    width = tok_ref.shape[1]

    @pl.when(slot == 0)
    def _():
        copies = piece_copies(pieces, offsets, spot_ref, whole, sems)
        for copy in copies:
            copy.start()
        for copy in copies:
            copy.wait()

    mod = mod_ref[0]
    branch_two = dot_nn(act_ref[...], whole[...]) + bias_ref[...]
    live = spot_ref[2] > slot
    cot = jnp.where(live, cot_ref[...].astype(F32), 0.0)
    gate = jnp.sum(cot * branch_two, axis=0, keepdims=True)
    for place in range(slots):

        @pl.when(slot == place)
        def _():
            gate_ref[place : place + 1, :] = gate

    mid = tok_ref[...].astype(F32) + mod_part(mod, 0, 2, width) * branch_ref[...]
    block = mid + mod_part(mod, 0, 5, width) * branch_two
    block_ref[...] = jnp.where(live, block, 0.0).astype(BF16)


def out_call(spot, act_low, tokens, branch_one, cot, modulation, bias, weight, slots):
    rows, width = tokens.shape
    hidden_units = act_low.shape[1]
    pieces, offsets = weight
    by_slot = pl.BlockSpec((rows // slots, width), lambda s: (s, 0))
    return pl.pallas_call(
        functools.partial(out_kernel, offsets, slots),
        grid=(slots,),
        in_specs=specs(1, pltpu.SMEM)
        + [
            pl.BlockSpec((rows // slots, hidden_units), lambda s: (s, 0)),
            by_slot,
            by_slot,
            by_slot,
            pl.BlockSpec((1, 1, 6 * width), lambda s: (s, 0, 0)),
            pl.BlockSpec((1, width), lambda s: (0, 0)),
        ]
        + specs(len(pieces), pl.ANY),
        out_specs=[by_slot, pl.BlockSpec((slots, width), lambda s: (0, 0))],
        out_shape=[shape((rows, width), BF16), shape((slots, width), F32)],
        scratch_shapes=[
            pltpu.VMEM((hidden_units, width), BF16),
            pltpu.SemaphoreType.DMA((len(pieces),)),
        ],
        name="fc2_fwd",
        **params(2 * rows * width * hidden_units, 2 * (rows + width) * hidden_units),
    )(spot, act_low, tokens, branch_one, cot, modulation[:, None, :], bias, *pieces)


def mlp_bwd_kernel(one_offsets, two_offsets, slots, *refs):
    count, both = len(one_offsets), len(one_offsets) + len(two_offsets)
    spot_ref, low_ref, deriv_ref, tok_ref, branch_ref, cot_ref, mod_ref = refs[:7]
    one_pieces = refs[7 : 7 + count]
    two_pieces = refs[7 + count : 7 + both]
    (low_pre_ref, fc1_b_ref, mid_ref, low_one_ref, sums_ref, one, two, acc, sems_one, sems_two) = refs[
        7 + both :
    ]
    step = pl.program_id(0)
    copies_two = piece_copies(two_pieces, two_offsets, spot_ref, two, sems_two)
    copies_one = piece_copies(one_pieces, one_offsets, spot_ref, one, sems_one)

    @pl.when(step == 0)
    def _():
        for copy in copies_two + copies_one:
            copy.start()
        acc[...] = jnp.zeros_like(acc)
        for copy in copies_two:
            copy.wait()

    ff = pl.ds(pl.multiple_of(step * FF_BLOCK, FF_BLOCK), FF_BLOCK)
    grad_pre = dot_nt(low_ref[...], two[ff, :]) * deriv_ref[...]
    fc1_b_ref[...] = jnp.sum(grad_pre, axis=0, keepdims=True)
    low_pre = grad_pre.astype(BF16)
    low_pre_ref[...] = low_pre

    @pl.when(step == 0)
    def _():
        for copy in copies_one:
            copy.wait()

    acc[...] += dot_nt(low_pre, one[:, ff])

    @pl.when(step == pl.num_programs(0) - 1)
    def _():
        rows, width = tok_ref.shape
        seq = rows // slots
        for slot in range(slots):
            at = pl.ds(slot * seq, seq)
            branch = branch_ref[at, :]
            cot = jnp.where(spot_ref[2] > slot, cot_ref[at, :].astype(F32), 0.0)
            gate_one = mod_part(mod_ref, slot, 2, width)
            normed, inv_std = row_norm(tok_ref[at, :].astype(F32) + gate_one * branch)
            grad_hidden = acc[at, :]
            scale = 1.0 + mod_part(mod_ref, slot, 4, width)
            grad_mid = cot + norm_back(grad_hidden * scale, normed, inv_std)
            mid_ref[at, :] = grad_mid
            grad_branch = gate_one * grad_mid
            low_one_ref[at, :] = grad_branch.astype(BF16)

            def put(part, value):
                sums_ref[part, slot : slot + 1, :] = jnp.sum(value, axis=0, keepdims=True)

            put(0, grad_mid * branch)
            put(1, grad_hidden)
            put(2, grad_hidden * normed)
            put(3, grad_branch)
            put(4, mod_part(mod_ref, slot, 5, width) * cot)


def mlp_bwd_call(spot, low_two, derivative, tokens, branch_one, cot, modulation, one, two, slots):
    rows, width = tokens.shape
    hidden_units = derivative.shape[1]
    block = pl.BlockSpec((rows, FF_BLOCK), lambda j: (0, j))
    whole = pl.BlockSpec((rows, width), lambda j: (0, 0))
    return pl.pallas_call(
        functools.partial(mlp_bwd_kernel, one[1], two[1], slots),
        grid=(hidden_units // FF_BLOCK,),
        in_specs=specs(1, pltpu.SMEM)
        + [whole, block, whole, whole, whole, pl.BlockSpec((slots, 6 * width), lambda j: (0, 0))]
        + specs(len(one[0]) + len(two[0]), pl.ANY),
        out_specs=[
            block,
            pl.BlockSpec((1, FF_BLOCK), lambda j: (0, j)),
            whole,
            whole,
            pl.BlockSpec((5, slots, width), lambda j: (0, 0, 0)),
        ],
        out_shape=[
            shape((rows, hidden_units), BF16),
            shape((1, hidden_units), F32),
            shape((rows, width), F32),
            shape((rows, width), BF16),
            shape((5, slots, width), F32),
        ],
        scratch_shapes=[
            pltpu.VMEM((width, hidden_units), BF16),
            pltpu.VMEM((hidden_units, width), BF16),
            pltpu.VMEM((rows, width), F32),
            pltpu.SemaphoreType.DMA((len(one[0]),)),
            pltpu.SemaphoreType.DMA((len(two[0]),)),
        ],
        name="mlp_bwd",
        **params(4 * rows * width * hidden_units, 6 * rows * hidden_units + 4 * width * hidden_units),
    )(spot, low_two, derivative, tokens, branch_one, cot, modulation, *one[0], *two[0])


def attn_bwd_kernel(qkv_ref, grad_ref, out_ref, bias_ref):
    rows = qkv_ref.shape[0]
    width = grad_ref.shape[1]
    first = pair_masks(rows)
    for pair in range(HEADS // 2):
        query_cols = pl.ds(pair * 128, 128)
        key_cols = pl.ds(width + pair * 128, 128)
        value_cols = pl.ds(2 * width + pair * 128, 128)
        query_pair = qkv_ref[:, query_cols]
        key_pair = qkv_ref[:, key_cols]
        value_pair = qkv_ref[:, value_cols]
        grad_pair = grad_ref[:, query_cols]
        grads = []
        for head in range(2):
            keep = first if head == 0 else jnp.logical_not(first)
            none = jnp.zeros_like(query_pair)
            scores = dot_nt(key_pair, jnp.where(keep, query_pair, none)) * HEAD_DIM ** (-0.5)
            exped = jnp.exp(scores - jnp.max(scores, axis=0, keepdims=True))
            probs = exped * (1.0 / jnp.sum(exped, axis=0, keepdims=True))
            grad_probs = dot_nt(value_pair, jnp.where(keep, grad_pair, none))
            dots = jnp.sum(probs * grad_probs, axis=0, keepdims=True)
            grad_scores = (probs * (grad_probs - dots) * HEAD_DIM ** (-0.5)).astype(BF16)
            grads.append(
                (
                    dot_tn(grad_scores, key_pair),
                    dot_nn(grad_scores, query_pair),
                    dot_nn(probs.astype(BF16), grad_pair),
                )
            )
        grad_query, grad_key, grad_value = (
            jnp.where(first, left, right) for left, right in zip(grads[0], grads[1])
        )
        out_ref[:, query_cols] = grad_query.astype(BF16)
        out_ref[:, key_cols] = grad_key.astype(BF16)
        out_ref[:, value_cols] = grad_value.astype(BF16)
        bias_ref[0, :, query_cols] = jnp.sum(grad_query, axis=0, keepdims=True)
        bias_ref[0, :, key_cols] = jnp.sum(grad_value, axis=0, keepdims=True)


def attn_bwd_call(qkv, grad_mixed, slots):
    rows, width = grad_mixed.shape
    seq = rows // slots
    return pl.pallas_call(
        attn_bwd_kernel,
        grid=(slots,),
        in_specs=[
            pl.BlockSpec((seq, 3 * width), lambda s: (s, 0)),
            pl.BlockSpec((seq, width), lambda s: (s, 0)),
        ],
        out_specs=[
            pl.BlockSpec((seq, 3 * width), lambda s: (s, 0)),
            pl.BlockSpec((1, 1, 2 * width), lambda s: (s, 0, 0)),
        ],
        out_shape=[
            shape((rows, 3 * width), BF16),
            shape((slots, 1, 2 * width), F32),
        ],
        name="attn_bwd",
        **params(20 * rows * width * seq, 16 * rows * width, rows * seq * HEADS),
    )(qkv, grad_mixed)


def mixed_bwd_kernel(offsets, *refs):
    count = len(offsets)
    spot_ref, low_ref = refs[:2]
    pieces = refs[2 : 2 + count]
    out_ref, whole, sems = refs[2 + count :]
    copies = piece_copies(pieces, offsets, spot_ref, whole, sems)
    for copy in copies:
        copy.start()
    for copy in copies:
        copy.wait()
    out_ref[...] = dot_nt(low_ref[...], whole[...]).astype(BF16)


def mixed_bwd_call(spot, low_one, weight):
    rows, width = low_one.shape
    pieces, offsets = weight
    return pl.pallas_call(
        functools.partial(mixed_bwd_kernel, offsets),
        in_specs=specs(1, pltpu.SMEM) + specs(1) + specs(len(pieces), pl.ANY),
        out_specs=pl.BlockSpec(memory_space=pltpu.VMEM),
        out_shape=shape((rows, width), BF16),
        scratch_shapes=[
            pltpu.VMEM((width, width), BF16),
            pltpu.SemaphoreType.DMA((len(pieces),)),
        ],
        name="proj_bwd",
        **params(2 * rows * width * width, 4 * rows * width + 2 * width * width),
    )(spot, low_one, *pieces)


def input_bwd_kernel(offsets, slots, *refs):
    count = len(offsets)
    spot_ref, grad_ref, tok_ref, mid_ref, mod_ref, sums_ref, gate_ref, cond_ref = refs[:8]
    pieces = refs[8 : 8 + count]
    out_ref, mod_out, whole, sems = refs[8 + count :]
    copies = piece_copies(pieces, offsets, spot_ref, whole, sems)
    for copy in copies:
        copy.start()
    for copy in copies:
        copy.wait()
    rows, width = tok_ref.shape
    seq = rows // slots

    def put(slot, part, value):
        mod_out[slot : slot + 1, part * width : (part + 1) * width] = value.astype(BF16)

    for slot in range(slots):
        at = pl.ds(slot * seq, seq)
        row = slice(slot, slot + 1)
        grad_hidden = dot_nt(grad_ref[at, :], whole[...])
        normed, inv_std = row_norm(tok_ref[at, :].astype(F32))
        scale = 1.0 + mod_part(mod_ref, slot, 1, width)
        out_ref[at, :] = mid_ref[at, :] + norm_back(grad_hidden * scale, normed, inv_std)
        put(slot, 0, jnp.sum(grad_hidden, axis=0, keepdims=True))
        put(slot, 1, jnp.sum(grad_hidden * normed, axis=0, keepdims=True))
        for part in range(3):
            put(slot, 2 + part, sums_ref[part, row, :])
        put(slot, 5, gate_ref[row, :])
        cond = cond_ref[row, :].astype(F32)
        put(slot, 6, cond * (1.0 / (1.0 + jnp.exp(-cond))))


def input_bwd_call(spot, grad_qkv, tokens, grad_mid, modulation, sums, gate_sums, condition, weight, slots):
    rows, width = tokens.shape
    pieces, offsets = weight
    return pl.pallas_call(
        functools.partial(input_bwd_kernel, offsets, slots),
        in_specs=specs(1, pltpu.SMEM) + specs(7) + specs(len(pieces), pl.ANY),
        out_specs=specs(2),
        out_shape=[shape((rows, width), F32), shape((slots, 7 * width), BF16)],
        scratch_shapes=[
            pltpu.VMEM((width, 3 * width), BF16),
            pltpu.SemaphoreType.DMA((len(pieces),)),
        ],
        name="qkv_bwd",
        **params(6 * rows * width * width, 16 * rows * width + 6 * width * width),
    )(spot, grad_qkv, tokens, grad_mid, modulation, sums, gate_sums, condition, *pieces)


def split_store(core, total, depth, keep_ref, send_ref, cols):
    for far in range(total.shape[0] // (2 * depth)):
        even = total[2 * far * depth : (2 * far + 1) * depth]
        odd = total[(2 * far + 1) * depth : (2 * far + 2) * depth]
        keep_ref[far, :, cols] = jnp.where(core == 0, even, odd)
        send_ref[far, :, cols] = jnp.where(core == 0, odd, even).astype(BF16)


def wide_grad_kernel(spot_ref, left_ref, right_ref, keep_ref, send_ref):
    total = dot_tn(left_ref[...], right_ref[...])
    split_store(spot_ref[0] & 1, total, keep_ref.shape[1], keep_ref, send_ref, slice(None))


def wide_grad(spot, left, right, shards, name):
    rows, in_dim = left.shape
    out_dim = right.shape[1]
    depth = in_dim // shards
    block = out_dim // 2 if out_dim > 1024 else out_dim
    per_step = shards // 2 if in_dim <= 768 else 1
    out_block = pl.BlockSpec((per_step, depth, block), lambda i, j: (i, 0, j))
    dims = (shards // 2, depth, out_dim)
    return pl.pallas_call(
        wide_grad_kernel,
        grid=(shards // 2 // per_step, out_dim // block),
        in_specs=specs(1, pltpu.SMEM)
        + [
            pl.BlockSpec((rows, 2 * depth * per_step), lambda i, j: (0, i)),
            pl.BlockSpec((rows, block), lambda i, j: (0, j)),
        ],
        out_specs=[out_block, out_block],
        out_shape=[shape(dims, F32), shape(dims, BF16)],
        name=name,
        **params(2 * rows * in_dim * out_dim, 3 * in_dim * out_dim + 2 * rows * (in_dim + out_dim)),
    )(spot, left, right)


EXTRA = 256


def bias_rows(count):
    return [(start, min(EXTRA, count - start)) for start in range(0, count, EXTRA)]


def attn_grad_kernel(shards, *refs):
    spot_ref, hidden_ref, qkv_ref, mixed_ref, low_ref, qv_ref, sums_ref, fc1_ref = refs[:8]
    keep_a, send_a, keep_b, send_b, extra = refs[8:]
    depth = keep_a.shape[1]
    width = hidden_ref.shape[1]
    core = spot_ref[0] & 1
    total = dot_tn(hidden_ref[...], qkv_ref[...])
    split_store(core, total[:, : 2 * width], depth, keep_a, send_a, slice(None))
    split_store(core, total[:, 2 * width :], depth, keep_b, send_b, pl.ds(0, width))
    total = dot_tn(mixed_ref[...], low_ref[...])
    split_store(core, total, depth, keep_b, send_b, pl.ds(width, width))
    extra[...] = jnp.zeros_like(extra)
    biases = (
        jnp.sum(qv_ref[...], axis=0),
        jnp.sum(sums_ref[3], axis=0, keepdims=True),
        fc1_ref[...],
        jnp.sum(sums_ref[4], axis=0, keepdims=True),
    )
    for place in range(shards):
        row = place * depth
        for bias in biases:
            count = bias.shape[1] // shards
            for start, size in bias_rows(count):
                first = place * count + start
                extra[row : row + 1, :size] = bias[:, first : first + size]
                row += 1
    split_store(core, extra[...], depth, keep_b, send_b, pl.ds(2 * width, EXTRA))


def attn_grad(spot, hidden, grad_qkv, mixed, low_one, qv_sums, sums, fc1_sums, shards):
    rows, width = hidden.shape
    first = (shards // 2, width // shards, 2 * width)
    second = (shards // 2, width // shards, 2 * width + EXTRA)
    outs = pl.pallas_call(
        functools.partial(attn_grad_kernel, shards),
        in_specs=specs(1, pltpu.SMEM) + specs(7),
        out_specs=specs(4),
        out_shape=[shape(first, F32), shape(first, BF16), shape(second, F32), shape(second, BF16)],
        scratch_shapes=[pltpu.VMEM((width, EXTRA), F32)],
        name="attn_weight_grads",
        **params(8 * rows * width * width, 12 * width * width + 14 * rows * width),
    )(spot, hidden, grad_qkv, mixed, low_one, qv_sums, sums, fc1_sums)
    return outs[:2], outs[2:]


def round_kernel(kinds, spot_ref, *refs):
    ins = list(refs[: sum(kind[1] for kind in kinds)])
    outs = list(refs[len(ins) :])
    for kind, count in kinds:
        args, ins = ins[:count], ins[count:]
        if kind == "halve":
            keep_out, send_out, outs = outs[0], outs[1], outs[2:]
            keep_out[...] = args[0][...] + args[2][...].astype(F32)
            send_out[...] = (args[1][...] + args[3][...].astype(F32)).astype(BF16)
        elif kind == "merge":
            keep_out, send_out, outs = outs[0], outs[1], outs[2:]
            half = keep_out.shape[2] // 2
            for part in range(2):
                mine, other, sent_mine, sent_other = args[4 * part : 4 * part + 4]
                cols = slice(part * half, (part + 1) * half)
                keep_out[:, :, cols] = mine[...] + sent_mine[...].astype(F32)
                send_out[:, :, cols] = (other[...] + sent_other[...].astype(F32)).astype(BF16)
        elif kind == "add":
            out, outs = outs[0], outs[1:]
            out[...] = (args[0][...].astype(F32) + args[1][...].astype(F32)).astype(BF16)
        else:
            out, outs = outs[0], outs[1:]
            rows = args[0].shape[1]
            out[:, :rows, :] = args[0][...]
            out[:, rows:, :] = args[1][...]


SMALL_ROUND = 1 << 20


def round_call(spot, jobs):
    split = 2 if sum(value.size for job in jobs for value in job["args"]) > SMALL_ROUND else 1
    for job in jobs:
        cols = job["args"][0].shape[2] // (1 if job.get("part") is None else 2)
        if job["kind"] == "merge" or cols % 256:
            split = 1
    in_specs, args, out_specs, out_shape = [], [], [], []

    def halves_of(value, axis, bit, dim, base, dims, chunk):
        def spec(other):
            def place(j, spot_ref):
                half = high_bit(spot_ref, axis.number, bit)
                half = 1 - half if other else half
                return (half, 0, base + j) if dim == 0 else (0, half, base + j)

            return pl.BlockSpec((dims[0], dims[1], chunk), place)

        in_specs.extend([spec(False), spec(True)])
        args.extend([value, value])

    def plain(dims):
        return pl.BlockSpec((dims[0], dims[1], dims[2] // split), lambda j, spot_ref: (0, 0, j))

    kinds = []
    for job in jobs:
        values = job["args"]
        kind = job["kind"]
        dims = list(values[0].shape)
        before = len(args)
        if kind in ("halve", "merge"):
            axis, bit, dim = job["step"]
            dims[dim] //= 2
            part = job.get("part")
            if part is not None:
                dims[2] //= 2
            chunk = dims[2] // split
            base = 0 if part is None else part * split
            for value in values:
                halves_of(value, axis, bit, dim, base, dims, chunk)
            if kind == "merge":
                dims[2] *= 2
            out_specs += [plain(dims)] * 2
            out_shape += [shape(tuple(dims), F32), shape(tuple(dims), BF16)]
        else:
            in_specs += [plain(value.shape) for value in values]
            args += values
            if kind == "cat":
                dims[1] += values[1].shape[1]
            out_specs.append(plain(dims))
            out_shape.append(shape(tuple(dims), BF16))
        kinds.append((kind, len(args) - before))
    outs = pl.pallas_call(
        functools.partial(round_kernel, kinds),
        grid_spec=pltpu.PrefetchScalarGridSpec(
            num_scalar_prefetch=1, grid=(split,), in_specs=in_specs, out_specs=out_specs
        ),
        out_shape=out_shape,
        name="sum_round",
        **params(0, 0),
    )(spot, *args)
    outs = list(outs)
    results = []
    for kind, _ in kinds:
        count = 2 if kind in ("halve", "merge") else 1
        results.append(outs[:count])
        outs = outs[count:]
    return results


def first_row(spot_ref, terms, flips):
    row = 0
    for (number, bit, size), flip in zip(terms, flips):
        half = high_bit(spot_ref, number, bit)
        row = row + (1 - half if flip else half) * size
    return row


def row_places(spot_ref, refs, terms, flips, count):
    parts = []
    for ref in refs:
        parts += [(ref, slice(k * count, (k + 1) * count)) for k in range(ref.shape[1] // count)]
    for (ref, rows), flip in zip(parts, flips):
        at = first_row(spot_ref, terms, flip)
        if not isinstance(at, int):
            at = pl.multiple_of(at, 16)
        yield ref, rows, pl.ds(at, count)


def place_kernel(terms, flips, count, spot_ref, *refs):
    out_ref = refs[-1]
    for ref, rows, at in row_places(spot_ref, refs[:-1], terms, flips, count):
        out_ref[at, :] = ref[0, rows, :].astype(F32)


def place_rows(spot, done, rows):
    pieces, terms, flips, count = done
    cols = pieces[0].shape[2]
    return pl.pallas_call(
        functools.partial(place_kernel, terms, flips, count),
        in_specs=specs(1, pltpu.SMEM) + specs(len(pieces)),
        out_specs=pl.BlockSpec(memory_space=pltpu.VMEM),
        out_shape=shape((rows, cols), F32),
        name="place_rows",
        **params(0, rows * cols * 6),
    )(spot, *pieces)


def place_attn_kernel(plans, parts, biases, spot_ref, *refs):
    qkv_out, proj_out, *bias_outs, head = refs[2 * parts :]
    width = proj_out.shape[1]
    for ref, rows, at in row_places(spot_ref, refs[:parts], *plans[0]):
        qkv_out[at, : 2 * width] = ref[0, rows, :].astype(F32)
    for ref, rows, at in row_places(spot_ref, refs[parts : 2 * parts], *plans[1]):
        qkv_out[at, 2 * width :] = ref[0, rows, :width].astype(F32)
        proj_out[at, :] = ref[0, rows, width : 2 * width].astype(F32)
        head[at, :] = ref[0, rows, 2 * width :].astype(F32)
    row = 0
    for count, out in zip(biases, bias_outs):
        for start, size in bias_rows(count):
            out[start : start + size] = head[row, :size]
            row += 1


def place_attn(spot, first, second, rows, width, biases):
    parts = len(first[0])
    return pl.pallas_call(
        functools.partial(place_attn_kernel, (first[1:], second[1:]), parts, biases),
        in_specs=specs(1, pltpu.SMEM) + specs(2 * parts),
        out_specs=specs(2 + len(biases)),
        out_shape=[shape((rows, 3 * width), F32), shape((rows, width), F32)]
        + [shape((count,), F32) for count in biases],
        scratch_shapes=[pltpu.VMEM((rows, EXTRA), F32)],
        name="place_attn",
        **params(0, rows * width * 24),
    )(spot, *first[0], *second[0])


def cond_kernel(shards, spot_ref, grad_ref, cond_ref, out_ref):
    slots, width = cond_ref.shape
    depth = width // shards
    group = shards * slots
    for place in range(shards):
        total = jnp.zeros((slots, depth), F32)
        for offset in range(shards):
            first = offset * group + offset * slots
            part = grad_ref[first : first + slots, :]
            total = total + jnp.where((spot_ref[0] ^ offset) == place, part, 0.0)
        cond = cond_ref[:, place * depth : (place + 1) * depth].astype(F32)
        logistic = 1.0 / (1.0 + jnp.exp(-cond))
        out_ref[:, place * depth : (place + 1) * depth] = (
            total * logistic * (1.0 + cond * (1.0 - logistic))
        )


def cond_call(spot, grads, condition, shards):
    return pl.pallas_call(
        functools.partial(cond_kernel, shards),
        in_specs=specs(1, pltpu.SMEM) + specs(2),
        out_specs=pl.BlockSpec(memory_space=pltpu.VMEM),
        out_shape=shape(condition.shape, F32),
        name="grad_condition",
        **params(),
    )(spot, grads, condition)


def after(value, *others):
    return lax.optimization_barrier((value,) + others)[0]


class Axis:
    def __init__(self, name, size, number):
        self.name = name
        self.size = size
        self.number = number
        self.index = lax.axis_index(name)
        self.bits = [1 << k for k in range(size.bit_length() - 1)]

    def swap(self, value, bit):
        return lax.ppermute(value, self.name, [(i, i ^ bit) for i in range(self.size)])

    def high(self, bit):
        return (self.index & bit) != 0


def ordered(high, mine, other, axis=0):
    return jnp.where(
        high, jnp.concatenate([other, mine], axis), jnp.concatenate([mine, other], axis)
    )


def gather_ordered(value, axis):
    dims = value.shape
    value = value[None]
    for bit in reversed(axis.bits):
        other = axis.swap(value, bit)
        high = axis.high(bit)
        value = jnp.stack([jnp.where(high, other, value), jnp.where(high, value, other)], 1)
        value = value.reshape((-1,) + dims)
    return value


class Gather:
    def __init__(self, piece, shard, rep, split):
        self.shard, self.rep = shard, rep
        self.own = piece
        half = piece.shape[0] // 2
        self.split = split is not None and half % 16 == 0 and rep.size > 1
        self.send = piece
        if self.split:
            late = after(piece, split)
            self.send = lax.dynamic_slice_in_dim(late, rep.high(1).astype(jnp.int32) * half, half, 0)
        self.held = [(piece, 0, None)]
        self.fars = []
        self.swapped = []

    def near(self, *gate):
        for bit in reversed(self.shard.bits[1:]):
            for value, offset, part in list(self.held):
                if value is self.own and self.split:
                    value, part = self.send, "near"
                self.held.append((self.shard.swap(after(value, *gate), bit), offset ^ bit, part))
        return self.held[-1][0]

    def far(self, *gate):
        for value, offset, part in self.held:
            if part == "near":
                self.fars.append((self.rep.swap(after(value, *gate), 1), offset, "far"))
        return self.fars[-1][0] if self.fars else self.held[-1][0]

    def swap_own(self, *gate):
        self.swap(self.held[:1], *gate)

    def swap_near(self, *gate):
        self.swap(self.held[1:], *gate)

    def swap_far(self, *gate):
        self.swap(self.fars, *gate)

    def swap(self, held, *gate):
        for value, offset, part in held:
            self.swapped.append((self.shard.swap(after(value, *gate), 1), offset ^ 1, part))

    def pieces(self):
        every = self.held + self.fars + self.swapped
        rows = self.own.shape[0]
        return [value for value, _, _ in every], tuple((offset, part, rows) for _, offset, part in every)


def plan(order, rows):
    stages = []
    back = []
    for at, (axis, bit) in enumerate(order):
        if axis.name == "shard":
            stages.append((axis, bit, 0))
        elif rows // 2 % 16 == 0 and at < len(order) - 1:
            rows //= 2
            stages.append((axis, bit, 1))
            back.insert(0, (axis, bit, rows))
        else:
            stages.append((axis, bit, None))
    return stages, back


class Reduction:
    def __init__(self, keep, operand, sent, stages, back):
        self.keep = keep
        self.operand = (operand,)
        self.sent = (sent,)
        self.stages, self.back = stages, back
        self.at = 0
        self.steps = len(stages) + len(back)

    def running(self):
        return self.at < self.steps

    def jobs(self):
        if self.at < len(self.stages):
            dim = self.stages[self.at][2]
            if dim is not None:
                return [dict(kind="halve", args=[self.keep, self.sent[0]], step=self.stages[self.at])]
        if self.at <= len(self.stages):
            return [dict(kind="add", args=[self.keep, self.sent[0]])]
        return [dict(kind="cat", args=[self.whole, self.sent[0]])]

    def commit(self, results):
        if self.at < len(self.stages):
            axis, bit, _ = self.stages[self.at]
            self.keep, operand = results[0][0], results[0][-1]
        else:
            axis, bit, _ = self.back[self.at - len(self.stages)]
            operand = self.whole = results[0][0]
        self.operand = (operand,)
        self.sent = (axis.swap(operand, bit),)
        self.at += 1

    def finish(self):
        terms = [(axis.number, bit, size) for axis, bit, size in self.back]
        flips = [(False,) * len(terms)]
        for k in range(len(terms)):
            flips += [flip[:k] + (True,) + flip[k + 1 :] for flip in flips]
        if self.back:
            pieces = [self.whole, self.sent[0]]
        else:
            total = self.keep.astype(F32) + self.sent[0].astype(F32)
            pieces = [total.astype(BF16)]
        count = sum(piece.shape[1] for piece in pieces) // len(flips)
        return pieces, terms, flips, count


def one_way(pair, shard, order):
    keep, send = pair
    return Reduction(keep, send, shard.swap(send, 1), *plan(order, keep.shape[1]))


class TwoWay:
    def __init__(self, pair, shard, rep):
        self.keeps, send = pair[0], pair[1]
        self.operand = (send,)
        self.sent = (shard.swap(send, 1),)
        inner = [(shard, bit, 0) for bit in reversed(shard.bits[1:])]
        near = (rep, 1, 1)
        self.orders = (inner + [near], [near] + inner)
        rows = self.keeps.shape[1] // 2
        self.stages, self.back = plan([(rep, bit) for bit in rep.bits[1:]], rows)
        self.back = self.back + [(rep, 1, rows)]
        self.round = 0
        self.inner = None

    def running(self):
        return self.inner is None or self.inner.running()

    def jobs(self):
        if self.inner is not None:
            self.inner.sent = self.sent
            return self.inner.jobs()
        if self.round == len(self.orders[0]):
            args = [self.keeps[0], self.sent[0], self.keeps[1], self.sent[1]]
            return [dict(kind="merge", args=args, step=self.stages[0])]
        jobs = []
        for part, order in enumerate(self.orders):
            if self.round == 0:
                jobs.append(dict(args=[self.keeps, self.sent[0]], part=part))
            else:
                jobs.append(dict(args=[self.keeps[part], self.sent[part]]))
            jobs[part].update(kind="halve", step=order[self.round])
        return jobs

    def commit(self, results):
        if self.inner is None and self.round < len(self.orders[0]):
            self.keeps = [keep for keep, _ in results]
            self.operand = tuple(operand for _, operand in results)
            steps = [order[self.round] for order in self.orders]
            self.sent = tuple(
                axis.swap(operand, bit) for (axis, bit, _), operand in zip(steps, self.operand)
            )
            self.round += 1
            return
        if self.inner is None:
            self.inner = Reduction(None, None, None, self.stages, self.back)
        self.inner.commit(results)
        self.operand, self.sent = self.inner.operand, self.inner.sent

    def finish(self):
        self.inner.sent = self.sent
        return self.inner.finish()


def two_way(pair, shard, rep):
    rows = pair[0].shape[1]
    if len(rep.bits) > 1 and rows // 4 % 16 == 0 and shard.size > 2:
        return TwoWay(pair, shard, rep)
    order = [(shard, bit) for bit in reversed(shard.bits[1:])] + [(rep, bit) for bit in rep.bits]
    return one_way(pair, shard, order)


class Chain:
    def __init__(self, value, steps):
        self.value = value
        self.todo = list(steps)
        self.send_next()

    def running(self):
        return self.join is not None

    def send_next(self):
        self.operand = (self.value,)
        axis, bit, self.join = self.todo.pop(0)
        self.sent = (axis.swap(self.value, bit),)

    def jobs(self):
        return []

    def commit(self, results):
        self.value = self.join(self.value, self.sent[0])
        self.join = None
        if self.todo:
            self.send_next()


def together(spot, chains, *values):
    got = lax.optimization_barrier((tuple(chain.sent for chain in chains), values))
    jobs = []
    shares = []
    for chain, sent in zip(chains, got[0]):
        chain.sent = sent
        shares.append(chain.jobs() if chain.running() else [])
        jobs += shares[-1]
    results = round_call(spot, jobs) if jobs else []
    for chain, share in zip(chains, shares):
        if chain.running():
            chain.commit(results[: len(share)])
            results = results[len(share) :]
    return got[1][0] if len(values) == 1 else got[1]


def rounds(spot, chains, most):
    for _ in range(most):
        running = [chain for chain in chains if chain.running()]
        if not running:
            return
        together(spot, running)


def launched(value, *chains):
    return after(value, *[operand for chain in chains for operand in chain.operand])


def per_device(
    shard_size,
    rep_size,
    tokens,
    condition,
    counts,
    cotangent,
    ada_weight,
    ada_bias,
    qkv_weight,
    qv_bias,
    proj_weight,
    proj_bias,
    fc1_weight,
    fc1_bias,
    fc2_weight,
    fc2_bias,
):
    shard = Axis("shard", shard_size, 0)
    rep = Axis("rep", rep_size, 1)
    spot = jnp.stack([shard.index, rep.index]).astype(jnp.int32)
    slots, width = condition.shape
    seq = tokens.shape[0] // slots
    rows = slots * seq
    depth = ada_weight.shape[0]

    slots_here = condition[None]
    arrived = []
    for bit in reversed(shard.bits):
        arrived.append(shard.swap(slots_here, bit))
        slots_here = jnp.stack([slots_here, arrived[-1]], 1).reshape((-1,) + condition.shape)
    slots_here = slots_here.reshape(-1, width)
    silu_group = jax.nn.silu(slots_here.astype(F32)).astype(BF16)
    my_cols = lax.dynamic_slice_in_dim(silu_group, shard.index * depth, depth, 1)
    ada_late, counts, *bias_list = lax.optimization_barrier(
        (ada_bias, counts, qv_bias, proj_bias, fc1_bias, fc2_bias, slots_here)
    )[:-1]
    own_bias = lax.dynamic_update_slice(
        jnp.zeros((6 * width,), F32), ada_late.astype(F32), (shard.index * ada_bias.shape[0],)
    )
    modulation = dot_nn(my_cols, ada_weight) + own_bias[None]

    packed = jnp.concatenate(bias_list).astype(F32)
    packed = jnp.pad(packed, (0, 6 * width - packed.shape[0]))[None]
    qkv_gather = Gather(qkv_weight, shard, rep, condition)
    near = qkv_gather.near(arrived[0])
    qkv_gather.far()
    qkv_gather.swap_own(slots_here)
    queued = []
    partial = []
    for bit in reversed(shard.bits):
        half = modulation.shape[0] // 2
        send = jnp.concatenate([modulation[half:], packed], 0)
        queued.append(send if queued else after(send, near))
        came = shard.swap(queued[-1], bit)
        partial.append(came)
        modulation = modulation[:half] + came[:half]
        other, high = came[half:], shard.high(bit)
        packed = jnp.stack([jnp.where(high, other, packed), jnp.where(high, packed, other)], 1)
        packed = packed.reshape(-1, 6 * width)
    proj_gather = Gather(proj_weight, shard, rep, None)
    near_proj = proj_gather.near(queued[0])
    proj_gather.swap_own(slots_here)
    fc1_gather = Gather(fc1_weight, shard, rep, queued[0])
    fc2_gather = Gather(fc2_weight, shard, rep, queued[0])
    near_one = fc1_gather.near(partial[0])
    near_two = fc2_gather.near(near_proj)
    wide = []
    start = 0
    for bias in bias_list:
        wide.append(packed[:, start : start + bias.shape[0]].reshape(1, -1))
        start += bias.shape[0]
    qv_b, proj_b, fc1_b, fc2_b = wide

    spot = jnp.concatenate([spot, counts])
    cot = cotangent

    qkv_gather.swap_near()
    qkv_gather.swap_far()
    proj_gather.swap_near()
    qkv_w = qkv_gather.pieces()
    proj_w = proj_gather.pieces()
    qkv_b = jnp.concatenate([qv_b[:, :width], jnp.zeros((1, width), F32), qv_b[:, width:]], axis=1)
    hidden_one, qkv = qkv_call(spot, tokens, modulation, qkv_b, qkv_w, slots)
    far_one = fc1_gather.far(qkv)
    fc1_gather.swap_near(qkv)
    fc1_gather.swap_own(qkv)
    fc2_gather.swap_own(qkv)
    mixed, branch_one, hidden_two, low_two = attn_call(
        spot, after(qkv, near_one), tokens, cot, modulation, proj_b, proj_w, slots
    )
    far_two = fc2_gather.far(hidden_two)
    fc2_gather.swap_near(hidden_two)
    fc1_gather.swap_far(hidden_two)
    fc1_w = fc1_gather.pieces()
    act_low, derivative = gelu_call(spot, after(hidden_two, near_two), fc1_b, fc1_w)
    fc2_gather.swap_far(act_low)
    fc2_w = fc2_gather.pieces()

    shard_steps = [(shard, bit) for bit in reversed(shard.bits[1:])]
    low_bits = [(rep, bit) for bit in rep.bits[:1]]
    high_bits = [(rep, bit) for bit in rep.bits[1:]]
    keep, send = wide_grad(spot, act_low, after(low_two, far_two), shard.size, "fc2_grad")
    fc2_sum = two_way((keep, after(send, *fc2_w[0])), shard, rep)
    block_out, gate_sums = out_call(
        spot, launched(act_low, fc2_sum), tokens, branch_one, cot, modulation, fc2_b, fc2_w, slots
    )
    block_out, gate_sums = together(spot, [fc2_sum], block_out, gate_sums)
    low_pre, grad_fc1_b, grad_mid, low_one, sums = mlp_bwd_call(spot,
        launched(low_two, fc2_sum), derivative, tokens, branch_one, cot, modulation, fc1_w, fc2_w, slots
    )
    low_pre = together(spot, [fc2_sum], low_pre)
    keep, send = wide_grad(spot, hidden_two, launched(low_pre, fc2_sum), shard.size, "fc1_grad")
    keep, send, low_one = together(spot, [fc2_sum], keep, send, low_one)
    fc1_sum = two_way((keep, send), shard, rep)
    grad_mixed = mixed_bwd_call(spot, launched(low_one, fc1_sum, fc2_sum), proj_w)
    grad_mixed = together(spot, [fc1_sum, fc2_sum], grad_mixed)
    grad_qkv, qv_sums = attn_bwd_call(qkv, launched(grad_mixed, fc1_sum, fc2_sum), slots)
    grad_qkv, qv_sums = together(spot, [fc1_sum, fc2_sum], grad_qkv, qv_sums)
    first, second = attn_grad(
        spot,
        hidden_one,
        launched(grad_qkv, fc1_sum, fc2_sum),
        mixed,
        low_one,
        qv_sums,
        sums,
        grad_fc1_b,
        shard.size,
    )
    first, second, grad_qkv = together(spot, [fc1_sum, fc2_sum], first, second, grad_qkv)
    first_sum = one_way(first, shard, shard_steps + low_bits + high_bits)
    first_sum.back.reverse()
    second_sum = one_way(second, shard, low_bits + shard_steps + high_bits)
    grad_tokens, slot_values = input_bwd_call(spot,
        launched(grad_qkv, first_sum, second_sum, fc1_sum, fc2_sum),
        tokens,
        grad_mid,
        modulation,
        sums,
        gate_sums,
        condition,
        qkv_w,
        slots,
    )
    sums_list = [first_sum, second_sum, fc1_sum] + ([fc2_sum] if fc2_sum.running() else [])
    grad_tokens, slot_values = together(spot, sums_list, grad_tokens, slot_values)

    def append(mine, other):
        return jnp.concatenate([mine, other], 0)

    group_slots = Chain(slot_values, [(shard, bit, append) for bit in shard.bits])
    rounds(spot, sums_list + [group_slots], len(shard.bits))
    every = [(rep, bit, append) for bit in reversed(rep.bits)]
    all_slots = Chain(group_slots.value, every)
    grad_silu = dot_nt(group_slots.value[:, : 6 * width], ada_weight)
    to_cond = Chain(grad_silu, [(shard, bit, append) for bit in shard.bits])
    rounds(spot, sums_list + [all_slots, to_cond], 100)

    grad_cond = cond_call(spot, to_cond.value, condition, shard.size)

    mod_all = all_slots.value[:, : 6 * width]
    silu_cols = lax.dynamic_slice_in_dim(all_slots.value, 6 * width + shard.index * depth, depth, 1)
    grad_ada_w = dot_tn(silu_cols, mod_all)
    ada_b_all = jnp.sum(mod_all.astype(F32), axis=0)
    grad_ada_b = lax.dynamic_slice_in_dim(
        ada_b_all, shard.index * ada_bias.shape[0], ada_bias.shape[0], 0
    )

    grad_fc2_w = place_rows(spot, fc2_sum.finish(), fc2_weight.shape[0])
    grad_fc1_w = place_rows(spot, fc1_sum.finish(), fc1_weight.shape[0])
    bias_sizes = tuple(bias.shape[0] for bias in bias_list)
    grad_qkv_w, grad_proj_w, *bias_out = place_attn(
        spot, first_sum.finish(), second_sum.finish(), depth, width, bias_sizes
    )

    return (
        block_out,
        grad_tokens,
        grad_cond,
        grad_ada_w,
        grad_ada_b,
        grad_qkv_w,
        bias_out[0],
        grad_proj_w,
        bias_out[1],
        grad_fc1_w,
        bias_out[2],
        grad_fc2_w,
        bias_out[3],
    )


def solution(mesh):
    rows = P(("rep", "shard"), None)
    weights = (P("shard", None), P("shard"))
    return jax.shard_map(
        functools.partial(per_device, mesh.shape["shard"], mesh.shape["rep"]),
        mesh=mesh,
        in_specs=(rows, rows, P(("rep", "shard")), rows) + weights * 5,
        out_specs=(rows, rows, rows) + weights * 5,
        check_vma=False,
    )
```
